128 devices in a mesh: row: 16 (over y_lo, x, core), col: 8 (over y_hi, z).
Axes of the slice: x: 4, y: 4 (y_hi: 2, y_lo: 2; y = y_hi * 2 + y_lo), z: 4, core: 2. Of those that a mesh axis runs over, the one named last changes fastest.
Arguments:
- pair: bfloat16 [384, 384, 128], P('row', 'col'), may hold values from -6 to 6
- mask: int32 [384], replicated, may hold values 0 or 1
- in_gain: float32 [128], replicated, may hold values from 0.5 to 1.5
- in_bias: float32 [128], replicated, may hold values from -3 to 3
- w_in: bfloat16 [128, 640], replicated, may hold values from -0.5 to 0.5
- out_gain: float32 [128], replicated, may hold values from 0.5 to 1.5
- out_bias: float32 [128], replicated, may hold values from -3 to 3
- w_out: bfloat16 [128, 128], replicated, may hold values from -0.5 to 0.5
- cotangent: bfloat16 [384, 384, 128], P('row', 'col'), may hold values from -6 to 6
Outputs:
- update: bfloat16 [384, 384, 128], P('row', 'col')
- pair_grad: bfloat16 [384, 384, 128], P('row', 'col')
- w_in_grad: float32 [128, 640], replicated
- w_out_grad: float32 [128, 128], replicated
The draws below stay inside these ranges and needn't reach their ends.
Inputs may be any that keep to these rules, and one draw needn't show every extreme that they name: `mask`: 0 or 1 per residue.
All inputs are finite; a program needn't handle non-finite values.
Results may differ from the reference program's by a relative error of at most 0.013.
Values may be sent and summed in bfloat16 or wider, within the bound.
No kernel may reach another device: no remote copies, remote signals or barrier semaphores. Data moves between devices by JAX's collectives and lax.ppermute only.
A program may use at most 64 MiB of HBM per device.

```python
import jax
import jax.numpy as jnp
from jax import lax

C = 128
H = 128
N = 384


def set_ends(entries, key, low, top_value):
    index_at = [jax.random.randint(jax.random.fold_in(key, axis), (), 0, length) for axis, length in enumerate(entries.shape)]
    widest = entries.shape.index(max(entries.shape))
    neighbour = index_at[:widest] + [(index_at[widest] + 1) % entries.shape[widest]] + index_at[widest + 1:]
    return entries.at[tuple(index_at)].set(low).at[tuple(neighbour)].set(top_value)


def block_scale(key, shape, cuts, least, top_value):
    factor_of = 1.0
    for dim, blocks in cuts:
        heights = jax.random.uniform(jax.random.fold_in(jax.random.fold_in(key, 6), dim), (blocks,), jnp.float32, least / len(cuts), top_value / len(cuts))
        factor_of = factor_of * jnp.repeat(jnp.exp(heights), shape[dim] // blocks).reshape((-1,) + (1,) * (len(shape) - 1 - dim))
    return factor_of


def bell_draw(stream_key, dims, spread, reach, pieces=(), held_as=jnp.bfloat16):
    entries = jax.random.normal(stream_key, dims, jnp.float32) * spread
    if len(pieces) > 0:
        entries = block_scale(stream_key, dims, pieces, -0.22, 0.18) * entries
    return jnp.clip(entries, min=-reach, max=reach).astype(held_as)


def setup_inputs(seed: int = 0) -> dict:
    streams_of = jax.random.split(jax.random.key(seed), 10)
    return {
        "pair": bell_draw(streams_of[0], (N, N, C), 1.0, 6.0, ((0, 16), (1, 8))),
        "mask": set_ends((jax.random.randint(streams_of[1], (N,), 0, 8) < 7).astype(jnp.int32), jax.random.fold_in(streams_of[1], 1), 0, 1),
        "in_gain": jnp.clip(1.0 + 0.1 * jax.random.normal(streams_of[2], (C,), jnp.float32), 0.5, 1.5),
        "in_bias": bell_draw(streams_of[3], (C,), 0.5, 3.0, (), jnp.float32),
        "w_in": bell_draw(streams_of[4], (C, 4 * H + C), C ** -0.5, 0.5),
        "out_gain": jnp.clip(1.0 + 0.1 * jax.random.normal(streams_of[5], (H,), jnp.float32), 0.5, 1.5),
        "out_bias": bell_draw(streams_of[6], (H,), 0.5, 3.0, (), jnp.float32),
        "w_out": bell_draw(streams_of[7], (H, C), H ** -0.5, 0.5),
        "cotangent": bell_draw(streams_of[8], (N, N, C), 1.0, 6.0, ((0, 16), (1, 8))),
    }


def layer_norm(values, gain, shift):
    center = values - lax.optimization_barrier(jnp.mean(values, -1, keepdims=True))
    scale = lax.rsqrt(lax.optimization_barrier(jnp.mean(center * center, -1, keepdims=True)) + 1e-05)
    normal = center * scale
    return (normal * gain + shift, normal, scale)

def norm_back(grad, gain, normal, scale):
    weighted = grad * gain
    return scale * (weighted - lax.optimization_barrier(jnp.mean(weighted, -1, keepdims=True)) - normal * lax.optimization_barrier(jnp.mean(weighted * normal, -1, keepdims=True)))

def reference(pair, mask, in_gain, in_bias, w_in, out_gain, out_bias, w_out, cotangent):
    width = pair.shape[2]
    hidden = w_out.shape[0]
    normed, in_normal, in_scale = layer_norm(pair.astype(jnp.float32), in_gain, in_bias)
    normed = normed.astype(jnp.bfloat16)
    flat = normed.reshape(-1, width)
    pre = jnp.dot(flat, w_in, preferred_element_type=jnp.float32).reshape(N, N, -1)
    left_value = pre[..., :hidden]
    left_gate = jax.nn.sigmoid(pre[..., hidden:2 * hidden])
    right_value = pre[..., 2 * hidden:3 * hidden]
    right_gate = jax.nn.sigmoid(pre[..., 3 * hidden:4 * hidden])
    out_gate = jax.nn.sigmoid(pre[..., 4 * hidden:])
    mask_float = mask.astype(jnp.float32)
    pair_mask = (mask_float[:, None] * mask_float[None, :])[:, :, None]
    left = (pair_mask * left_gate * left_value).astype(jnp.bfloat16)
    right = (pair_mask * right_gate * right_value).astype(jnp.bfloat16)
    left_wide = left.astype(jnp.float32)
    right_wide = right.astype(jnp.float32)
    mixed = jnp.einsum('ikh,jkh->ijh', left_wide, right_wide)
    out_normed, out_normal, out_scale = layer_norm(mixed, out_gain, out_bias)
    out_normed = out_normed.astype(jnp.bfloat16)
    out_flat = out_normed.reshape(-1, hidden)
    projected = jnp.dot(out_flat, w_out, preferred_element_type=jnp.float32).reshape(N, N, width)
    update = (out_gate * projected).astype(jnp.bfloat16)
    upstream = cotangent.astype(jnp.float32)
    d_projected = (upstream * out_gate).astype(jnp.bfloat16)
    d_outgate = upstream * projected * out_gate * (1.0 - out_gate)
    d_flat = d_projected.reshape(-1, width)
    w_out_grad = jnp.einsum('nh,nc->hc', out_flat, d_flat, preferred_element_type=jnp.float32)
    d_outnormed = jnp.dot(d_flat, w_out.T, preferred_element_type=jnp.float32).reshape(N, N, hidden)
    d_mixed = norm_back(d_outnormed, out_gain, out_normal, out_scale).astype(jnp.bfloat16)
    d_wide = d_mixed.astype(jnp.float32)
    d_left = jnp.einsum('ijh,jkh->ikh', d_wide, right_wide)
    d_right = jnp.einsum('ijh,ikh->jkh', d_wide, left_wide)
    d_pre = jnp.concatenate([d_left * pair_mask * left_gate, d_left * pair_mask * left_value * left_gate * (1.0 - left_gate), d_right * pair_mask * right_gate, d_right * pair_mask * right_value * right_gate * (1.0 - right_gate), d_outgate], -1).astype(jnp.bfloat16)
    d_preflat = d_pre.reshape(-1, 4 * hidden + width)
    w_in_grad = jnp.einsum('nc,nf->cf', flat, d_preflat, preferred_element_type=jnp.float32)
    d_normed = jnp.dot(d_preflat, w_in.T, preferred_element_type=jnp.float32).reshape(N, N, width)
    pair_grad = norm_back(d_normed, in_gain, in_normal, in_scale).astype(jnp.bfloat16)
    return (update, pair_grad, w_in_grad, w_out_grad)
```

```python
import functools

import jax
import jax.numpy as jnp
from jax import lax
from jax.experimental import pallas as pl
from jax.experimental.pallas import tpu as pltpu
from jax.sharding import PartitionSpec as P

F32 = jnp.float32
BF16 = jnp.bfloat16
EPS = 1e-05
AXES = ("row", "col")

A, B, HALF, LANES = 24, 48, 64, 128
NR, NC, ND = 16, 8, 128
CELLS = A * B
H = 128
N = NR * A


def dot(x, y, contract):
    return lax.dot_general(x, y, (contract, ((), ())), preferred_element_type=F32)


NT = ((1,), (1,))
TN = ((0,), (0,))
NN = ((1,), (0,))


def lane_low(shape):
    return lax.broadcasted_iota(jnp.int32, shape, len(shape) - 1) < HALF


def swap_halves(x):
    return pltpu.roll(x, HALF, x.ndim - 1)


def pad_cells(x):
    return jnp.concatenate([x, jnp.zeros((HALF - B, x.shape[1]), x.dtype)], 0)


def two_sided(x):
    padded = pad_cells(x)
    none = jnp.zeros_like(padded)
    return jnp.concatenate(
        [jnp.concatenate([padded, none], 1), jnp.concatenate([none, padded], 1)], 0
    )


def column(row):
    at = lax.broadcasted_iota(jnp.int32, (H, LANES), 0)
    lane = lax.broadcasted_iota(jnp.int32, (H, LANES), 1)
    return jnp.sum(jnp.where(at == lane, row, 0.0), 1, keepdims=True)


def stacked_weights(w_ref):
    part = [w_ref[:, p * H : (p + 1) * H].astype(F32).T.astype(BF16) for p in range(4)]
    return jnp.concatenate(
        [jnp.concatenate([part[0], part[2]], 1), jnp.concatenate([part[1], part[3]], 1)], 0
    )


def project_kernel(mask_s, mask_ref, pair_ref, gain_ref, bias_ref, w_ref,
                   send_ref, normed_ref, pg_ref, pvg_ref, scratch):
    row = lax.axis_index("row")
    col = lax.axis_index("col")
    weights = stacked_weights(w_ref)
    at = lax.broadcasted_iota(jnp.int32, (N, LANES), 0)
    lane = lax.rem(lax.broadcasted_iota(jnp.int32, (N, LANES), 1), HALF)
    pick = jnp.where((at == col * B + lane) & (lane < B), 1.0, 0.0).astype(BF16)
    mask_row = jnp.broadcast_to(mask_ref[...].astype(F32), (8, N)).astype(BF16)
    col_mask = dot(mask_row, pick, NN)[0:1, :]
    gain, bias = gain_ref[...], bias_ref[...]
    for pair_at in range(A // 2):
        rows = pl.ds(pair_at * 2 * B, 2 * B)
        x = pair_ref[rows, :].astype(F32)
        center = x - jnp.mean(x, 1, keepdims=True)
        scale = lax.rsqrt(jnp.mean(center * center, 1, keepdims=True) + EPS)
        normed = (center * scale * gain + bias).astype(BF16)
        normed_ref[rows, :] = normed
        cells = jnp.concatenate([two_sided(normed[:B]), two_sided(normed[B:])], 0)
        pre = dot(weights, cells, NT)
        for k in range(2):
            a = pair_at * 2 + k
            value = pre[:H, k * LANES : (k + 1) * LANES]
            gate = jax.nn.sigmoid(pre[H:, k * LANES : (k + 1) * LANES])
            seen = col_mask * mask_s[row * A + a].astype(F32)
            pg = gate * seen
            out = pg * value
            pg_ref[a] = pg
            pvg_ref[a] = out * (1.0 - gate)
            scratch[pl.ds(a, H, stride=A), :] = out
    send_ref[...] = scratch[...].astype(BF16)


def gate_kernel(normed_ref, w_ref, cot_ref, w_out_ref, gain_ref, sig_ref, dproj_ref, wt_ref):
    gain = column(gain_ref[...])
    w_og = w_ref[:, 4 * H :]
    w_out = w_out_ref[...]
    sig = jax.nn.sigmoid(dot(normed_ref[...], w_og, NN))
    sig_ref[...] = sig
    dproj_ref[...] = (cot_ref[...].astype(F32) * sig).astype(BF16)
    for q in range(16):
        wt_ref[q] = dot(w_out, row_cells(dproj_ref, q), NT) * gain


def row_cells(ref, q):
    low = pad_cells(ref[q * B : (q + 1) * B, :])
    high = pad_cells(ref[(q + 16) * B : (q + 17) * B, :]) if q < 8 else jnp.zeros_like(low)
    return jnp.concatenate([low, high], 0)


def mix_kernel(recv_ref, send_ref, left_ref, right_ref, mixed):
    right_ref[...] = jnp.zeros_like(right_ref)
    low = lane_low((A, LANES))
    for r2 in range(NR // 2):
        for p in range(NC // 2):
            lefts, rights = [], []
            for r in (2 * r2, 2 * r2 + 1):
                both = recv_ref[pl.ds((r * NC + 2 * p) * A, 2 * A), :].astype(F32)
                x, y = both[:A], both[A:]
                lefts.append(jnp.where(low, x, swap_halves(y)))
                rights.append(jnp.where(low, swap_halves(x), y))
            lanes = slice(p * LANES, (p + 1) * LANES)
            left_ref[r2 * B : (r2 + 1) * B, lanes] = jnp.concatenate(lefts, 0).astype(BF16)
            right_ref[r2 * HALF : r2 * HALF + B, lanes] = jnp.concatenate(rights, 0).astype(BF16)
    mixed[...] = dot(left_ref[...], right_ref[...], NT)
    low = lane_low((8, LANES))
    for r in range(NR):
        for p in range(NC // 2):
            t0, t1, t2 = (
                mixed[r * A + 8 * t : r * A + 8 * t + 8, p * LANES : (p + 1) * LANES]
                for t in range(3)
            )
            rows = jnp.concatenate(
                [jnp.where(low, t0, swap_halves(t2)), t1,
                 jnp.where(low, swap_halves(t0), t2), swap_halves(t1)], 0
            )
            send_ref[pl.ds((r * NC + 2 * p) * 16, 32), :] = rows.astype(BF16)


def norm_cells(x):
    center = x - jnp.mean(x, 0, keepdims=True)
    scale = lax.rsqrt(jnp.mean(center * center, 0, keepdims=True) + EPS)
    return center * scale, scale


def d_mixed_kernel(recv_ref, wt_ref, send_ref, scratch):
    scratch[...] = recv_ref[...].astype(F32)
    for q in range(16):
        normal, scale = norm_cells(scratch[pl.ds(q, H, stride=16), :])
        wt = wt_ref[q]
        d = scale * (
            wt - jnp.mean(wt, 0, keepdims=True) - normal * jnp.mean(wt * normal, 0, keepdims=True)
        )
        scratch[pl.ds(q, H, stride=16), :] = d
    send_ref[...] = scratch[...].astype(BF16)


def update_kernel(recv_ref, w_out_ref, gain_ref, bias_ref, sig_ref, dproj_ref, cot_ref,
                  normed_ref, w_ref, update_ref, dn_ref, grads_ref, scratch, d_og):
    scratch[...] = recv_ref[...].astype(F32)
    gain, bias = column(gain_ref[...]), column(bias_ref[...])
    w_out = w_out_ref[...]
    grad = jnp.zeros((H, H), F32)
    for q in range(16):
        normal, _ = norm_cells(scratch[pl.ds(q, H, stride=16), :])
        normed = (normal * gain + bias).astype(BF16)
        projected = dot(normed, w_out, TN)
        grad = grad + dot(normed, row_cells(dproj_ref, q), NN)
        for k in range(2 if q < 8 else 1):
            rows = pl.ds((q + 16 * k) * B, B)
            sig = sig_ref[rows, :]
            proj = projected[k * HALF : k * HALF + B]
            update_ref[rows, :] = (sig * proj).astype(BF16)
            d_og[rows, :] = (cot_ref[rows, :].astype(F32) * proj * sig * (1.0 - sig)).astype(BF16)
    grads_ref[1] = grad
    grads_ref[0] = dot(d_og[...], normed_ref[...], TN)
    dn_ref[...] = dot(d_og[...], w_ref[:, 4 * H :], NT)


def back_kernel(recv_ref, left_ref, right_ref, send_ref, d_mixed, d_left, d_right):
    low = lane_low((8, LANES))
    for r2 in range(NR // 2):
        for p in range(NC // 2):
            rows = []
            for r in (2 * r2, 2 * r2 + 1):
                both = recv_ref[pl.ds((r * NC + 2 * p) * 16, 32), :].astype(F32)
                x0, x1, y0, y1 = (both[8 * t : 8 * t + 8] for t in range(4))
                rows += [jnp.where(low, x0, swap_halves(y0)), jnp.where(low, x1, swap_halves(y1)),
                         jnp.where(low, swap_halves(x0), y0)]
            d_mixed[r2 * B : (r2 + 1) * B, p * LANES : (p + 1) * LANES] = (
                jnp.concatenate(rows, 0).astype(BF16)
            )
    d = d_mixed[...]
    d_left[...] = dot(d, right_ref[...], NN)
    d_right[...] = dot(d, left_ref[...], TN)
    low = lane_low((A, LANES))
    for r in range(NR):
        for p in range(NC // 2):
            lanes = slice(p * LANES, (p + 1) * LANES)
            x = d_left[r * A : (r + 1) * A, lanes]
            start = (r // 2) * HALF + (r % 2) * A
            y = d_right[start : start + A, lanes]
            rows = jnp.concatenate(
                [jnp.where(low, x, swap_halves(y)), jnp.where(low, swap_halves(x), y)], 0
            )
            send_ref[pl.ds((r * NC + 2 * p) * A, 2 * A), :] = rows.astype(BF16)


def grad_kernel(recv_ref, pg_ref, pvg_ref, normed_ref, grads_ref, send_ref, dvg_ref,
                scratch, packed):
    scratch[...] = recv_ref[...].astype(F32)
    total = jnp.zeros((2 * H, 2 * H), F32)
    for pair_at in range(A // 2):
        sides, cells = [], []
        for k in range(2):
            a = pair_at * 2 + k
            d = scratch[pl.ds(a, H, stride=A), :]
            side = jnp.concatenate([d * pg_ref[a], d * pvg_ref[a]], 0).astype(BF16)
            dvg_ref[a] = side
            sides.append(side)
            cells.append(two_sided(normed_ref[a * B : (a + 1) * B, :]))
        total = total + dot(jnp.concatenate(sides, 1), jnp.concatenate(cells, 0), NN)
    blocks = [total[:H, :H], total[H:, :H], total[:H, H:], total[H:, H:],
              grads_ref[0], grads_ref[1], jnp.zeros((H, H), F32), jnp.zeros((H, H), F32)]
    for g, block in enumerate(blocks):
        packed[pl.ds(g, H, stride=8), :] = block
    send_ref[...] = packed[...].astype(BF16)


def pair_grad_kernel(dvg_ref, dn_ref, pair_ref, gain_ref, w_ref, out_ref):
    weights = stacked_weights(w_ref)
    gain = gain_ref[...]
    for a in range(A):
        rows = pl.ds(a * B, B)
        both = dot(dvg_ref[a], weights, TN)
        d = both[:B, :H] + both[HALF : HALF + B, H:] + dn_ref[rows, :]
        x = pair_ref[rows, :].astype(F32)
        center = x - jnp.mean(x, 1, keepdims=True)
        scale = lax.rsqrt(jnp.mean(center * center, 1, keepdims=True) + EPS)
        normal = center * scale
        weighted = d * gain
        out_ref[rows, :] = (
            scale * (weighted - jnp.mean(weighted, 1, keepdims=True)
                     - normal * jnp.mean(weighted * normal, 1, keepdims=True))
        ).astype(BF16)


def sum_kernel(recv_ref, send_ref):
    total = jnp.sum(recv_ref[...].astype(F32).reshape(ND, 8, LANES), 0)
    twice = jnp.concatenate([total, total], 0).astype(BF16)
    for s in range(ND // 2):
        send_ref[s * 16 : (s + 1) * 16, :] = twice


def unpack_kernel(recv_ref, w_in_ref, w_out_ref, scratch):
    scratch[...] = recv_ref[...].astype(F32)
    for g in range(5):
        w_in_ref[:, g * H : (g + 1) * H] = scratch[pl.ds(g, H, stride=8), :].T
    w_out_ref[...] = scratch[pl.ds(5, H, stride=8), :]


def call(kernel, outs, scratch, args, flops, smem=0):
    in_specs = [pl.BlockSpec(memory_space=pltpu.SMEM)] * smem
    in_specs += [pl.BlockSpec(memory_space=pltpu.VMEM)] * (len(args) - smem)
    size = lambda v: v.size * v.dtype.itemsize
    shapes = [jax.ShapeDtypeStruct(s, d) for s, d in outs]
    total = sum(size(v) for v in args) + sum(size(v) for v in shapes)
    return pl.pallas_call(
        kernel,
        out_shape=shapes,
        in_specs=in_specs,
        out_specs=[pl.BlockSpec(memory_space=pltpu.VMEM)] * len(shapes),
        scratch_shapes=[pltpu.VMEM(s, d) for s, d in scratch],
        cost_estimate=pl.CostEstimate(flops=flops, bytes_accessed=total, transcendentals=0),
        compiler_params=pltpu.CompilerParams(vmem_limit_bytes=40 * 2**20),
    )(*args)


def exchange(x, rows):
    moved = lax.all_to_all(x.reshape(ND, rows, LANES), AXES, 0, 0, tiled=True)
    return moved.reshape(ND * rows, LANES)


def on_device(pair, mask, in_gain, in_bias, w_in, out_gain, out_bias, w_out, cotangent):
    pair2 = pair.reshape(CELLS, H)
    cot2 = cotangent.reshape(CELLS, H)
    line = lambda v: v.reshape(1, -1)
    send, normed, pg, pvg = call(
        project_kernel,
        [((ND * A, LANES), BF16), ((CELLS, H), BF16), ((A, H, LANES), F32), ((A, H, LANES), F32)],
        [((ND * A, LANES), F32)],
        [mask, line(mask), pair2, line(in_gain), line(in_bias), w_in],
        400_000_000, smem=1,
    )
    recv = exchange(send, A)
    sig, dproj, wt = call(
        gate_kernel,
        [((CELLS, H), F32), ((CELLS, H), BF16), ((16, H, LANES), F32)],
        [],
        [normed, w_in, cot2, w_out, line(out_gain)],
        100_000_000,
    )
    send, left, right = call(
        mix_kernel,
        [((ND * 16, LANES), BF16), ((N, 512), BF16), ((512, 512), BF16)],
        [((N, 512), F32)],
        [recv],
        200_000_000,
    )
    mixed = exchange(send, 16)
    (send,) = call(
        d_mixed_kernel, [((ND * 16, LANES), BF16)], [((ND * 16, LANES), F32)], [mixed, wt], 10_000_000
    )
    recv = exchange(send, 16)
    update, dn, grads = call(
        update_kernel,
        [((CELLS, H), BF16), ((CELLS, H), F32), ((2, H, H), F32)],
        [((ND * 16, LANES), F32), ((CELLS, H), BF16)],
        [mixed, w_out, line(out_gain), line(out_bias), sig, dproj, cot2, normed, w_in],
        200_000_000,
    )
    (send,) = call(
        back_kernel,
        [((ND * A, LANES), BF16)],
        [((N, 512), BF16), ((N, 512), F32), ((512, 512), F32)],
        [recv, left, right],
        400_000_000,
    )
    recv = exchange(send, A)
    send, dvg = call(
        grad_kernel,
        [((ND * 8, LANES), BF16), ((A, 2 * H, LANES), BF16)],
        [((ND * A, LANES), F32), ((ND * 8, LANES), F32)],
        [recv, pg, pvg, normed, grads],
        400_000_000,
    )
    recv = exchange(send, 8)
    (pair_grad,) = call(
        pair_grad_kernel, [((CELLS, H), BF16)], [], [dvg, dn, pair2, line(in_gain), w_in], 400_000_000
    )
    (send,) = call(sum_kernel, [((ND * 8, LANES), BF16)], [], [recv], 1_000_000)
    recv = exchange(send, 8)
    w_in_grad, w_out_grad = call(
        unpack_kernel,
        [((H, 5 * H), F32), ((H, H), F32)],
        [((ND * 8, LANES), F32)],
        [recv],
        1_000_000,
    )
    return (update.reshape(A, B, H), pair_grad.reshape(A, B, H), w_in_grad, w_out_grad)


def solution(mesh):
    placed = (P("row", "col", None), P(), P(), P(), P(), P(), P(), P(), P("row", "col", None))
    return jax.shard_map(
        on_device,
        mesh=mesh,
        in_specs=placed,
        out_specs=(P("row", "col", None), P("row", "col", None), P(), P()),
        check_vma=False,
    )
```

```python
import jax
import jax.numpy as jnp
from jax import lax
from jax.experimental import pallas as pl
from jax.experimental.pallas import tpu as pltpu
from jax.sharding import PartitionSpec as P

F32 = jnp.float32
BF16 = jnp.bfloat16
EPS = 1e-05
AXES = ("row", "col")

A, B, HALF, LANES = 24, 48, 64, 128
NR, NC, ND = 16, 8, 128
CELLS = A * B
H = 128
N = NR * A
BOTH, ONE, SUMS = 18, 12, 6
GROUP = NC * BOTH
SINGLE = NC * ONE

NT = ((1,), (1,))
TN = ((0,), (0,))
NN = ((1,), (0,))
VMEM_SPEC = pl.BlockSpec(memory_space=pltpu.VMEM)
HBM_SPEC = pl.BlockSpec(memory_space=pltpu.HBM)


def dot(x, y, contract):
    return lax.dot_general(x, y, (contract, ((), ())), preferred_element_type=F32)


def roll(x, shift):
    return pltpu.roll(x, shift % LANES, x.ndim - 1)


def lane_of(shape):
    return lax.broadcasted_iota(jnp.int32, shape, len(shape) - 1)


def two_sided(x):
    none = jnp.zeros_like(x)
    rest = jnp.zeros((LANES - 2 * B, 2 * x.shape[1]), x.dtype)
    return jnp.concatenate(
        [jnp.concatenate([x, none], 1), jnp.concatenate([none, x], 1), rest], 0
    )


def row_cells(ref, q):
    none = jnp.zeros((HALF - B, H), BF16)
    return jnp.concatenate(
        [ref[q * B : (q + 1) * B, :], none, ref[(q + ONE) * B : (q + ONE + 1) * B, :], none], 0
    )


def column(row):
    at = lax.broadcasted_iota(jnp.int32, (H, LANES), 0)
    return jnp.sum(jnp.where(at == lane_of((H, LANES)), row, 0.0), 1, keepdims=True)


def stacked_weights(w_ref, first, second):
    part = [w_ref[:, p * H : (p + 1) * H].astype(F32).T.astype(BF16) for p in range(4)]
    value = jnp.concatenate([part[2 * first], part[2 * second]], 1)
    gate = jnp.concatenate([part[2 * first + 1], part[2 * second + 1]], 1)
    return jnp.concatenate([value, gate], 0)


def column_mask(mask_s):
    start = lax.axis_index("col") * B
    lane = lane_of((8, LANES))
    place = jnp.where(lane < B, lane, lane - B)
    out = jnp.zeros((8, LANES), F32)
    for b in range(B):
        out = jnp.where(place == b, mask_s[start + b].astype(F32), out)
    return out[0:1, :]


def gate_parts(weights, normed, pair_at, col_mask, mask_s):
    cells = jnp.concatenate([two_sided(normed[:B]), two_sided(normed[B:])], 0)
    pre = dot(weights, cells, NT)
    start = lax.axis_index("row") * A
    for k in range(2):
        value = pre[:H, k * LANES : (k + 1) * LANES]
        gate = jax.nn.sigmoid(pre[H:, k * LANES : (k + 1) * LANES])
        seen = col_mask * mask_s[start + 2 * pair_at + k].astype(F32)
        yield value, gate, gate * seen


def pack_both(block, third, a):
    shift = LANES - 32 if a < 8 else HALF
    return jnp.where(lane_of(block.shape) < 2 * B, block, roll(third, shift))


def pack_tail(third, n):
    lane = lane_of(third(n).shape)
    out = roll(third(n), -HALF)
    for m in range(1, 4):
        out = jnp.where(lane >= 32 * m, roll(third(2 * m + n), 32 * m - HALF), out)
    return out


def unpack_third(block, s):
    first, second, last = block(s), block(8 + s), block(16 + s % 2)
    lane = lane_of(first.shape)
    return jnp.where(
        lane < 32, roll(first, 32),
        jnp.where(lane < HALF, roll(second, HALF), roll(last, HALF - 32 * (s // 2))),
    )


def norm_rows(x):
    center = x - jnp.mean(x, 1, keepdims=True)
    scale = lax.rsqrt(jnp.mean(center * center, 1, keepdims=True) + EPS)
    return center * scale, scale


def norm_cells(x):
    center = x - jnp.mean(x, 0, keepdims=True)
    scale = lax.rsqrt(jnp.mean(center * center, 0, keepdims=True) + EPS)
    return center * scale, scale


def project_kernel(mask_h, pair_h, gain_h, bias_h, w_h, send_ref, normed_ref,
                   mask_s, pair_v, gain_v, bias_v, w_v, third, scratch, sems):
    copies = [
        pltpu.make_async_copy(src, dst, sems.at[n])
        for n, (src, dst) in enumerate(
            [(w_h, w_v), (pair_h, pair_v), (mask_h, mask_s), (gain_h, gain_v), (bias_h, bias_v)]
        )
    ]
    for copy in copies:
        copy.start()
    for copy in copies:
        copy.wait()
    weights = stacked_weights(w_v, 0, 1)
    col_mask = column_mask(mask_s)
    gain, bias = gain_v[...], bias_v[...]
    for pair_at in (8, 9, 10, 11, 0, 1, 2, 3, 4, 5, 6, 7):
        rows = pl.ds(pair_at * 2 * B, 2 * B)
        normal, _ = norm_rows(pair_v[rows, :].astype(F32))
        normed = (normal * gain + bias).astype(BF16)
        normed_ref[rows, :] = normed
        for k, (value, _, pg) in enumerate(gate_parts(weights, normed, pair_at, col_mask, mask_s)):
            a = pair_at * 2 + k
            if a >= 16:
                third[a - 16] = pg * value
            else:
                scratch[pl.ds(a, H, stride=BOTH), :] = pack_both(pg * value, third[a % 8], a)
        if pair_at == 11:
            for n in range(2):
                scratch[pl.ds(16 + n, H, stride=BOTH), :] = pack_tail(lambda s: third[s], n)
    send_ref[...] = scratch[...].astype(BF16)


def gate_kernel(normed_ref, w_ref, cot_ref, pair_ref, dproj_ref, normal_ref, scale_ref):
    sig = jax.nn.sigmoid(dot(normed_ref[...], w_ref[:, 4 * H :], NN))
    dproj_ref[...] = (cot_ref[...].astype(F32) * sig).astype(BF16)
    normal, scale = norm_rows(pair_ref[...].astype(F32))
    normal_ref[...] = normal
    scale_ref[...] = jnp.broadcast_to(scale, (CELLS, H))


def order_matrix():
    target = lax.broadcasted_iota(jnp.int32, (512, N), 0)
    at = lax.broadcasted_iota(jnp.int32, (512, N), 1)
    a, r = at >> 4, at & 15
    place = (r >> 1) * HALF + (r & 1) * A + a
    return jnp.where(target == place, 1.0, 0.0).astype(BF16)


def mix_kernel(recv_ref, send_ref, both_h, order_ref, scratch, both, right, mixed, out, sem):
    scratch[...] = recv_ref[...].astype(F32)
    lane = lane_of((NR, LANES))
    for c in range(NC):
        block = lambda p: scratch[pl.ds(c * BOTH + p, NR, stride=GROUP), :]
        lanes = slice(c * LANES, (c + 1) * LANES)
        for a in range(A):
            x = block(a) if a < 16 else unpack_third(block, a - 16)
            rows = slice(a * NR, (a + 1) * NR)
            both[rows, lanes] = x.astype(BF16)
            right[rows, lanes] = jnp.where(lane < B, roll(x, -B), 0.0).astype(BF16)
    copy = pltpu.make_async_copy(both, both_h, sem)
    copy.start()
    order = order_matrix()
    order_ref[...] = order
    product = dot(both[...], right[...], NT).astype(BF16)
    mixed[...] = dot(product, order, NT)
    low = lane < HALF
    for q in range(ONE):
        for p in range(NC // 2):
            lanes = slice(p * LANES, (p + 1) * LANES)
            x = mixed[q * NR : (q + 1) * NR, lanes]
            y = mixed[(q + ONE) * NR : (q + ONE + 1) * NR, lanes]
            out[pl.ds(2 * p * ONE + q, NR, stride=SINGLE), :] = jnp.where(low, x, roll(y, HALF))
            out[pl.ds((2 * p + 1) * ONE + q, NR, stride=SINGLE), :] = jnp.where(low, roll(x, HALF), y)
    send_ref[...] = out[...].astype(BF16)
    copy.wait()


def d_mixed_kernel(recv_ref, dproj_ref, w_out_ref, gain_ref, send_ref, scratch):
    scratch[...] = recv_ref[...].astype(F32)
    gain = column(gain_ref[...])
    w_out = w_out_ref[...]
    for q in range(ONE):
        wt = dot(w_out, row_cells(dproj_ref, q), NT) * gain
        normal, scale = norm_cells(scratch[pl.ds(q, H, stride=ONE), :])
        scratch[pl.ds(q, H, stride=ONE), :] = scale * (
            wt - jnp.mean(wt, 0, keepdims=True) - normal * jnp.mean(wt * normal, 0, keepdims=True)
        )
    send_ref[...] = scratch[...].astype(BF16)


def update_kernel(mask_s, recv_ref, w_out_ref, gain_ref, bias_ref, dproj_ref, cot_ref,
                  normed_ref, w_ref, update_ref, d_og_ref, grads_ref, pg_h, pvg_h,
                  scratch, pg_v, pvg_v, sems):
    weights = stacked_weights(w_ref, 1, 0)
    col_mask = column_mask(mask_s)
    for pair_at in range(A // 2):
        normed = normed_ref[pl.ds(pair_at * 2 * B, 2 * B), :]
        for k, (value, gate, pg) in enumerate(gate_parts(weights, normed, pair_at, col_mask, mask_s)):
            pg_v[2 * pair_at + k] = pg.astype(BF16)
            pvg_v[2 * pair_at + k] = (pg * value * (1.0 - gate)).astype(BF16)
    copies = [pltpu.make_async_copy(pg_v, pg_h, sems.at[0]),
              pltpu.make_async_copy(pvg_v, pvg_h, sems.at[1])]
    for copy in copies:
        copy.start()
    scratch[...] = recv_ref[...].astype(F32)
    gain, bias = column(gain_ref[...]), column(bias_ref[...])
    w_out, w_og = w_out_ref[...], w_ref[:, 4 * H :]
    grad = jnp.zeros((H, H), F32)
    for q in range(ONE):
        normal, _ = norm_cells(scratch[pl.ds(q, H, stride=ONE), :])
        out_normed = (normal * gain + bias).astype(BF16)
        projected = dot(out_normed, w_out, TN)
        grad = grad + dot(out_normed, row_cells(dproj_ref, q), NN)
        for k in range(2):
            rows = pl.ds((q + ONE * k) * B, B)
            sig = jax.nn.sigmoid(dot(normed_ref[rows, :], w_og, NN))
            proj = projected[k * HALF : k * HALF + B]
            update_ref[rows, :] = (sig * proj).astype(BF16)
            d_og_ref[rows, :] = (
                cot_ref[rows, :].astype(F32) * proj * sig * (1.0 - sig)
            ).astype(BF16)
    grads_ref[0] = dot(d_og_ref[...], normed_ref[...], TN)
    grads_ref[1] = grad
    for copy in copies:
        copy.wait()


def back_kernel(recv_ref, both_h, order_ref, send_ref, both, scratch, d_tile, first, second, out, sem):
    copy = pltpu.make_async_copy(both_h, both, sem)
    copy.start()
    scratch[...] = recv_ref[...].astype(F32)
    low = lane_of((NR, LANES)) < HALF
    for q in range(ONE):
        for p in range(NC // 2):
            lanes = slice(p * LANES, (p + 1) * LANES)
            x = scratch[pl.ds(2 * p * ONE + q, NR, stride=SINGLE), :]
            y = scratch[pl.ds((2 * p + 1) * ONE + q, NR, stride=SINGLE), :]
            d_tile[q * NR : (q + 1) * NR, lanes] = jnp.where(low, x, roll(y, HALF)).astype(BF16)
            d_tile[(q + ONE) * NR : (q + ONE + 1) * NR, lanes] = (
                jnp.where(low, roll(x, HALF), y).astype(BF16)
            )
    d = dot(d_tile[...], order_ref[...], NN).astype(BF16)
    copy.wait()
    first[...] = dot(d, both[...], TN)
    second[...] = dot(d, both[...], NN)
    lane = lane_of((NR, LANES))
    for c in range(NC):
        lanes = slice(c * LANES, (c + 1) * LANES)

        def block(a):
            rows = slice(a * NR, (a + 1) * NR)
            return jnp.where(lane < B, first[rows, lanes], second[rows, lanes])

        third = [block(16 + s) for s in range(8)]
        for a in range(16):
            out[pl.ds(c * BOTH + a, NR, stride=GROUP), :] = pack_both(block(a), third[a % 8], a)
        for n in range(2):
            out[pl.ds(c * BOTH + 16 + n, NR, stride=GROUP), :] = pack_tail(lambda s: third[s], n)
    send_ref[...] = out[...].astype(BF16)


def start_gates(pg_h, pvg_h, pg_v, pvg_v, sems):
    copies = []
    for pair_at in range(A // 2):
        part = pl.ds(2 * pair_at, 2)
        two = [pltpu.make_async_copy(src.at[part], dst.at[part], sems.at[n, pair_at])
               for n, (src, dst) in enumerate([(pg_h, pg_v), (pvg_h, pvg_v)])]
        for copy in two:
            copy.start()
        copies.append(two)
    return copies


def gated(scratch, a, pg_v, pvg_v):
    block = lambda p: scratch[pl.ds(p, H, stride=BOTH), :]
    d = block(a) if a < 16 else unpack_third(block, a - 16)
    return jnp.concatenate([d * pg_v[a].astype(F32), d * pvg_v[a].astype(F32)], 0).astype(BF16)


def grad_kernel(recv_ref, pg_h, pvg_h, normed_ref, grads_ref, send_ref,
                scratch, packed, pg_v, pvg_v, sems):
    copies = start_gates(pg_h, pvg_h, pg_v, pvg_v, sems)
    scratch[...] = recv_ref[...].astype(F32)
    packed[pl.ds(4, H, stride=SUMS), :] = grads_ref[0]
    packed[pl.ds(5, H, stride=SUMS), :] = grads_ref[1]
    total = jnp.zeros((2 * H, 2 * H), F32)
    for pair_at in range(A // 2):
        for copy in copies[pair_at]:
            copy.wait()
        a = 2 * pair_at
        sides = [gated(scratch, a + k, pg_v, pvg_v) for k in range(2)]
        cells = [two_sided(normed_ref[(a + k) * B : (a + k + 1) * B, :]) for k in range(2)]
        total = total + dot(jnp.concatenate(sides, 1), jnp.concatenate(cells, 0), NN)
    for g, block in enumerate([total[:H, H:], total[H:, H:], total[:H, :H], total[H:, :H]]):
        packed[pl.ds(g, H, stride=SUMS), :] = block
    send_ref[...] = packed[...].astype(BF16)


def pair_grad_kernel(recv_ref, pg_h, pvg_h, d_og_ref, normal_ref, scale_ref, gain_ref, w_ref,
                     out_ref, scratch, pg_v, pvg_v, sems):
    copies = start_gates(pg_h, pvg_h, pg_v, pvg_v, sems)
    scratch[...] = recv_ref[...].astype(F32)
    weights = stacked_weights(w_ref, 1, 0)
    w_og = w_ref[:, 4 * H :]
    gain = gain_ref[...]
    for a in range(A):
        if a % 2 == 0:
            for copy in copies[a // 2]:
                copy.wait()
        rows = pl.ds(a * B, B)
        both = dot(gated(scratch, a, pg_v, pvg_v), weights, TN)
        d = both[:B, :H] + both[B : 2 * B, H:] + dot(d_og_ref[rows, :], w_og, NT)
        normal = normal_ref[rows, :]
        weighted = d * gain
        out_ref[rows, :] = (
            scale_ref[rows, :] * (weighted - jnp.mean(weighted, 1, keepdims=True)
                                  - normal * jnp.mean(weighted * normal, 1, keepdims=True))
        ).astype(BF16)


def sum_kernel(recv_ref, send_ref):
    parts = jnp.sum(recv_ref[...].astype(F32).reshape(16, 8 * SUMS, LANES), 0)
    total = parts[:SUMS]
    for k in range(1, 8):
        total = total + parts[k * SUMS : (k + 1) * SUMS]
    many = jnp.concatenate([total] * 8, 0).astype(BF16)
    for s in range(16):
        send_ref[s * 8 * SUMS : (s + 1) * 8 * SUMS, :] = many


def unpack_kernel(recv_ref, w_in_ref, w_out_ref, scratch):
    scratch[...] = recv_ref[...].astype(F32)
    for g in range(5):
        w_in_ref[:, g * H : (g + 1) * H] = scratch[pl.ds(g, H, stride=SUMS), :].T
    w_out_ref[...] = scratch[pl.ds(5, H, stride=SUMS), :]


def call(kernel, args, outs, scratch, flops, hbm_in=(), smem_in=(), hbm_out=()):
    shapes = [jax.ShapeDtypeStruct(s, d) for s, d in outs]
    specs = [
        HBM_SPEC if n in hbm_in else pl.BlockSpec(memory_space=pltpu.SMEM) if n in smem_in else VMEM_SPEC
        for n in range(len(args))
    ]
    moved = sum(v.size * v.dtype.itemsize for v in list(args) + shapes)
    return pl.pallas_call(
        kernel,
        out_shape=shapes,
        in_specs=specs,
        out_specs=[HBM_SPEC if n in hbm_out else VMEM_SPEC for n in range(len(shapes))],
        scratch_shapes=scratch,
        cost_estimate=pl.CostEstimate(flops=flops, bytes_accessed=moved, transcendentals=0),
        compiler_params=pltpu.CompilerParams(vmem_limit_bytes=40 * 2**20),
    )(*args)


def vm(*shape, dtype=F32):
    return pltpu.VMEM(shape, dtype)


def exchange(x, *tile):
    moved = lax.all_to_all(x.reshape(ND, *tile, LANES), AXES, 0, 0, tiled=True)
    return moved.reshape(x.shape)


def on_device(pair, mask, in_gain, in_bias, w_in, out_gain, out_bias, w_out, cotangent):
    pair2 = pair.reshape(CELLS, H)
    cot2 = cotangent.reshape(CELLS, H)
    line = lambda v: v.reshape(1, -1)
    dma = pltpu.SemaphoreType.DMA
    both_shape, one_shape, sum_shape = ((ND * n, LANES) for n in (BOTH, ONE, SUMS))
    gates = [vm(A, H, LANES, dtype=BF16)] * 2

    send, normed = call(
        project_kernel,
        [mask, pair2, line(in_gain), line(in_bias), w_in],
        [(both_shape, BF16), ((CELLS, H), BF16)],
        [pltpu.SMEM((N,), jnp.int32), vm(CELLS, H, dtype=BF16), vm(1, H), vm(1, H),
         vm(H, 5 * H, dtype=BF16), vm(8, H, LANES), vm(*both_shape), dma((5,))],
        400_000_000, hbm_in=range(5),
    )
    recv = exchange(send, 9, 2)
    dproj, normal, scale = call(
        gate_kernel,
        [normed, w_in, cot2, pair2],
        [((CELLS, H), BF16), ((CELLS, H), F32), ((CELLS, H), F32)],
        [],
        100_000_000,
    )
    send, both, order = call(
        mix_kernel,
        [recv],
        [(one_shape, BF16), ((N, NC * LANES), BF16), ((512, N), BF16)],
        [vm(*both_shape), vm(N, NC * LANES, dtype=BF16), vm(N, NC * LANES, dtype=BF16),
         vm(N, 512), vm(*one_shape), dma],
        400_000_000, hbm_out=(1,),
    )
    mixed = exchange(send, 3, 4)
    (send,) = call(
        d_mixed_kernel,
        [mixed, dproj, w_out, line(out_gain)],
        [(one_shape, BF16)],
        [vm(*one_shape)],
        50_000_000,
    )
    recv = exchange(send, 3, 4)
    update, d_og, grads, pg, pvg = call(
        update_kernel,
        [mask, mixed, w_out, line(out_gain), line(out_bias), dproj, cot2, normed, w_in],
        [((CELLS, H), BF16), ((CELLS, H), BF16), ((2, H, H), F32),
         ((A, H, LANES), BF16), ((A, H, LANES), BF16)],
        [vm(*one_shape), *gates, dma((2,))],
        600_000_000, smem_in=(0,), hbm_out=(3, 4),
    )
    (send,) = call(
        back_kernel,
        [recv, both, order],
        [(both_shape, BF16)],
        [vm(N, NC * LANES, dtype=BF16), vm(*one_shape), vm(N, 512, dtype=BF16),
         vm(N, NC * LANES), vm(N, NC * LANES), vm(*both_shape), dma],
        800_000_000, hbm_in=(1,),
    )
    recv = exchange(send, 9, 2)
    (send,) = call(
        grad_kernel,
        [recv, pg, pvg, normed, grads],
        [(sum_shape, BF16)],
        [vm(*both_shape), vm(*sum_shape), *gates, dma((2, A // 2))],
        400_000_000, hbm_in=(1, 2),
    )
    parts = exchange(send, 3, 2)
    (pair_grad,) = call(
        pair_grad_kernel,
        [recv, pg, pvg, d_og, normal, scale, line(in_gain), w_in],
        [((CELLS, H), BF16)],
        [vm(*both_shape), *gates, dma((2, A // 2))],
        400_000_000, hbm_in=(1, 2),
    )
    (send,) = call(sum_kernel, [parts], [(sum_shape, BF16)], [], 1_000_000)
    sums = exchange(send, 3, 2)
    w_in_grad, w_out_grad = call(
        unpack_kernel,
        [sums],
        [((H, 5 * H), F32), ((H, H), F32)],
        [vm(*sum_shape)],
        1_000_000,
    )
    return (update.reshape(A, B, H), pair_grad.reshape(A, B, H), w_in_grad, w_out_grad)


def solution(mesh):
    placed = (P("row", "col", None), P(), P(), P(), P(), P(), P(), P(), P("row", "col", None))
    return jax.shard_map(
        on_device,
        mesh=mesh,
        in_specs=placed,
        out_specs=(P("row", "col", None), P("row", "col", None), P(), P()),
        check_vma=False,
    )
```

```python
import math

import jax
import jax.numpy as jnp
from jax import lax
from jax.experimental import pallas as pl
from jax.experimental.pallas import tpu as pltpu
from jax.sharding import PartitionSpec as P

F32 = jnp.float32
BF16 = jnp.bfloat16
EPS = 1e-05
AXES = ("row", "col")

A, B, HALF, LANES = 24, 48, 64, 128
NR, NC, ND = 16, 8, 128
CELLS = A * B
H = 128
N = NR * A
BOTH, ONE, SUMS = 18, 12, 6

NT = ((1,), (1,))
TN = ((0,), (0,))
NN = ((1,), (0,))
VMEM_SPEC = pl.BlockSpec(memory_space=pltpu.VMEM)
HBM_SPEC = pl.BlockSpec(memory_space=pltpu.HBM)


def dot(x, y, contract):
    return lax.dot_general(x, y, (contract, ((), ())), preferred_element_type=F32)


def roll(x, shift):
    return pltpu.roll(x, shift % LANES, x.ndim - 1)


def lane_of(shape):
    return lax.broadcasted_iota(jnp.int32, shape, len(shape) - 1)


def two_sided(x):
    none = jnp.zeros_like(x)
    rest = jnp.zeros((LANES - 2 * B, 2 * x.shape[1]), x.dtype)
    return jnp.concatenate(
        [jnp.concatenate([x, none], 1), jnp.concatenate([none, x], 1), rest], 0
    )


def row_cells(ref, q):
    none = jnp.zeros((HALF - B, H), BF16)
    return jnp.concatenate(
        [ref[q * B : (q + 1) * B, :], none, ref[(q + ONE) * B : (q + ONE + 1) * B, :], none], 0
    )


def column(row):
    at = lax.broadcasted_iota(jnp.int32, (H, LANES), 0)
    return jnp.sum(jnp.where(at == lane_of((H, LANES)), row, 0.0), 1, keepdims=True)


def stacked_weights(w_ref):
    part = [w_ref[:, p * H : (p + 1) * H].astype(F32).T.astype(BF16) for p in range(4)]
    return jnp.concatenate(
        [jnp.concatenate([part[0], part[2]], 1), jnp.concatenate([part[1], part[3]], 1)], 0
    )


def column_mask(mask_s):
    start = lax.axis_index("col") * B
    lane = lane_of((8, LANES))
    place = jnp.where(lane < B, lane, lane - B)
    out = jnp.zeros((8, LANES), F32)
    for b in range(B):
        out = jnp.where(place == b, mask_s[start + b].astype(F32), out)
    return out[0:1, :]


def gate_parts(weights, normed, pair_at, col_mask, mask_s):
    cells = jnp.concatenate([two_sided(normed[:B]), two_sided(normed[B:])], 0)
    pre = dot(weights, cells, NT)
    start = lax.axis_index("row") * A
    for k in range(2):
        value = pre[:H, k * LANES : (k + 1) * LANES]
        gate = jax.nn.sigmoid(pre[H:, k * LANES : (k + 1) * LANES])
        seen = col_mask * mask_s[start + 2 * pair_at + k].astype(F32)
        yield value, gate, gate * seen


def pack_both(block, third, a):
    shift = LANES - 32 if a < 8 else HALF
    return jnp.where(lane_of(block.shape) < 2 * B, block, roll(third, shift))


def pack_tail(third, n):
    lane = lane_of((H, LANES))
    out = roll(third[4 * n], -HALF)
    for m in range(1, 4):
        out = jnp.where(lane >= 32 * m, roll(third[4 * n + m], 32 * m - HALF), out)
    return out


def unpack_third(block, s):
    first, second, last = block(s), block(8 + s), block(16 + s // 4)
    lane = lane_of(first.shape)
    return jnp.where(
        lane < 32, roll(first, 32),
        jnp.where(lane < HALF, roll(second, HALF), roll(last, HALF - 32 * (s % 4))),
    )


def norm_rows(x):
    center = x - jnp.mean(x, 1, keepdims=True)
    scale = lax.rsqrt(jnp.mean(center * center, 1, keepdims=True) + EPS)
    return center * scale, scale


def norm_cells(x):
    center = x - jnp.mean(x, 0, keepdims=True)
    scale = lax.rsqrt(jnp.mean(center * center, 0, keepdims=True) + EPS)
    return center * scale, scale


def project_kernel(mask_h, pair_h, gain_h, bias_h, w_h, send_ref, normed_ref,
                   mask_s, pair_v, gain_v, bias_v, w_v, third, scratch, sems):
    copies = [
        pltpu.make_async_copy(src, dst, sems.at[n])
        for n, (src, dst) in enumerate(
            [(w_h, w_v), (pair_h, pair_v), (mask_h, mask_s), (gain_h, gain_v), (bias_h, bias_v)]
        )
    ]
    for copy in copies:
        copy.start()
    for copy in copies:
        copy.wait()
    weights = stacked_weights(w_v)
    col_mask = column_mask(mask_s)
    gain, bias = gain_v[...], bias_v[...]
    for pair_at in (8, 9, 10, 11, 0, 1, 2, 3, 4, 5, 6, 7):
        rows = pl.ds(pair_at * 2 * B, 2 * B)
        normal, _ = norm_rows(pair_v[rows, :].astype(F32))
        normed = (normal * gain + bias).astype(BF16)
        normed_ref[rows, :] = normed
        for k, (value, _, pg) in enumerate(gate_parts(weights, normed, pair_at, col_mask, mask_s)):
            a = pair_at * 2 + k
            if a >= 16:
                third[a - 16] = pg * value
            else:
                scratch[pl.ds(a, H, stride=BOTH), :] = pack_both(pg * value, third[a % 8], a)
        if pair_at == 11:
            for n in range(2):
                scratch[pl.ds(16 + n, H, stride=BOTH), :] = pack_tail(third, n)
    send_ref[...] = scratch[...].astype(BF16)


def gate_kernel(normed_ref, w_ref, cot_ref, pair_ref, gain_ref,
                dproj_ref, normal_ref, scale_ref, spread_ref):
    spread_ref[...] = jnp.broadcast_to(column(gain_ref[...]), (H, LANES))
    sig = jax.nn.sigmoid(dot(normed_ref[...], w_ref[:, 4 * H :], NN))
    dproj_ref[...] = (cot_ref[...].astype(F32) * sig).astype(BF16)
    normal, scale = norm_rows(pair_ref[...].astype(F32))
    normal_ref[...] = normal
    scale_ref[...] = jnp.broadcast_to(scale, (CELLS, H))


def third_tile(scratch, start, first, second):
    lane, at = lane_of((8, LANES)), lax.broadcasted_iota(jnp.int32, (8, LANES), 0)
    tail = jnp.where(
        at < 4,
        jnp.broadcast_to(scratch[pl.ds(start + 16, 1), :], (8, LANES)),
        jnp.broadcast_to(scratch[pl.ds(start + 17, 1), :], (8, LANES)),
    )
    last = roll(tail, HALF)
    for m in range(1, 4):
        last = jnp.where((at & 3) == m, roll(tail, HALF - 32 * m), last)
    return jnp.where(lane < 32, roll(first, 32), jnp.where(lane < HALF, roll(second, HALF), last))


def store_both(out, start, x):
    lane, at = lane_of((8, LANES)), lax.broadcasted_iota(jnp.int32, (8, LANES), 0)
    t0, t1, t2 = x[:8], x[8:16], x[16:]
    out[pl.ds(start, 8), :] = jnp.where(lane < 2 * B, t0, roll(t2, LANES - 32))
    out[pl.ds(start + 8, 8), :] = jnp.where(lane < 2 * B, t1, roll(t2, HALF))
    tail = jnp.zeros((8, LANES), F32)
    for m in range(4):
        here = ((at & 3) == m) & (lane >= 32 * m) & (lane < 32 * m + 32)
        tail = jnp.where(here, roll(t2, 32 * m - HALF), tail)
    tail = tail + pltpu.roll(tail, 1, 0)
    tail = tail + pltpu.roll(tail, 2, 0)
    out[pl.ds(start + 16, 1), :] = tail[3:4]
    out[pl.ds(start + 17, 1), :] = tail[7:8]


def mix_kernel(recv_ref, send_ref, left_h, right_h, left_ref, right_ref, scratch, mixed, out, sems):
    scratch[...] = recv_ref[...].astype(F32)
    right_ref[...] = jnp.zeros_like(right_ref)
    lane = lane_of((A, LANES))
    for r2 in range(NR // 2):
        for p in range(NC // 2):
            lefts, rights = [], []
            for r in (2 * r2, 2 * r2 + 1):
                two = []
                for c in (2 * p, 2 * p + 1):
                    start = (r * NC + c) * BOTH
                    top = scratch[pl.ds(start, 16), :]
                    two.append(
                        jnp.concatenate([top, third_tile(scratch, start, top[:8], top[8:])], 0)
                    )
                x, y = two
                lefts.append(jnp.where(lane < HALF, x, roll(y, HALF)))
                rights.append(
                    jnp.where(
                        lane < HALF,
                        jnp.where(lane < B, roll(x, -B), 0.0),
                        jnp.where(lane < HALF + B, roll(y, HALF - B), 0.0),
                    )
                )
            lanes = slice(p * LANES, (p + 1) * LANES)
            left_ref[r2 * B : (r2 + 1) * B, lanes] = jnp.concatenate(lefts, 0).astype(BF16)
            right_ref[r2 * HALF : r2 * HALF + B, lanes] = jnp.concatenate(rights, 0).astype(BF16)
    copies = [pltpu.make_async_copy(left_ref, left_h, sems.at[0]),
              pltpu.make_async_copy(right_ref, right_h, sems.at[1])]
    for copy in copies:
        copy.start()
    mixed[...] = dot(left_ref[...], right_ref[...], NT)
    low = lane_of((ONE, LANES)) < HALF
    for r in range(NR):
        for p in range(NC // 2):
            lanes = slice(p * LANES, (p + 1) * LANES)
            x = mixed[pl.ds(r * A, ONE), lanes]
            y = mixed[pl.ds(r * A + ONE, ONE), lanes]
            start = (r * NC + 2 * p) * ONE
            out[pl.ds(start, ONE), :] = jnp.where(low, x, roll(y, HALF))
            out[pl.ds(start + ONE, ONE), :] = jnp.where(low, roll(x, HALF), y)
    send_ref[...] = out[...].astype(BF16)
    for copy in copies:
        copy.wait()


def d_mixed_kernel(recv_ref, dproj_ref, w_out_ref, spread_ref, send_ref, scratch):
    scratch[...] = recv_ref[...].astype(F32)
    gain = spread_ref[...]
    w_out = w_out_ref[...]
    for q in range(ONE):
        wt = dot(w_out, row_cells(dproj_ref, q), NT) * gain
        normal, scale = norm_cells(scratch[pl.ds(q, H, stride=ONE), :])
        scratch[pl.ds(q, H, stride=ONE), :] = scale * (
            wt - jnp.mean(wt, 0, keepdims=True) - normal * jnp.mean(wt * normal, 0, keepdims=True)
        )
    send_ref[...] = scratch[...].astype(BF16)


def update_kernel(mask_s, recv_ref, w_out_ref, gain_ref, bias_ref, dproj_ref, cot_ref,
                  normed_ref, w_ref, update_ref, d_og_ref, grads_ref, pg_h, pvg_h,
                  scratch, pg_v, pvg_v, sems):
    weights = stacked_weights(w_ref)
    col_mask = column_mask(mask_s)
    for pair_at in range(A // 2):
        normed = normed_ref[pl.ds(pair_at * 2 * B, 2 * B), :]
        for k, (value, gate, pg) in enumerate(gate_parts(weights, normed, pair_at, col_mask, mask_s)):
            pg_v[2 * pair_at + k] = pg.astype(BF16)
            pvg_v[2 * pair_at + k] = (pg * value * (1.0 - gate)).astype(BF16)
    copies = [pltpu.make_async_copy(pg_v, pg_h, sems.at[0]),
              pltpu.make_async_copy(pvg_v, pvg_h, sems.at[1])]
    for copy in copies:
        copy.start()
    scratch[...] = recv_ref[...].astype(F32)
    gain, bias = column(gain_ref[...]), column(bias_ref[...])
    w_out, w_og = w_out_ref[...], w_ref[:, 4 * H :]
    grad = jnp.zeros((H, H), F32)
    for q in range(ONE):
        normal, _ = norm_cells(scratch[pl.ds(q, H, stride=ONE), :])
        out_normed = (normal * gain + bias).astype(BF16)
        projected = dot(out_normed, w_out, TN)
        grad = grad + dot(out_normed, row_cells(dproj_ref, q), NN)
        for k in range(2):
            rows = pl.ds((q + ONE * k) * B, B)
            sig = jax.nn.sigmoid(dot(normed_ref[rows, :], w_og, NN))
            proj = projected[k * HALF : k * HALF + B]
            update_ref[rows, :] = (sig * proj).astype(BF16)
            d_og_ref[rows, :] = (
                cot_ref[rows, :].astype(F32) * proj * sig * (1.0 - sig)
            ).astype(BF16)
    grads_ref[0] = dot(d_og_ref[...], normed_ref[...], TN).astype(BF16)
    grads_ref[1] = grad.astype(BF16)
    for copy in copies:
        copy.wait()


def back_kernel(recv_ref, left_h, right_h, pg_h, pvg_h, send_ref, pg_ref, pvg_ref,
                left_ref, right_ref, scratch, d_tile, d_left, d_right, out, sems):
    copies = [
        pltpu.make_async_copy(src, dst, sems.at[n])
        for n, (src, dst) in enumerate(
            [(right_h, right_ref), (left_h, left_ref), (pg_h, pg_ref), (pvg_h, pvg_ref)]
        )
    ]
    for copy in copies:
        copy.start()
    scratch[...] = recv_ref[...].astype(F32)
    low = lane_of((ONE, LANES)) < HALF
    for r in range(NR):
        for p in range(NC // 2):
            lanes = slice(p * LANES, (p + 1) * LANES)
            start = (r * NC + 2 * p) * ONE
            x = scratch[pl.ds(start, ONE), :]
            y = scratch[pl.ds(start + ONE, ONE), :]
            d_tile[pl.ds(r * A, ONE), lanes] = jnp.where(low, x, roll(y, HALF))
            d_tile[pl.ds(r * A + ONE, ONE), lanes] = jnp.where(low, roll(x, HALF), y)
    d = d_tile[...].astype(BF16)
    copies[0].wait()
    copies[1].wait()
    d_left[...] = dot(d, right_ref[...], NN)
    d_right[...] = dot(d, left_ref[...], TN)
    lane = lane_of((A, LANES))
    for r in range(NR):
        for p in range(NC // 2):
            lanes = slice(p * LANES, (p + 1) * LANES)
            x = d_left[r * A : (r + 1) * A, lanes]
            at = (r // 2) * HALF + (r % 2) * A
            y = d_right[at : at + A, lanes]
            start = (r * NC + 2 * p) * BOTH
            store_both(out, start, jnp.where(lane < B, x, roll(y, B)))
            store_both(out, start + BOTH, jnp.where(lane < B, roll(x, HALF), roll(y, B - HALF)))
    send_ref[...] = out[...].astype(BF16)
    copies[2].wait()
    copies[3].wait()


def gated(scratch, a, pg_v, pvg_v):
    block = lambda p: scratch[pl.ds(p, H, stride=BOTH), :]
    d = block(a) if a < 16 else unpack_third(block, a - 16)
    return jnp.concatenate([d * pg_v[a].astype(F32), d * pvg_v[a].astype(F32)], 0).astype(BF16)


def grad_kernel(recv_ref, pg_v, pvg_v, normed_ref, grads_ref, send_ref, scratch, packed):
    scratch[...] = recv_ref[...].astype(F32)
    for g in range(2):
        packed[pl.ds(4 + g, H, stride=SUMS), :] = grads_ref[g].astype(F32)
    total = jnp.zeros((2 * H, 2 * H), F32)
    for pair_at in range(A // 2):
        a = 2 * pair_at
        sides = [gated(scratch, a + k, pg_v, pvg_v) for k in range(2)]
        cells = [two_sided(normed_ref[(a + k) * B : (a + k + 1) * B, :]) for k in range(2)]
        total = total + dot(jnp.concatenate(sides, 1), jnp.concatenate(cells, 0), NN)
    for g, block in enumerate([total[:H, :H], total[H:, :H], total[:H, H:], total[H:, H:]]):
        packed[pl.ds(g, H, stride=SUMS), :] = block
    send_ref[...] = packed[...].astype(BF16)


def pair_grad_kernel(recv_ref, pg_h, pvg_h, d_og_ref, normal_ref, scale_ref, gain_ref, w_ref,
                     out_ref, scratch, pg_v, pvg_v, sems):
    copies = [pltpu.make_async_copy(pg_h, pg_v, sems.at[0]),
              pltpu.make_async_copy(pvg_h, pvg_v, sems.at[1])]
    for copy in copies:
        copy.start()
    scratch[...] = recv_ref[...].astype(F32)
    weights = stacked_weights(w_ref)
    w_og = w_ref[:, 4 * H :]
    gain = gain_ref[...]
    for copy in copies:
        copy.wait()
    for a in range(A):
        rows = pl.ds(a * B, B)
        both = dot(gated(scratch, a, pg_v, pvg_v), weights, TN)
        d = both[:B, :H] + both[B : 2 * B, H:] + dot(d_og_ref[rows, :], w_og, NT)
        normal = normal_ref[rows, :]
        weighted = d * gain
        out_ref[rows, :] = (
            scale_ref[rows, :] * (weighted - jnp.mean(weighted, 1, keepdims=True)
                                  - normal * jnp.mean(weighted * normal, 1, keepdims=True))
        ).astype(BF16)


def sum_kernel(recv_ref, send_ref):
    parts = jnp.sum(recv_ref[...].astype(F32).reshape(16, 8 * SUMS, LANES), 0)
    total = parts[:SUMS]
    for k in range(1, 8):
        total = total + parts[k * SUMS : (k + 1) * SUMS]
    many = jnp.concatenate([total] * 8, 0).astype(BF16)
    for s in range(16):
        send_ref[s * 8 * SUMS : (s + 1) * 8 * SUMS, :] = many


def unpack_kernel(recv_ref, w_in_ref, w_out_ref, scratch):
    scratch[...] = recv_ref[...].astype(F32)
    for g in range(5):
        w_in_ref[:, g * H : (g + 1) * H] = scratch[pl.ds(g, H, stride=SUMS), :].T
    w_out_ref[...] = scratch[pl.ds(5, H, stride=SUMS), :]


def call(kernel, args, outs, scratch, flops, hbm_in=(), smem_in=(), hbm_out=()):
    shapes = [
        pltpu.HBM(s, d) if n in hbm_out else jax.ShapeDtypeStruct(s, d)
        for n, (s, d) in enumerate(outs)
    ]
    args = [
        pltpu.with_memory_space_constraint(v, pltpu.HBM) if n in hbm_in else v
        for n, v in enumerate(args)
    ]
    specs = [
        HBM_SPEC if n in hbm_in else pl.BlockSpec(memory_space=pltpu.SMEM) if n in smem_in else VMEM_SPEC
        for n in range(len(args))
    ]
    moved = 2 * (sum(v.size for v in args) + sum(math.prod(s) for s, _ in outs))
    return pl.pallas_call(
        kernel,
        out_shape=shapes,
        in_specs=specs,
        out_specs=[HBM_SPEC if n in hbm_out else VMEM_SPEC for n in range(len(shapes))],
        scratch_shapes=scratch,
        cost_estimate=pl.CostEstimate(flops=flops, bytes_accessed=moved, transcendentals=0),
        compiler_params=pltpu.CompilerParams(vmem_limit_bytes=40 * 2**20),
    )(*args)


def vm(*shape, dtype=F32):
    return pltpu.VMEM(shape, dtype)


def exchange(x, *tile):
    moved = lax.all_to_all(x.reshape(ND, *tile, LANES), AXES, 0, 0, tiled=True)
    return moved.reshape(x.shape)


def on_device(pair, mask, in_gain, in_bias, w_in, out_gain, out_bias, w_out, cotangent):
    pair2 = pair.reshape(CELLS, H)
    cot2 = cotangent.reshape(CELLS, H)
    line = lambda v: v.reshape(1, -1)
    dma = pltpu.SemaphoreType.DMA
    both_shape, one_shape, sum_shape = ((ND * n, LANES) for n in (BOTH, ONE, SUMS))
    gates = [vm(A, H, LANES, dtype=BF16)] * 2

    send, normed = call(
        project_kernel,
        [mask, pair2, line(in_gain), line(in_bias), w_in],
        [(both_shape, BF16), ((CELLS, H), BF16)],
        [pltpu.SMEM((N,), jnp.int32), vm(CELLS, H, dtype=BF16), vm(1, H), vm(1, H),
         vm(H, 5 * H, dtype=BF16), vm(8, H, LANES), vm(*both_shape), dma((5,))],
        400_000_000, hbm_in=range(5),
    )
    recv = exchange(send, 9, 2)
    dproj, normal, scale, spread = call(
        gate_kernel,
        [normed, w_in, cot2, pair2, line(out_gain)],
        [((CELLS, H), BF16), ((CELLS, H), F32), ((CELLS, H), F32), ((H, LANES), F32)],
        [],
        100_000_000,
    )
    send, left, right = call(
        mix_kernel,
        [recv],
        [(one_shape, BF16), ((N, 512), BF16), ((512, 512), BF16)],
        [vm(N, 512, dtype=BF16), vm(512, 512, dtype=BF16), vm(*both_shape), vm(N, 512),
         vm(*one_shape), dma((2,))],
        400_000_000, hbm_out=(1, 2),
    )
    mixed = exchange(send, 3, 4)
    (send,) = call(
        d_mixed_kernel,
        [mixed, dproj, w_out, spread],
        [(one_shape, BF16)],
        [vm(*one_shape)],
        50_000_000,
    )
    recv = exchange(send, 3, 4)
    update, d_og, grads, pg, pvg = call(
        update_kernel,
        [mask, mixed, w_out, line(out_gain), line(out_bias), dproj, cot2, normed, w_in],
        [((CELLS, H), BF16), ((CELLS, H), BF16), ((2, H, H), BF16),
         ((A, H, LANES), BF16), ((A, H, LANES), BF16)],
        [vm(*one_shape), *gates, dma((2,))],
        600_000_000, smem_in=(0,), hbm_out=(3, 4),
    )
    send, pg_near, pvg_near = call(
        back_kernel,
        [recv, left, right, pg, pvg],
        [(both_shape, BF16), ((A, H, LANES), BF16), ((A, H, LANES), BF16)],
        [vm(N, 512, dtype=BF16), vm(512, 512, dtype=BF16), vm(*one_shape), vm(N, 512),
         vm(N, 512), vm(512, 512), vm(*both_shape), dma((4,))],
        800_000_000, hbm_in=(1, 2, 3, 4),
    )
    recv = exchange(send, 9, 2)
    (send,) = call(
        grad_kernel,
        [recv, pg_near, pvg_near, normed, grads],
        [(sum_shape, BF16)],
        [vm(*both_shape), vm(*sum_shape)],
        400_000_000,
    )
    parts = exchange(send, 3, 2)
    (pair_grad,) = call(
        pair_grad_kernel,
        [recv, pg, pvg, d_og, normal, scale, line(in_gain), w_in],
        [((CELLS, H), BF16)],
        [vm(*both_shape), *gates, dma((2,))],
        400_000_000, hbm_in=(1, 2),
    )
    (send,) = call(sum_kernel, [parts], [(sum_shape, BF16)], [], 1_000_000)
    sums = exchange(send, 3, 2)
    w_in_grad, w_out_grad = call(
        unpack_kernel,
        [sums],
        [((H, 5 * H), F32), ((H, H), F32)],
        [vm(*sum_shape)],
        1_000_000,
    )
    return (update.reshape(A, B, H), pair_grad.reshape(A, B, H), w_in_grad, w_out_grad)


def solution(mesh):
    placed = (P("row", "col", None), P(), P(), P(), P(), P(), P(), P(), P("row", "col", None))
    return jax.shard_map(
        on_device,
        mesh=mesh,
        in_specs=placed,
        out_specs=(P("row", "col", None), P("row", "col", None), P(), P()),
        check_vma=False,
    )
```

```python
import math

import jax
import jax.numpy as jnp
from jax import lax
from jax.experimental import pallas as pl
from jax.experimental.pallas import tpu as pltpu
from jax.sharding import PartitionSpec as P

F32 = jnp.float32
BF16 = jnp.bfloat16
EPS = 1e-05
AXES = ("row", "col")

A, B, HALF, LANES = 24, 48, 64, 128
NR, NC, ND = 16, 8, 128
CELLS = A * B
H = 128
N = NR * A
BOTH, ONE, SUMS = 24, 12, 6

NT = ((1,), (1,))
TN = ((0,), (0,))
NN = ((1,), (0,))
VMEM_SPEC = pl.BlockSpec(memory_space=pltpu.VMEM)
HBM_SPEC = pl.BlockSpec(memory_space=pltpu.HBM)


def dot(x, y, contract):
    return lax.dot_general(x, y, (contract, ((), ())), preferred_element_type=F32)


def roll(x, shift):
    return pltpu.roll(x, shift % LANES, x.ndim - 1)


def lane_of(shape):
    return lax.broadcasted_iota(jnp.int32, shape, len(shape) - 1)


def two_sided(x):
    padded = jnp.concatenate([x, jnp.zeros((HALF - B, x.shape[1]), x.dtype)], 0)
    none = jnp.zeros_like(padded)
    return jnp.concatenate(
        [jnp.concatenate([padded, none], 1), jnp.concatenate([none, padded], 1)], 0
    )


def row_cells(ref, q):
    none = jnp.zeros((HALF - B, H), BF16)
    return jnp.concatenate(
        [ref[q * B : (q + 1) * B, :], none, ref[(q + ONE) * B : (q + ONE + 1) * B, :], none], 0
    )


def column(row):
    at = lax.broadcasted_iota(jnp.int32, (H, LANES), 0)
    return jnp.sum(jnp.where(at == lane_of((H, LANES)), row, 0.0), 1, keepdims=True)


def stacked_weights(w_ref):
    part = [w_ref[:, p * H : (p + 1) * H].astype(F32).T.astype(BF16) for p in range(4)]
    return jnp.concatenate(
        [jnp.concatenate([part[0], part[2]], 1), jnp.concatenate([part[1], part[3]], 1)], 0
    )


def column_mask(mask_s):
    start = lax.axis_index("col") * B
    lane = lane_of((8, LANES))
    place = lane & (HALF - 1)
    out = jnp.zeros((8, LANES), F32)
    for b in range(B):
        out = jnp.where(place == b, mask_s[start + b].astype(F32), out)
    return out[0:1, :]


def gate_parts(weights, normed, pair_at, col_mask, mask_s):
    cells = jnp.concatenate([two_sided(normed[:B]), two_sided(normed[B:])], 0)
    pre = dot(weights, cells, NT)
    start = lax.axis_index("row") * A
    for k in range(2):
        value = pre[:H, k * LANES : (k + 1) * LANES]
        gate = jax.nn.sigmoid(pre[H:, k * LANES : (k + 1) * LANES])
        seen = col_mask * mask_s[start + 2 * pair_at + k].astype(F32)
        yield value, gate, gate * seen


def norm_rows(x):
    center = x - jnp.mean(x, 1, keepdims=True)
    scale = lax.rsqrt(jnp.mean(center * center, 1, keepdims=True) + EPS)
    return center * scale, scale


def norm_cells(x):
    center = x - jnp.mean(x, 0, keepdims=True)
    scale = lax.rsqrt(jnp.mean(center * center, 0, keepdims=True) + EPS)
    return center * scale, scale


def project_kernel(mask_h, pair_h, gain_h, bias_h, w_h, send_ref, normed_ref,
                   mask_s, pair_v, gain_v, bias_v, w_v, scratch, sems):
    copies = [
        pltpu.make_async_copy(src, dst, sems.at[n])
        for n, (src, dst) in enumerate(
            [(w_h, w_v), (pair_h, pair_v), (mask_h, mask_s), (gain_h, gain_v), (bias_h, bias_v)]
        )
    ]
    for copy in copies:
        copy.start()
    for copy in copies:
        copy.wait()
    weights = stacked_weights(w_v)
    col_mask = column_mask(mask_s)
    gain, bias = gain_v[...], bias_v[...]
    for pair_at in range(A // 2):
        rows = pl.ds(pair_at * 2 * B, 2 * B)
        normal, _ = norm_rows(pair_v[rows, :].astype(F32))
        normed = (normal * gain + bias).astype(BF16)
        normed_ref[rows, :] = normed
        for k, (value, _, pg) in enumerate(gate_parts(weights, normed, pair_at, col_mask, mask_s)):
            scratch[pl.ds(pair_at * 2 + k, H, stride=BOTH), :] = pg * value
    send_ref[...] = scratch[...].astype(BF16)


def gate_kernel(normed_ref, w_ref, cot_ref, pair_ref, gain_ref,
                dproj_ref, normal_ref, scale_ref, spread_ref):
    spread_ref[...] = jnp.broadcast_to(column(gain_ref[...]), (H, LANES))
    sig = jax.nn.sigmoid(dot(normed_ref[...], w_ref[:, 4 * H :], NN))
    dproj_ref[...] = (cot_ref[...].astype(F32) * sig).astype(BF16)
    normal, scale = norm_rows(pair_ref[...].astype(F32))
    normal_ref[...] = normal
    scale_ref[...] = jnp.broadcast_to(scale, (CELLS, H))


def mix_kernel(recv_ref, send_ref, left_h, right_h, left_ref, right_ref, mixed, out, sems):
    right_ref[...] = jnp.zeros_like(right_ref)
    low = lane_of((A, LANES)) < HALF
    for r2 in range(NR // 2):
        for p in range(NC // 2):
            lefts, rights = [], []
            for r in (2 * r2, 2 * r2 + 1):
                both = recv_ref[pl.ds((r * NC + 2 * p) * BOTH, 2 * BOTH), :].astype(F32)
                x, y = both[:A], both[A:]
                lefts.append(jnp.where(low, x, roll(y, HALF)))
                rights.append(jnp.where(low, roll(x, HALF), y))
            lanes = slice(p * LANES, (p + 1) * LANES)
            left_ref[r2 * B : (r2 + 1) * B, lanes] = jnp.concatenate(lefts, 0).astype(BF16)
            right_ref[r2 * HALF : r2 * HALF + B, lanes] = jnp.concatenate(rights, 0).astype(BF16)
    copies = [pltpu.make_async_copy(left_ref, left_h, sems.at[0]),
              pltpu.make_async_copy(right_ref, right_h, sems.at[1])]
    for copy in copies:
        copy.start()
    mixed[...] = dot(left_ref[...], right_ref[...], NT)
    low = lane_of((ONE, LANES)) < HALF
    for r in range(NR):
        for p in range(NC // 2):
            lanes = slice(p * LANES, (p + 1) * LANES)
            x = mixed[pl.ds(r * A, ONE), lanes]
            y = mixed[pl.ds(r * A + ONE, ONE), lanes]
            start = (r * NC + 2 * p) * ONE
            out[pl.ds(start, ONE), :] = jnp.where(low, x, roll(y, HALF))
            out[pl.ds(start + ONE, ONE), :] = jnp.where(low, roll(x, HALF), y)
    send_ref[...] = out[...].astype(BF16)
    for copy in copies:
        copy.wait()


def d_mixed_kernel(recv_ref, dproj_ref, w_out_ref, spread_ref, send_ref, scratch):
    scratch[...] = recv_ref[...].astype(F32)
    gain = spread_ref[...]
    w_out = w_out_ref[...]
    for q in range(ONE):
        wt = dot(w_out, row_cells(dproj_ref, q), NT) * gain
        normal, scale = norm_cells(scratch[pl.ds(q, H, stride=ONE), :])
        scratch[pl.ds(q, H, stride=ONE), :] = scale * (
            wt - jnp.mean(wt, 0, keepdims=True) - normal * jnp.mean(wt * normal, 0, keepdims=True)
        )
    send_ref[...] = scratch[...].astype(BF16)


def update_kernel(mask_s, recv_ref, w_out_ref, gain_ref, bias_ref, dproj_ref, cot_ref,
                  normed_ref, w_ref, update_ref, d_og_ref, grads_ref, pg_h, pvg_h,
                  scratch, pg_v, pvg_v, sems):
    weights = stacked_weights(w_ref)
    col_mask = column_mask(mask_s)
    for pair_at in range(A // 2):
        normed = normed_ref[pl.ds(pair_at * 2 * B, 2 * B), :]
        for k, (value, gate, pg) in enumerate(gate_parts(weights, normed, pair_at, col_mask, mask_s)):
            pg_v[2 * pair_at + k] = pg.astype(BF16)
            pvg_v[2 * pair_at + k] = (pg * value * (1.0 - gate)).astype(BF16)
    copies = [pltpu.make_async_copy(pg_v, pg_h, sems.at[0]),
              pltpu.make_async_copy(pvg_v, pvg_h, sems.at[1])]
    for copy in copies:
        copy.start()
    scratch[...] = recv_ref[...].astype(F32)
    gain, bias = column(gain_ref[...]), column(bias_ref[...])
    w_out, w_og = w_out_ref[...], w_ref[:, 4 * H :]
    grad = jnp.zeros((H, H), F32)
    for q in range(ONE):
        normal, _ = norm_cells(scratch[pl.ds(q, H, stride=ONE), :])
        out_normed = (normal * gain + bias).astype(BF16)
        projected = dot(out_normed, w_out, TN)
        grad = grad + dot(out_normed, row_cells(dproj_ref, q), NN)
        for k in range(2):
            rows = pl.ds((q + ONE * k) * B, B)
            sig = jax.nn.sigmoid(dot(normed_ref[rows, :], w_og, NN))
            proj = projected[k * HALF : k * HALF + B]
            update_ref[rows, :] = (sig * proj).astype(BF16)
            d_og_ref[rows, :] = (
                cot_ref[rows, :].astype(F32) * proj * sig * (1.0 - sig)
            ).astype(BF16)
    grads_ref[0] = dot(d_og_ref[...], normed_ref[...], TN).astype(BF16)
    grads_ref[1] = grad.astype(BF16)
    for copy in copies:
        copy.wait()


def back_kernel(recv_ref, left_h, right_h, pg_h, pvg_h, send_ref, pg_ref, pvg_ref,
                left_ref, right_ref, scratch, d_tile, d_left, d_right, sems):
    copies = [
        pltpu.make_async_copy(src, dst, sems.at[n])
        for n, (src, dst) in enumerate(
            [(right_h, right_ref), (left_h, left_ref), (pg_h, pg_ref), (pvg_h, pvg_ref)]
        )
    ]
    for copy in copies:
        copy.start()
    scratch[...] = recv_ref[...].astype(F32)
    low = lane_of((ONE, LANES)) < HALF
    for r in range(NR):
        for p in range(NC // 2):
            lanes = slice(p * LANES, (p + 1) * LANES)
            start = (r * NC + 2 * p) * ONE
            x = scratch[pl.ds(start, ONE), :]
            y = scratch[pl.ds(start + ONE, ONE), :]
            d_tile[pl.ds(r * A, ONE), lanes] = jnp.where(low, x, roll(y, HALF))
            d_tile[pl.ds(r * A + ONE, ONE), lanes] = jnp.where(low, roll(x, HALF), y)
    d = d_tile[...].astype(BF16)
    copies[0].wait()
    copies[1].wait()
    d_left[...] = dot(d, right_ref[...], NN)
    d_right[...] = dot(d, left_ref[...], TN)
    low = lane_of((A, LANES)) < HALF
    for r in range(NR):
        for p in range(NC // 2):
            lanes = slice(p * LANES, (p + 1) * LANES)
            x = d_left[r * A : (r + 1) * A, lanes]
            at = (r // 2) * HALF + (r % 2) * A
            y = d_right[at : at + A, lanes]
            rows = jnp.concatenate(
                [jnp.where(low, x, roll(y, HALF)), jnp.where(low, roll(x, HALF), y)], 0
            )
            send_ref[pl.ds((r * NC + 2 * p) * BOTH, 2 * BOTH), :] = rows.astype(BF16)
    copies[2].wait()
    copies[3].wait()


def gated(scratch, a, pg_v, pvg_v):
    d = scratch[pl.ds(a, H, stride=BOTH), :]
    return jnp.concatenate([d * pg_v[a].astype(F32), d * pvg_v[a].astype(F32)], 0).astype(BF16)


def grad_kernel(recv_ref, pg_v, pvg_v, normed_ref, grads_ref, send_ref, scratch, packed):
    scratch[...] = recv_ref[...].astype(F32)
    for g in range(2):
        packed[pl.ds(4 + g, H, stride=SUMS), :] = grads_ref[g].astype(F32)
    total = jnp.zeros((2 * H, 2 * H), F32)
    for pair_at in range(A // 2):
        a = 2 * pair_at
        sides = [gated(scratch, a + k, pg_v, pvg_v) for k in range(2)]
        cells = [two_sided(normed_ref[(a + k) * B : (a + k + 1) * B, :]) for k in range(2)]
        total = total + dot(jnp.concatenate(sides, 1), jnp.concatenate(cells, 0), NN)
    for g, block in enumerate([total[:H, :H], total[H:, :H], total[:H, H:], total[H:, H:]]):
        packed[pl.ds(g, H, stride=SUMS), :] = block
    send_ref[...] = packed[...].astype(BF16)


def pair_grad_kernel(recv_ref, pg_h, pvg_h, d_og_ref, normal_ref, scale_ref, gain_ref, w_ref,
                     out_ref, scratch, pg_v, pvg_v, sems):
    copies = [pltpu.make_async_copy(pg_h, pg_v, sems.at[0]),
              pltpu.make_async_copy(pvg_h, pvg_v, sems.at[1])]
    for copy in copies:
        copy.start()
    scratch[...] = recv_ref[...].astype(F32)
    weights = stacked_weights(w_ref)
    w_og = w_ref[:, 4 * H :]
    gain = gain_ref[...]
    for copy in copies:
        copy.wait()
    for a in range(A):
        rows = pl.ds(a * B, B)
        both = dot(gated(scratch, a, pg_v, pvg_v), weights, TN)
        d = both[:B, :H] + both[HALF : HALF + B, H:] + dot(d_og_ref[rows, :], w_og, NT)
        normal = normal_ref[rows, :]
        weighted = d * gain
        out_ref[rows, :] = (
            scale_ref[rows, :] * (weighted - jnp.mean(weighted, 1, keepdims=True)
                                  - normal * jnp.mean(weighted * normal, 1, keepdims=True))
        ).astype(BF16)


def sum_kernel(recv_ref, send_ref):
    parts = jnp.sum(recv_ref[...].astype(F32).reshape(16, 8 * SUMS, LANES), 0)
    total = parts[:SUMS]
    for k in range(1, 8):
        total = total + parts[k * SUMS : (k + 1) * SUMS]
    many = jnp.concatenate([total] * 8, 0).astype(BF16)
    for s in range(16):
        send_ref[s * 8 * SUMS : (s + 1) * 8 * SUMS, :] = many


def unpack_kernel(recv_ref, w_in_ref, w_out_ref, scratch):
    scratch[...] = recv_ref[...].astype(F32)
    for g in range(5):
        w_in_ref[:, g * H : (g + 1) * H] = scratch[pl.ds(g, H, stride=SUMS), :].T
    w_out_ref[...] = scratch[pl.ds(5, H, stride=SUMS), :]


def call(kernel, args, outs, scratch, flops, hbm_in=(), smem_in=(), hbm_out=()):
    shapes = [
        pltpu.HBM(s, d) if n in hbm_out else jax.ShapeDtypeStruct(s, d)
        for n, (s, d) in enumerate(outs)
    ]
    args = [
        pltpu.with_memory_space_constraint(v, pltpu.HBM) if n in hbm_in else v
        for n, v in enumerate(args)
    ]
    specs = [
        HBM_SPEC if n in hbm_in else pl.BlockSpec(memory_space=pltpu.SMEM) if n in smem_in else VMEM_SPEC
        for n in range(len(args))
    ]
    moved = 2 * (sum(v.size for v in args) + sum(math.prod(s) for s, _ in outs))
    return pl.pallas_call(
        kernel,
        out_shape=shapes,
        in_specs=specs,
        out_specs=[HBM_SPEC if n in hbm_out else VMEM_SPEC for n in range(len(shapes))],
        scratch_shapes=scratch,
        cost_estimate=pl.CostEstimate(flops=flops, bytes_accessed=moved, transcendentals=0),
        compiler_params=pltpu.CompilerParams(vmem_limit_bytes=40 * 2**20),
    )(*args)


def vm(*shape, dtype=F32):
    return pltpu.VMEM(shape, dtype)


def exchange(x, *tile):
    moved = lax.all_to_all(x.reshape(ND, *tile, LANES), AXES, 0, 0, tiled=True)
    return moved.reshape(x.shape)


def on_device(pair, mask, in_gain, in_bias, w_in, out_gain, out_bias, w_out, cotangent):
    pair2 = pair.reshape(CELLS, H)
    cot2 = cotangent.reshape(CELLS, H)
    line = lambda v: v.reshape(1, -1)
    dma = pltpu.SemaphoreType.DMA
    both_shape, one_shape, sum_shape = ((ND * n, LANES) for n in (BOTH, ONE, SUMS))
    gates = [vm(A, H, LANES, dtype=BF16)] * 2

    send, normed = call(
        project_kernel,
        [mask, pair2, line(in_gain), line(in_bias), w_in],
        [(both_shape, BF16), ((CELLS, H), BF16)],
        [pltpu.SMEM((N,), jnp.int32), vm(CELLS, H, dtype=BF16), vm(1, H), vm(1, H),
         vm(H, 5 * H, dtype=BF16), vm(*both_shape), dma((5,))],
        400_000_000, hbm_in=range(5),
    )
    recv = exchange(send, BOTH)
    dproj, normal, scale, spread = call(
        gate_kernel,
        [normed, w_in, cot2, pair2, line(out_gain)],
        [((CELLS, H), BF16), ((CELLS, H), F32), ((CELLS, H), F32), ((H, LANES), F32)],
        [],
        100_000_000,
    )
    send, left, right = call(
        mix_kernel,
        [recv],
        [(one_shape, BF16), ((N, 512), BF16), ((512, 512), BF16)],
        [vm(N, 512, dtype=BF16), vm(512, 512, dtype=BF16), vm(N, 512), vm(*one_shape),
         dma((2,))],
        400_000_000, hbm_out=(1, 2),
    )
    mixed = exchange(send, 3, 4)
    (send,) = call(
        d_mixed_kernel,
        [mixed, dproj, w_out, spread],
        [(one_shape, BF16)],
        [vm(*one_shape)],
        50_000_000,
    )
    recv = exchange(send, 3, 4)
    update, d_og, grads, pg, pvg = call(
        update_kernel,
        [mask, mixed, w_out, line(out_gain), line(out_bias), dproj, cot2, normed, w_in],
        [((CELLS, H), BF16), ((CELLS, H), BF16), ((2, H, H), BF16),
         ((A, H, LANES), BF16), ((A, H, LANES), BF16)],
        [vm(*one_shape), *gates, dma((2,))],
        600_000_000, smem_in=(0,), hbm_out=(3, 4),
    )
    send, pg_near, pvg_near = call(
        back_kernel,
        [recv, left, right, pg, pvg],
        [(both_shape, BF16), ((A, H, LANES), BF16), ((A, H, LANES), BF16)],
        [vm(N, 512, dtype=BF16), vm(512, 512, dtype=BF16), vm(*one_shape), vm(N, 512),
         vm(N, 512), vm(512, 512), dma((4,))],
        800_000_000, hbm_in=(1, 2, 3, 4),
    )
    recv = exchange(send, BOTH)
    (send,) = call(
        grad_kernel,
        [recv, pg_near, pvg_near, normed, grads],
        [(sum_shape, BF16)],
        [vm(*both_shape), vm(*sum_shape)],
        400_000_000,
    )
    parts = exchange(send, 3, 2)
    (pair_grad,) = call(
        pair_grad_kernel,
        [recv, pg, pvg, d_og, normal, scale, line(in_gain), w_in],
        [((CELLS, H), BF16)],
        [vm(*both_shape), *gates, dma((2,))],
        400_000_000, hbm_in=(1, 2),
    )
    (send,) = call(sum_kernel, [parts], [(sum_shape, BF16)], [], 1_000_000)
    sums = exchange(send, 3, 2)
    w_in_grad, w_out_grad = call(
        unpack_kernel,
        [sums],
        [((H, 5 * H), F32), ((H, H), F32)],
        [vm(*sum_shape)],
        1_000_000,
    )
    return (update.reshape(A, B, H), pair_grad.reshape(A, B, H), w_in_grad, w_out_grad)


def solution(mesh):
    placed = (P("row", "col", None), P(), P(), P(), P(), P(), P(), P(), P("row", "col", None))
    return jax.shard_map(
        on_device,
        mesh=mesh,
        in_specs=placed,
        out_specs=(P("row", "col", None), P("row", "col", None), P(), P()),
        check_vma=False,
    )
```

```python
import math

import jax
import jax.numpy as jnp
from jax import lax
from jax.experimental import pallas as pl
from jax.experimental.pallas import tpu as pltpu
from jax.sharding import PartitionSpec as P

F32 = jnp.float32
BF16 = jnp.bfloat16
EPS = 1e-05
AXES = ("row", "col")

A, B, HALF, LANES = 24, 48, 64, 128
NR, NC, ND = 16, 8, 128
CELLS = A * B
H = 128
N = NR * A
BOTH, ONE, SUMS = 18, 12, 6

NT = ((1,), (1,))
TN = ((0,), (0,))
NN = ((1,), (0,))
VMEM_SPEC = pl.BlockSpec(memory_space=pltpu.VMEM)
HBM_SPEC = pl.BlockSpec(memory_space=pltpu.HBM)


def dot(x, y, contract):
    return lax.dot_general(x, y, (contract, ((), ())), preferred_element_type=F32)


def roll(x, shift):
    return pltpu.roll(x, shift % LANES, x.ndim - 1)


def lane_of(shape):
    return lax.broadcasted_iota(jnp.int32, shape, len(shape) - 1)


def two_sided(x):
    none = jnp.zeros_like(x)
    rest = jnp.zeros((LANES - 2 * B, 2 * x.shape[1]), x.dtype)
    return jnp.concatenate(
        [jnp.concatenate([x, none], 1), jnp.concatenate([none, x], 1), rest], 0
    )


def row_cells(ref, q):
    none = jnp.zeros((HALF - B, H), BF16)
    return jnp.concatenate(
        [ref[q * B : (q + 1) * B, :], none, ref[(q + ONE) * B : (q + ONE + 1) * B, :], none], 0
    )


def column(row):
    at = lax.broadcasted_iota(jnp.int32, (H, LANES), 0)
    return jnp.sum(jnp.where(at == lane_of((H, LANES)), row, 0.0), 1, keepdims=True)


def stacked_weights(w_ref):
    part = [w_ref[:, p * H : (p + 1) * H].astype(F32).T.astype(BF16) for p in range(4)]
    return jnp.concatenate(
        [jnp.concatenate([part[0], part[2]], 1), jnp.concatenate([part[1], part[3]], 1)], 0
    )


def column_mask(mask_s):
    start = lax.axis_index("col") * B
    lane = lane_of((8, LANES))
    place = jnp.where(lane < B, lane, lane - B)
    out = jnp.zeros((8, LANES), F32)
    for b in range(B):
        out = jnp.where(place == b, mask_s[start + b].astype(F32), out)
    return out[0:1, :]


def gate_parts(weights, normed, pair_at, col_mask, mask_s):
    cells = jnp.concatenate([two_sided(normed[:B]), two_sided(normed[B:])], 0)
    pre = dot(weights, cells, NT)
    start = lax.axis_index("row") * A
    for k in range(2):
        value = pre[:H, k * LANES : (k + 1) * LANES]
        gate = jax.nn.sigmoid(pre[H:, k * LANES : (k + 1) * LANES])
        seen = col_mask * mask_s[start + 2 * pair_at + k].astype(F32)
        yield value, gate, gate * seen


def pack_both(block, third, a):
    shift = LANES - 32 if a < 8 else HALF
    return jnp.where(lane_of(block.shape) < 2 * B, block, roll(third, shift))


def pack_tail(third, n):
    lane = lane_of((H, LANES))
    out = roll(third[4 * n], -HALF)
    for m in range(1, 4):
        out = jnp.where(lane >= 32 * m, roll(third[4 * n + m], 32 * m - HALF), out)
    return out


def unpack_third(block, s):
    first, second, last = block(s), block(8 + s), block(16 + s // 4)
    lane = lane_of(first.shape)
    return jnp.where(
        lane < 32, roll(first, 32),
        jnp.where(lane < HALF, roll(second, HALF), roll(last, HALF - 32 * (s % 4))),
    )


def norm_rows(x):
    center = x - jnp.mean(x, 1, keepdims=True)
    scale = lax.rsqrt(jnp.mean(center * center, 1, keepdims=True) + EPS)
    return center * scale, scale


def norm_cells(x):
    center = x - jnp.mean(x, 0, keepdims=True)
    scale = lax.rsqrt(jnp.mean(center * center, 0, keepdims=True) + EPS)
    return center * scale, scale


def project_kernel(mask_h, pair_h, gain_h, bias_h, w_h, send_ref, normed_ref,
                   mask_s, pair_v, gain_v, bias_v, w_v, third, scratch, sems):
    copies = [
        pltpu.make_async_copy(src, dst, sems.at[n])
        for n, (src, dst) in enumerate(
            [(w_h, w_v), (pair_h, pair_v), (mask_h, mask_s), (gain_h, gain_v), (bias_h, bias_v)]
        )
    ]
    for copy in copies:
        copy.start()
    for copy in copies:
        copy.wait()
    weights = stacked_weights(w_v)
    col_mask = column_mask(mask_s)
    gain, bias = gain_v[...], bias_v[...]
    for pair_at in (8, 9, 10, 11, 0, 1, 2, 3, 4, 5, 6, 7):
        rows = pl.ds(pair_at * 2 * B, 2 * B)
        normal, _ = norm_rows(pair_v[rows, :].astype(F32))
        normed = (normal * gain + bias).astype(BF16)
        normed_ref[rows, :] = normed
        for k, (value, _, pg) in enumerate(gate_parts(weights, normed, pair_at, col_mask, mask_s)):
            a = pair_at * 2 + k
            if a >= 16:
                third[a - 16] = pg * value
            else:
                scratch[pl.ds(a, H, stride=BOTH), :] = pack_both(pg * value, third[a % 8], a)
        if pair_at == 11:
            for n in range(2):
                scratch[pl.ds(16 + n, H, stride=BOTH), :] = pack_tail(third, n)
    send_ref[...] = scratch[...].astype(BF16)


def gate_kernel(normed_ref, w_ref, cot_ref, pair_ref, gain_ref,
                dproj_ref, normal_ref, scale_ref, spread_ref):
    spread_ref[...] = jnp.broadcast_to(column(gain_ref[...]), (H, LANES))
    sig = jax.nn.sigmoid(dot(normed_ref[...], w_ref[:, 4 * H :], NN))
    dproj_ref[...] = (cot_ref[...].astype(F32) * sig).astype(BF16)
    normal, scale = norm_rows(pair_ref[...].astype(F32))
    normal_ref[...] = normal
    scale_ref[...] = jnp.broadcast_to(scale, (CELLS, H))


def pick(lane, *parts):
    out = parts[-1]
    for n in range(len(parts) - 3, -1, -2):
        out = jnp.where(lane < parts[n + 1], parts[n], out)
    return out


def by_row(x, shift, step):
    at = lax.broadcasted_iota(jnp.int32, (8, LANES), 0) & 3
    out = roll(x, shift)
    for m in range(1, 4):
        out = jnp.where(at == m, roll(x, shift + step * m), out)
    return out


def two_rows(scratch, start):
    first, second = (
        jnp.broadcast_to(scratch[pl.ds(start + n, 1), :], (8, LANES)) for n in range(2)
    )
    return jnp.where(lax.broadcasted_iota(jnp.int32, (8, LANES), 0) < 4, first, second)


def mix_kernel(recv_ref, send_ref, left_h, right_h, left_ref, right_ref, scratch, mixed, out, sems):
    scratch[...] = recv_ref[...].astype(F32)
    right_ref[...] = jnp.zeros_like(right_ref)
    lane, wide = lane_of((8, LANES)), lane_of((16, LANES))
    for r2 in range(NR // 2):
        for p in range(NC // 2):
            lefts, rights = [], []
            for r in (2 * r2, 2 * r2 + 1):
                start = (r * NC + 2 * p) * BOTH
                x, y = scratch[pl.ds(start, 16), :], scratch[pl.ds(start + BOTH, 16), :]
                x_tail, y_tail = two_rows(scratch, start + 16), two_rows(scratch, start + BOTH + 16)
                lefts += [
                    jnp.where(wide < HALF, x, roll(y, HALF)),
                    pick(lane, roll(x[:8], 32), 32, roll(x[8:], HALF), HALF, roll(y[:8], 96), 96, y[8:]),
                ]
                rights += [
                    pick(wide, roll(x, -B), B, 0.0, HALF, roll(y, HALF - B), HALF + B, 0.0),
                    pick(lane, roll(x[8:], 16), 16, by_row(x_tail, 16, -32), B, 0.0, HALF,
                         roll(y[8:], 80), 80, by_row(y_tail, 80, -32), HALF + B, 0.0),
                ]
            lanes = slice(p * LANES, (p + 1) * LANES)
            left_ref[r2 * B : (r2 + 1) * B, lanes] = jnp.concatenate(lefts, 0).astype(BF16)
            right_ref[r2 * HALF : r2 * HALF + B, lanes] = jnp.concatenate(rights, 0).astype(BF16)
    copies = [pltpu.make_async_copy(left_ref, left_h, sems.at[0]),
              pltpu.make_async_copy(right_ref, right_h, sems.at[1])]
    for copy in copies:
        copy.start()
    mixed[...] = dot(left_ref[...], right_ref[...], NT)
    low = lane_of((ONE, LANES)) < HALF
    for r in range(NR):
        for p in range(NC // 2):
            lanes = slice(p * LANES, (p + 1) * LANES)
            x = mixed[pl.ds(r * A, ONE), lanes]
            y = mixed[pl.ds(r * A + ONE, ONE), lanes]
            start = (r * NC + 2 * p) * ONE
            out[pl.ds(start, ONE), :] = jnp.where(low, x, roll(y, HALF))
            out[pl.ds(start + ONE, ONE), :] = jnp.where(low, roll(x, HALF), y)
    send_ref[...] = out[...].astype(BF16)
    for copy in copies:
        copy.wait()


def d_mixed_kernel(recv_ref, dproj_ref, w_out_ref, spread_ref, send_ref, scratch):
    scratch[...] = recv_ref[...].astype(F32)
    gain = spread_ref[...]
    w_out = w_out_ref[...]
    for q in range(ONE):
        wt = dot(w_out, row_cells(dproj_ref, q), NT) * gain
        normal, scale = norm_cells(scratch[pl.ds(q, H, stride=ONE), :])
        scratch[pl.ds(q, H, stride=ONE), :] = scale * (
            wt - jnp.mean(wt, 0, keepdims=True) - normal * jnp.mean(wt * normal, 0, keepdims=True)
        )
    send_ref[...] = scratch[...].astype(BF16)


def update_kernel(mask_s, recv_ref, w_out_ref, gain_ref, bias_ref, dproj_ref, cot_ref,
                  normed_ref, w_ref, update_ref, d_og_ref, grads_ref, pg_h, pvg_h,
                  scratch, pg_v, pvg_v, sems):
    weights = stacked_weights(w_ref)
    col_mask = column_mask(mask_s)
    for pair_at in range(A // 2):
        normed = normed_ref[pl.ds(pair_at * 2 * B, 2 * B), :]
        for k, (value, gate, pg) in enumerate(gate_parts(weights, normed, pair_at, col_mask, mask_s)):
            pg_v[2 * pair_at + k] = pg.astype(BF16)
            pvg_v[2 * pair_at + k] = (pg * value * (1.0 - gate)).astype(BF16)
    copies = [pltpu.make_async_copy(pg_v, pg_h, sems.at[0]),
              pltpu.make_async_copy(pvg_v, pvg_h, sems.at[1])]
    for copy in copies:
        copy.start()
    scratch[...] = recv_ref[...].astype(F32)
    gain, bias = column(gain_ref[...]), column(bias_ref[...])
    w_out, w_og = w_out_ref[...], w_ref[:, 4 * H :]
    grad = jnp.zeros((H, H), F32)
    for q in range(ONE):
        normal, _ = norm_cells(scratch[pl.ds(q, H, stride=ONE), :])
        out_normed = (normal * gain + bias).astype(BF16)
        projected = dot(out_normed, w_out, TN)
        grad = grad + dot(out_normed, row_cells(dproj_ref, q), NN)
        for k in range(2):
            rows = pl.ds((q + ONE * k) * B, B)
            sig = jax.nn.sigmoid(dot(normed_ref[rows, :], w_og, NN))
            proj = projected[k * HALF : k * HALF + B]
            update_ref[rows, :] = (sig * proj).astype(BF16)
            d_og_ref[rows, :] = (
                cot_ref[rows, :].astype(F32) * proj * sig * (1.0 - sig)
            ).astype(BF16)
    grads_ref[0] = dot(d_og_ref[...], normed_ref[...], TN).astype(BF16)
    grads_ref[1] = grad.astype(BF16)
    for copy in copies:
        copy.wait()


def back_kernel(recv_ref, left_h, right_h, pg_h, pvg_h, send_ref, pg_ref, pvg_ref,
                left_ref, right_ref, scratch, d_tile, d_left, d_right, out, tails, sems):
    copies = [
        pltpu.make_async_copy(src, dst, sems.at[n])
        for n, (src, dst) in enumerate(
            [(right_h, right_ref), (left_h, left_ref), (pg_h, pg_ref), (pvg_h, pvg_ref)]
        )
    ]
    for copy in copies:
        copy.start()
    scratch[...] = recv_ref[...].astype(F32)
    low = lane_of((ONE, LANES)) < HALF
    for r in range(NR):
        for p in range(NC // 2):
            lanes = slice(p * LANES, (p + 1) * LANES)
            start = (r * NC + 2 * p) * ONE
            x = scratch[pl.ds(start, ONE), :]
            y = scratch[pl.ds(start + ONE, ONE), :]
            d_tile[pl.ds(r * A, ONE), lanes] = jnp.where(low, x, roll(y, HALF))
            d_tile[pl.ds(r * A + ONE, ONE), lanes] = jnp.where(low, roll(x, HALF), y)
    d = d_tile[...].astype(BF16)
    copies[0].wait()
    copies[1].wait()
    d_left[...] = dot(d, right_ref[...], NN)
    d_right[...] = dot(d, left_ref[...], TN)
    lane = lane_of((8, LANES))
    mine = (lane >> 5) == (lax.broadcasted_iota(jnp.int32, (8, LANES), 0) & 3)
    for r in range(NR):
        for p in range(NC // 2):
            lanes = slice(p * LANES, (p + 1) * LANES)
            at = (r // 2) * HALF + (r % 2) * A
            x0, x1, x2 = (d_left[r * A + 8 * t : r * A + 8 * t + 8, lanes] for t in range(3))
            y0, y1, y2 = (d_right[at + 8 * t : at + 8 * t + 8, lanes] for t in range(3))
            first = (r * NC + 2 * p) * BOTH
            second = first + BOTH
            out[pl.ds(first, 8), :] = pick(lane, x0, B, roll(y0, B), 2 * B, roll(x2, 96))
            out[pl.ds(first + 8, 8), :] = pick(
                lane, x1, B, roll(y1, B), 2 * B, roll(x2, HALF), 112, roll(y2, 112)
            )
            out[pl.ds(second, 8), :] = pick(lane, roll(x0, HALF), B, roll(y0, -16), 2 * B, roll(x2, 32))
            out[pl.ds(second + 8, 8), :] = pick(
                lane, roll(x1, HALF), B, roll(y1, -16), 2 * B, x2, 112, roll(y2, B)
            )
            for start, shift in ((first, -16), (second, -80)):
                row = start // BOTH * 8
                tails[row : row + 8, :] = jnp.where(mine, by_row(y2, shift, 32), 0.0)
    quarters = [tails[pl.ds(n, 2 * ND, stride=4), :] for n in range(4)]
    tails[: 2 * ND, :] = quarters[0] + quarters[1] + quarters[2] + quarters[3]
    for n in range(2):
        out[pl.ds(16 + n, ND, stride=BOTH), :] = tails[pl.ds(n, ND, stride=2), :]
    send_ref[...] = out[...].astype(BF16)
    copies[2].wait()
    copies[3].wait()


def gated(scratch, a, pg_v, pvg_v):
    block = lambda p: scratch[pl.ds(p, H, stride=BOTH), :]
    d = block(a) if a < 16 else unpack_third(block, a - 16)
    return jnp.concatenate([d * pg_v[a].astype(F32), d * pvg_v[a].astype(F32)], 0).astype(BF16)


def grad_kernel(recv_ref, pg_v, pvg_v, normed_ref, grads_ref, send_ref, scratch, packed):
    scratch[...] = recv_ref[...].astype(F32)
    for g in range(2):
        packed[pl.ds(4 + g, H, stride=SUMS), :] = grads_ref[g].astype(F32)
    total = jnp.zeros((2 * H, 2 * H), F32)
    for pair_at in range(A // 2):
        a = 2 * pair_at
        sides = [gated(scratch, a + k, pg_v, pvg_v) for k in range(2)]
        cells = [two_sided(normed_ref[(a + k) * B : (a + k + 1) * B, :]) for k in range(2)]
        total = total + dot(jnp.concatenate(sides, 1), jnp.concatenate(cells, 0), NN)
    for g, block in enumerate([total[:H, :H], total[H:, :H], total[:H, H:], total[H:, H:]]):
        packed[pl.ds(g, H, stride=SUMS), :] = block
    send_ref[...] = packed[...].astype(BF16)


def pair_grad_kernel(recv_ref, pg_h, pvg_h, d_og_ref, normal_ref, scale_ref, gain_ref, w_ref,
                     out_ref, scratch, pg_v, pvg_v, sems):
    copies = [pltpu.make_async_copy(pg_h, pg_v, sems.at[0]),
              pltpu.make_async_copy(pvg_h, pvg_v, sems.at[1])]
    for copy in copies:
        copy.start()
    scratch[...] = recv_ref[...].astype(F32)
    weights = stacked_weights(w_ref)
    w_og = w_ref[:, 4 * H :]
    gain = gain_ref[...]
    for copy in copies:
        copy.wait()
    for a in range(A):
        rows = pl.ds(a * B, B)
        both = dot(gated(scratch, a, pg_v, pvg_v), weights, TN)
        d = both[:B, :H] + both[B : 2 * B, H:] + dot(d_og_ref[rows, :], w_og, NT)
        normal = normal_ref[rows, :]
        weighted = d * gain
        out_ref[rows, :] = (
            scale_ref[rows, :] * (weighted - jnp.mean(weighted, 1, keepdims=True)
                                  - normal * jnp.mean(weighted * normal, 1, keepdims=True))
        ).astype(BF16)


def sum_kernel(recv_ref, send_ref):
    parts = jnp.sum(recv_ref[...].astype(F32).reshape(16, 8 * SUMS, LANES), 0)
    total = parts[:SUMS]
    for k in range(1, 8):
        total = total + parts[k * SUMS : (k + 1) * SUMS]
    many = jnp.concatenate([total] * 8, 0).astype(BF16)
    for s in range(16):
        send_ref[s * 8 * SUMS : (s + 1) * 8 * SUMS, :] = many


def unpack_kernel(recv_ref, w_in_ref, w_out_ref, scratch):
    scratch[...] = recv_ref[...].astype(F32)
    for g in range(5):
        w_in_ref[:, g * H : (g + 1) * H] = scratch[pl.ds(g, H, stride=SUMS), :].T
    w_out_ref[...] = scratch[pl.ds(5, H, stride=SUMS), :]


def call(kernel, args, outs, scratch, flops, hbm_in=(), smem_in=(), hbm_out=()):
    shapes = [
        pltpu.HBM(s, d) if n in hbm_out else jax.ShapeDtypeStruct(s, d)
        for n, (s, d) in enumerate(outs)
    ]
    args = [
        pltpu.with_memory_space_constraint(v, pltpu.HBM) if n in hbm_in else v
        for n, v in enumerate(args)
    ]
    specs = [
        HBM_SPEC if n in hbm_in else pl.BlockSpec(memory_space=pltpu.SMEM) if n in smem_in else VMEM_SPEC
        for n in range(len(args))
    ]
    moved = 2 * (sum(v.size for v in args) + sum(math.prod(s) for s, _ in outs))
    return pl.pallas_call(
        kernel,
        out_shape=shapes,
        in_specs=specs,
        out_specs=[HBM_SPEC if n in hbm_out else VMEM_SPEC for n in range(len(shapes))],
        scratch_shapes=scratch,
        cost_estimate=pl.CostEstimate(flops=flops, bytes_accessed=moved, transcendentals=0),
        compiler_params=pltpu.CompilerParams(vmem_limit_bytes=40 * 2**20),
    )(*args)


def vm(*shape, dtype=F32):
    return pltpu.VMEM(shape, dtype)


def exchange(x, *tile):
    moved = lax.all_to_all(x.reshape(ND, *tile, LANES), AXES, 0, 0, tiled=True)
    return moved.reshape(x.shape)


def on_device(pair, mask, in_gain, in_bias, w_in, out_gain, out_bias, w_out, cotangent):
    pair2 = pair.reshape(CELLS, H)
    cot2 = cotangent.reshape(CELLS, H)
    line = lambda v: v.reshape(1, -1)
    dma = pltpu.SemaphoreType.DMA
    both_shape, one_shape, sum_shape = ((ND * n, LANES) for n in (BOTH, ONE, SUMS))
    gates = [vm(A, H, LANES, dtype=BF16)] * 2

    send, normed = call(
        project_kernel,
        [mask, pair2, line(in_gain), line(in_bias), w_in],
        [(both_shape, BF16), ((CELLS, H), BF16)],
        [pltpu.SMEM((N,), jnp.int32), vm(CELLS, H, dtype=BF16), vm(1, H), vm(1, H),
         vm(H, 5 * H, dtype=BF16), vm(8, H, LANES), vm(*both_shape), dma((5,))],
        400_000_000, hbm_in=range(5),
    )
    recv = exchange(send, 9, 2)
    dproj, normal, scale, spread = call(
        gate_kernel,
        [normed, w_in, cot2, pair2, line(out_gain)],
        [((CELLS, H), BF16), ((CELLS, H), F32), ((CELLS, H), F32), ((H, LANES), F32)],
        [],
        100_000_000,
    )
    send, left, right = call(
        mix_kernel,
        [recv],
        [(one_shape, BF16), ((N, 512), BF16), ((512, 512), BF16)],
        [vm(N, 512, dtype=BF16), vm(512, 512, dtype=BF16), vm(*both_shape), vm(N, 512),
         vm(*one_shape), dma((2,))],
        400_000_000, hbm_out=(1, 2),
    )
    mixed = exchange(send, 3, 4)
    (send,) = call(
        d_mixed_kernel,
        [mixed, dproj, w_out, spread],
        [(one_shape, BF16)],
        [vm(*one_shape)],
        50_000_000,
    )
    recv = exchange(send, 3, 4)
    update, d_og, grads, pg, pvg = call(
        update_kernel,
        [mask, mixed, w_out, line(out_gain), line(out_bias), dproj, cot2, normed, w_in],
        [((CELLS, H), BF16), ((CELLS, H), BF16), ((2, H, H), BF16),
         ((A, H, LANES), BF16), ((A, H, LANES), BF16)],
        [vm(*one_shape), *gates, dma((2,))],
        600_000_000, smem_in=(0,), hbm_out=(3, 4),
    )
    send, pg_near, pvg_near = call(
        back_kernel,
        [recv, left, right, pg, pvg],
        [(both_shape, BF16), ((A, H, LANES), BF16), ((A, H, LANES), BF16)],
        [vm(N, 512, dtype=BF16), vm(512, 512, dtype=BF16), vm(*one_shape), vm(N, 512),
         vm(N, 512), vm(512, 512), vm(*both_shape), vm(8 * ND, LANES),
         dma((4,))],
        800_000_000, hbm_in=(1, 2, 3, 4),
    )
    recv = exchange(send, 9, 2)
    (send,) = call(
        grad_kernel,
        [recv, pg_near, pvg_near, normed, grads],
        [(sum_shape, BF16)],
        [vm(*both_shape), vm(*sum_shape)],
        400_000_000,
    )
    parts = exchange(send, 3, 2)
    (pair_grad,) = call(
        pair_grad_kernel,
        [recv, pg, pvg, d_og, normal, scale, line(in_gain), w_in],
        [((CELLS, H), BF16)],
        [vm(*both_shape), *gates, dma((2,))],
        400_000_000, hbm_in=(1, 2),
    )
    (send,) = call(sum_kernel, [parts], [(sum_shape, BF16)], [], 1_000_000)
    sums = exchange(send, 3, 2)
    w_in_grad, w_out_grad = call(
        unpack_kernel,
        [sums],
        [((H, 5 * H), F32), ((H, H), F32)],
        [vm(*sum_shape)],
        1_000_000,
    )
    return (update.reshape(A, B, H), pair_grad.reshape(A, B, H), w_in_grad, w_out_grad)


def solution(mesh):
    placed = (P("row", "col", None), P(), P(), P(), P(), P(), P(), P(), P("row", "col", None))
    return jax.shard_map(
        on_device,
        mesh=mesh,
        in_specs=placed,
        out_specs=(P("row", "col", None), P("row", "col", None), P(), P()),
        check_vma=False,
    )
```

```python
import math

import jax
import jax.numpy as jnp
from jax import lax
from jax.experimental import pallas as pl
from jax.experimental.pallas import tpu as pltpu
from jax.sharding import PartitionSpec as P

F32 = jnp.float32
BF16 = jnp.bfloat16
EPS = 1e-05
AXES = ("row", "col")

A, B, HALF, LANES = 24, 48, 64, 128
NR, NC, ND = 16, 8, 128
CELLS = A * B
H = 128
N = NR * A
BOTH, ONE, SUMS = 18, 10, 6

NT = ((1,), (1,))
TN = ((0,), (0,))
NN = ((1,), (0,))
VMEM_SPEC = pl.BlockSpec(memory_space=pltpu.VMEM)
HBM_SPEC = pl.BlockSpec(memory_space=pltpu.HBM)


def dot(x, y, contract):
    return lax.dot_general(x, y, (contract, ((), ())), preferred_element_type=F32)


def roll(x, shift):
    return pltpu.roll(x, shift % LANES, x.ndim - 1)


def lane_of(shape):
    return lax.broadcasted_iota(jnp.int32, shape, len(shape) - 1)


def two_sided(x):
    none = jnp.zeros_like(x)
    rest = jnp.zeros((LANES - 2 * B, 2 * x.shape[1]), x.dtype)
    return jnp.concatenate(
        [jnp.concatenate([x, none], 1), jnp.concatenate([none, x], 1), rest], 0
    )


def pieces(q):
    if q == 8:
        return [((16 + n) * B + 32, 16 * n, 16) for n in range(8)]
    return [(q * B, 0, B), ((8 + q) * B, B, B), ((16 + q) * B, 2 * B, 32)]


def row_cells(ref, q):
    return jnp.concatenate([ref[at : at + size, :] for at, _, size in pieces(q)], 0)


def column(row):
    at = lax.broadcasted_iota(jnp.int32, (H, LANES), 0)
    return jnp.sum(jnp.where(at == lane_of((H, LANES)), row, 0.0), 1, keepdims=True)


def stacked_weights(w_ref):
    part = [w_ref[:, p * H : (p + 1) * H].astype(F32).T.astype(BF16) for p in range(4)]
    return jnp.concatenate(
        [jnp.concatenate([part[0], part[2]], 1), jnp.concatenate([part[1], part[3]], 1)], 0
    )


def column_mask(mask_s):
    start = lax.axis_index("col") * B
    lane = lane_of((8, LANES))
    place = jnp.where(lane < B, lane, lane - B)
    out = jnp.zeros((8, LANES), F32)
    for b in range(B):
        out = jnp.where(place == b, mask_s[start + b].astype(F32), out)
    return out[0:1, :]


def gate_parts(weights, normed, pair_at, col_mask, mask_s):
    cells = jnp.concatenate([two_sided(normed[:B]), two_sided(normed[B:])], 0)
    pre = dot(weights, cells, NT)
    start = lax.axis_index("row") * A
    for k in range(2):
        value = pre[:H, k * LANES : (k + 1) * LANES]
        gate = jax.nn.sigmoid(pre[H:, k * LANES : (k + 1) * LANES])
        seen = col_mask * mask_s[start + 2 * pair_at + k].astype(F32)
        yield value, gate, gate * seen


def pack_both(block, third, a):
    shift = LANES - 32 if a < 8 else HALF
    return jnp.where(lane_of(block.shape) < 2 * B, block, roll(third, shift))


def pack_tail(third, n):
    lane = lane_of((H, LANES))
    out = roll(third[4 * n], -HALF)
    for m in range(1, 4):
        out = jnp.where(lane >= 32 * m, roll(third[4 * n + m], 32 * m - HALF), out)
    return out


def unpack_third(block, s):
    first, second, last = block(s), block(8 + s), block(16 + s // 4)
    lane = lane_of(first.shape)
    return jnp.where(
        lane < 32, roll(first, 32),
        jnp.where(lane < HALF, roll(second, HALF), roll(last, HALF - 32 * (s % 4))),
    )


def norm_rows(x):
    center = x - jnp.mean(x, 1, keepdims=True)
    scale = lax.rsqrt(jnp.mean(center * center, 1, keepdims=True) + EPS)
    return center * scale, scale


def norm_cells(x):
    center = x - jnp.mean(x, 0, keepdims=True)
    scale = lax.rsqrt(jnp.mean(center * center, 0, keepdims=True) + EPS)
    return center * scale, scale


def project_kernel(mask_h, pair_h, gain_h, bias_h, w_h, send_ref, normed_ref,
                   mask_s, pair_v, gain_v, bias_v, w_v, third, scratch, sems):
    copies = [
        pltpu.make_async_copy(src, dst, sems.at[n])
        for n, (src, dst) in enumerate(
            [(mask_h, mask_s), (gain_h, gain_v), (bias_h, bias_v), (w_h, w_v)]
        )
    ]
    parts = [
        pltpu.make_async_copy(pair_h.at[rows], pair_v.at[rows], sems.at[4 + n])
        for n, rows in enumerate(pl.ds(start * CELLS // 3, CELLS // 3) for start in (2, 0, 1))
    ]
    for copy in copies[3:] + parts + copies[:3]:
        copy.start()
    copies[3].wait()
    weights = stacked_weights(w_v)
    for copy in copies[:3]:
        copy.wait()
    col_mask = column_mask(mask_s)
    gain, bias = gain_v[...], bias_v[...]
    for n, pair_at in enumerate((8, 9, 10, 11, 0, 1, 2, 3, 4, 5, 6, 7)):
        if n % 4 == 0:
            parts[n // 4].wait()
        rows = pl.ds(pair_at * 2 * B, 2 * B)
        normal, _ = norm_rows(pair_v[rows, :].astype(F32))
        normed = (normal * gain + bias).astype(BF16)
        normed_ref[rows, :] = normed
        for k, (value, _, pg) in enumerate(gate_parts(weights, normed, pair_at, col_mask, mask_s)):
            a = pair_at * 2 + k
            if a >= 16:
                third[a - 16] = pg * value
            else:
                scratch[pl.ds(a, H, stride=BOTH), :] = pack_both(pg * value, third[a % 8], a)
        if pair_at == 11:
            for n in range(2):
                scratch[pl.ds(16 + n, H, stride=BOTH), :] = pack_tail(third, n)
    send_ref[...] = scratch[...].astype(BF16)


def gate_kernel(normed_ref, w_ref, cot_ref, pair_ref, gain_ref,
                dproj_ref, normal_ref, scale_ref, spread_ref):
    spread_ref[...] = jnp.broadcast_to(column(gain_ref[...]), (H, LANES))
    sig = jax.nn.sigmoid(dot(normed_ref[...], w_ref[:, 4 * H :], NN))
    dproj_ref[...] = (cot_ref[...].astype(F32) * sig).astype(BF16)
    normal, scale = norm_rows(pair_ref[...].astype(F32))
    normal_ref[...] = normal
    scale_ref[...] = jnp.broadcast_to(scale, (CELLS, H))


def pick(lane, *parts):
    out = parts[-1]
    for n in range(len(parts) - 3, -1, -2):
        out = jnp.where(lane < parts[n + 1], parts[n], out)
    return out


def mix_kernel(recv_ref, send_ref, left_h, right_h, left_ref, right_ref, scratch, third, mixed,
               out, sems):
    scratch[...] = recv_ref[...].astype(F32)
    lane, wide = lane_of((8, LANES)), lane_of((NR, LANES))
    for p in range(NC // 2):
        for n in range(8):
            x, y = (
                scratch[pl.ds(c * BOTH + 16 + n // 4, NR, stride=NC * BOTH), :]
                for c in (2 * p, 2 * p + 1)
            )
            shift = -32 * (n % 4)
            third[pl.ds(p * LANES + n, NR, stride=8), :] = jnp.where(
                wide < HALF, roll(x, shift + 16), roll(y, shift + 80)
            )
    for r2 in range(NR // 2):
        right_ref[r2 * HALF + B : (r2 + 1) * HALF, :] = jnp.zeros((HALF - B, 512), BF16)
        for p in range(NC // 2):
            lefts, rights = [], []
            for r in (2 * r2, 2 * r2 + 1):
                start = (r * NC + 2 * p) * BOTH
                x, y = scratch[pl.ds(start, 16), :], scratch[pl.ds(start + BOTH, 16), :]
                tail = third[p * LANES + r * 8 : p * LANES + r * 8 + 8, :]
                lefts += [
                    jnp.where(wide < HALF, x, roll(y, HALF)),
                    pick(lane, roll(x[:8], 32), 32, roll(x[8:], HALF), HALF, roll(y[:8], 96), 96, y[8:]),
                ]
                rights += [
                    pick(wide, roll(x, -B), B, 0.0, HALF, roll(y, HALF - B), HALF + B, 0.0),
                    pick(lane, roll(x[8:], 16), 16, tail, B, 0.0, HALF,
                         roll(y[8:], 80), 80, tail, HALF + B, 0.0),
                ]
            lanes = slice(p * LANES, (p + 1) * LANES)
            left_ref[r2 * B : (r2 + 1) * B, lanes] = jnp.concatenate(lefts, 0).astype(BF16)
            right_ref[r2 * HALF : r2 * HALF + B, lanes] = jnp.concatenate(rights, 0).astype(BF16)
    copies = [pltpu.make_async_copy(left_ref, left_h, sems.at[0]),
              pltpu.make_async_copy(right_ref, right_h, sems.at[1])]
    for copy in copies:
        copy.start()
    product = dot(left_ref[...], right_ref[...], NT)
    for p in range(NC // 2):
        mixed[p * N : (p + 1) * N, :] = product[:, p * LANES : (p + 1) * LANES]
    for r in range(NR):
        for p in range(NC // 2):
            t0, t1, t2 = (
                mixed[p * N + r * A + 8 * t : p * N + r * A + 8 * t + 8, :] for t in range(3)
            )
            start = (r * NC + 2 * p) * ONE
            out[pl.ds(start, 8), :] = pick(lane, t0, B, roll(t1, B), 2 * B, roll(t2, 96))
            out[pl.ds(start + ONE, 8), :] = pick(
                lane, roll(t0, HALF), B, roll(t1, -16), 2 * B, roll(t2, 32)
            )
    out[pl.ds(9, ND, stride=ONE), :] = jnp.zeros((ND, LANES), F32)
    group = wide >> 4
    for p in range(NC // 2):
        first = second = jnp.zeros((NR, LANES), F32)
        for n in range(8):
            t2 = mixed[pl.ds(p * N + 16 + n, NR, stride=A), :]
            first = jnp.where(group == n, roll(t2, 16 * n - 32), first)
            second = jnp.where(group == n, roll(t2, 16 * n - 96), second)
        out[pl.ds(2 * p * ONE + 8, NR, stride=NC * ONE), :] = first
        out[pl.ds((2 * p + 1) * ONE + 8, NR, stride=NC * ONE), :] = second
    send_ref[...] = out[...].astype(BF16)
    for copy in copies:
        copy.wait()


def d_mixed_kernel(recv_ref, dproj_ref, w_out_ref, spread_ref, send_ref, scratch):
    scratch[...] = recv_ref[...].astype(F32)
    gain = spread_ref[...]
    w_out = w_out_ref[...]
    for q in range(9):
        wt = dot(w_out, row_cells(dproj_ref, q), NT) * gain
        normal, scale = norm_cells(scratch[pl.ds(q, H, stride=ONE), :])
        scratch[pl.ds(q, H, stride=ONE), :] = scale * (
            wt - jnp.mean(wt, 0, keepdims=True) - normal * jnp.mean(wt * normal, 0, keepdims=True)
        )
    send_ref[...] = scratch[...].astype(BF16)


def update_kernel(mask_s, recv_ref, w_out_ref, gain_ref, bias_ref, dproj_ref, cot_ref,
                  normed_ref, w_ref, update_ref, d_og_ref, grads_ref, pg_h, pvg_h,
                  scratch, pg_v, pvg_v, sems):
    weights = stacked_weights(w_ref)
    col_mask = column_mask(mask_s)
    for pair_at in range(A // 2):
        normed = normed_ref[pl.ds(pair_at * 2 * B, 2 * B), :]
        for k, (value, gate, pg) in enumerate(gate_parts(weights, normed, pair_at, col_mask, mask_s)):
            pg_v[2 * pair_at + k] = pg.astype(BF16)
            pvg_v[2 * pair_at + k] = (pg * value * (1.0 - gate)).astype(BF16)
    copies = [pltpu.make_async_copy(pg_v, pg_h, sems.at[0]),
              pltpu.make_async_copy(pvg_v, pvg_h, sems.at[1])]
    for copy in copies:
        copy.start()
    scratch[...] = recv_ref[...].astype(F32)
    gain, bias = column(gain_ref[...]), column(bias_ref[...])
    w_out, w_og = w_out_ref[...], w_ref[:, 4 * H :]
    grad = jnp.zeros((H, H), F32)
    for q in range(9):
        normal, _ = norm_cells(scratch[pl.ds(q, H, stride=ONE), :])
        out_normed = (normal * gain + bias).astype(BF16)
        projected = dot(out_normed, w_out, TN)
        grad = grad + dot(out_normed, row_cells(dproj_ref, q), NN)
        gates = jax.nn.sigmoid(dot(row_cells(normed_ref, q), w_og, NN))
        for at, lane, size in pieces(q):
            rows = pl.ds(at, size)
            sig, proj = gates[lane : lane + size], projected[lane : lane + size]
            update_ref[rows, :] = (sig * proj).astype(BF16)
            d_og_ref[rows, :] = (
                cot_ref[rows, :].astype(F32) * proj * sig * (1.0 - sig)
            ).astype(BF16)
    grads_ref[0] = dot(d_og_ref[...], normed_ref[...], TN).astype(BF16)
    grads_ref[1] = grad.astype(BF16)
    for copy in copies:
        copy.wait()


def back_kernel(recv_ref, left_h, right_h, pg_h, pvg_h, send_ref, pg_ref, pvg_ref,
                left_ref, right_ref, scratch, d_tile, d_left, d_right, out, sems):
    copies = [
        pltpu.make_async_copy(src, dst, sems.at[n])
        for n, (src, dst) in enumerate(
            [(right_h, right_ref), (left_h, left_ref), (pg_h, pg_ref), (pvg_h, pvg_ref)]
        )
    ]
    for copy in copies:
        copy.start()
    scratch[...] = recv_ref[...].astype(F32)
    lane, wide = lane_of((8, LANES)), lane_of((NR, LANES))
    for p in range(NC // 2):
        x, y = (
            scratch[pl.ds(c * ONE + 8, NR, stride=NC * ONE), :] for c in (2 * p, 2 * p + 1)
        )
        for n in range(8):
            d_tile[pl.ds(p * N + 16 + n, NR, stride=A), :] = jnp.where(
                wide < HALF, roll(x, 32 - 16 * n), roll(y, 96 - 16 * n)
            )
    for r in range(NR):
        for p in range(NC // 2):
            start = (r * NC + 2 * p) * ONE
            x, y = scratch[pl.ds(start, 8), :], scratch[pl.ds(start + ONE, 8), :]
            at = p * N + r * A
            tail = d_tile[at + 16 : at + 24, :]
            d_tile[at : at + 8, :] = jnp.where(lane < HALF, x, roll(y, HALF))
            d_tile[at + 8 : at + 16, :] = jnp.where(lane < HALF, roll(x, -B), roll(y, 16))
            d_tile[at + 16 : at + 24, :] = pick(
                lane, roll(x, 32), 32, tail, HALF, roll(y, 96), 96, tail
            )
    d = jnp.concatenate([d_tile[p * N : (p + 1) * N, :].astype(BF16) for p in range(4)], 1)
    copies[0].wait()
    copies[1].wait()
    d_left[...] = dot(d, right_ref[...], NN)
    product = dot(d, left_ref[...], TN)
    for p in range(NC // 2):
        d_right[p * 512 : (p + 1) * 512, :] = product[:, p * LANES : (p + 1) * LANES]
    for r in range(NR):
        for p in range(NC // 2):
            lanes = slice(p * LANES, (p + 1) * LANES)
            at = p * 512 + (r // 2) * HALF + (r % 2) * A
            x0, x1, x2 = (d_left[r * A + 8 * t : r * A + 8 * t + 8, lanes] for t in range(3))
            y0, y1, y2 = (d_right[at + 8 * t : at + 8 * t + 8, :] for t in range(3))
            start = (r * NC + 2 * p) * BOTH
            out[pl.ds(start, 8), :] = pick(lane, x0, B, roll(y0, B), 2 * B, roll(x2, 96))
            out[pl.ds(start + 8, 8), :] = pick(
                lane, x1, B, roll(y1, B), 2 * B, roll(x2, HALF), 112, roll(y2, 112)
            )
            start = start + BOTH
            out[pl.ds(start, 8), :] = pick(lane, roll(x0, HALF), B, roll(y0, -16), 2 * B, roll(x2, 32))
            out[pl.ds(start + 8, 8), :] = pick(
                lane, roll(x1, HALF), B, roll(y1, -16), 2 * B, x2, 112, roll(y2, B)
            )
    group = lane >> 5
    for p in range(NC // 2):
        for odd in range(2):
            for half in range(2):
                first = second = jnp.zeros((8, LANES), F32)
                for m in range(4):
                    at = p * 512 + odd * A + 16 + 4 * half + m
                    y2 = d_right[pl.ds(at, 8, stride=HALF), :]
                    first = jnp.where(group == m, roll(y2, 32 * m - 16), first)
                    second = jnp.where(group == m, roll(y2, 32 * m - 80), second)
                start = (odd * NC + 2 * p) * BOTH + 16 + half
                out[pl.ds(start, 8, stride=2 * NC * BOTH), :] = first
                out[pl.ds(start + BOTH, 8, stride=2 * NC * BOTH), :] = second
    send_ref[...] = out[...].astype(BF16)
    copies[2].wait()
    copies[3].wait()


def gated(scratch, a, pg_v, pvg_v):
    block = lambda p: scratch[pl.ds(p, H, stride=BOTH), :]
    d = block(a) if a < 16 else unpack_third(block, a - 16)
    return jnp.concatenate([d * pg_v[a].astype(F32), d * pvg_v[a].astype(F32)], 0).astype(BF16)


def grad_kernel(recv_ref, pg_v, pvg_v, normed_ref, grads_ref, send_ref, scratch, packed):
    scratch[...] = recv_ref[...].astype(F32)
    for g in range(2):
        packed[pl.ds(4 + g, H, stride=SUMS), :] = grads_ref[g].astype(F32)
    total = jnp.zeros((2 * H, 2 * H), F32)
    for pair_at in range(A // 2):
        a = 2 * pair_at
        sides = [gated(scratch, a + k, pg_v, pvg_v) for k in range(2)]
        cells = [two_sided(normed_ref[(a + k) * B : (a + k + 1) * B, :]) for k in range(2)]
        total = total + dot(jnp.concatenate(sides, 1), jnp.concatenate(cells, 0), NN)
    for g, block in enumerate([total[:H, :H], total[H:, :H], total[:H, H:], total[H:, H:]]):
        packed[pl.ds(g, H, stride=SUMS), :] = block
    send_ref[...] = packed[...].astype(BF16)


def pair_grad_kernel(recv_ref, pg_h, pvg_h, d_og_ref, normal_ref, scale_ref, gain_ref, w_ref,
                     out_ref, scratch, pg_v, pvg_v, sems):
    copies = [pltpu.make_async_copy(pg_h, pg_v, sems.at[0]),
              pltpu.make_async_copy(pvg_h, pvg_v, sems.at[1])]
    for copy in copies:
        copy.start()
    scratch[...] = recv_ref[...].astype(F32)
    weights = stacked_weights(w_ref)
    w_og = w_ref[:, 4 * H :]
    gain = gain_ref[...]
    for copy in copies:
        copy.wait()
    for a in range(A):
        rows = pl.ds(a * B, B)
        both = dot(gated(scratch, a, pg_v, pvg_v), weights, TN)
        d = both[:B, :H] + both[B : 2 * B, H:] + dot(d_og_ref[rows, :], w_og, NT)
        normal = normal_ref[rows, :]
        weighted = d * gain
        out_ref[rows, :] = (
            scale_ref[rows, :] * (weighted - jnp.mean(weighted, 1, keepdims=True)
                                  - normal * jnp.mean(weighted * normal, 1, keepdims=True))
        ).astype(BF16)


def sum_kernel(recv_ref, send_ref):
    parts = jnp.sum(recv_ref[...].astype(F32).reshape(16, 8 * SUMS, LANES), 0)
    total = parts[:SUMS]
    for k in range(1, 8):
        total = total + parts[k * SUMS : (k + 1) * SUMS]
    many = jnp.concatenate([total] * 8, 0).astype(BF16)
    for s in range(16):
        send_ref[s * 8 * SUMS : (s + 1) * 8 * SUMS, :] = many


def unpack_kernel(recv_ref, w_in_ref, w_out_ref, scratch):
    scratch[...] = recv_ref[...].astype(F32)
    for g in range(5):
        w_in_ref[:, g * H : (g + 1) * H] = scratch[pl.ds(g, H, stride=SUMS), :].T
    w_out_ref[...] = scratch[pl.ds(5, H, stride=SUMS), :]


def call(kernel, args, outs, scratch, flops, hbm_in=(), smem_in=(), hbm_out=()):
    shapes = [
        pltpu.HBM(s, d) if n in hbm_out else jax.ShapeDtypeStruct(s, d)
        for n, (s, d) in enumerate(outs)
    ]
    args = [
        pltpu.with_memory_space_constraint(v, pltpu.HBM) if n in hbm_in else v
        for n, v in enumerate(args)
    ]
    specs = [
        HBM_SPEC if n in hbm_in else pl.BlockSpec(memory_space=pltpu.SMEM) if n in smem_in else VMEM_SPEC
        for n in range(len(args))
    ]
    moved = 2 * (sum(v.size for v in args) + sum(math.prod(s) for s, _ in outs))
    return pl.pallas_call(
        kernel,
        out_shape=shapes,
        in_specs=specs,
        out_specs=[HBM_SPEC if n in hbm_out else VMEM_SPEC for n in range(len(shapes))],
        scratch_shapes=scratch,
        cost_estimate=pl.CostEstimate(flops=flops, bytes_accessed=moved, transcendentals=0),
        compiler_params=pltpu.CompilerParams(vmem_limit_bytes=40 * 2**20),
    )(*args)


def vm(*shape, dtype=F32):
    return pltpu.VMEM(shape, dtype)


def exchange(x, *tile):
    moved = lax.all_to_all(x.reshape(ND, *tile, LANES), AXES, 0, 0, tiled=True)
    return moved.reshape(x.shape)


def on_device(pair, mask, in_gain, in_bias, w_in, out_gain, out_bias, w_out, cotangent):
    pair2 = pair.reshape(CELLS, H)
    cot2 = cotangent.reshape(CELLS, H)
    line = lambda v: v.reshape(1, -1)
    dma = pltpu.SemaphoreType.DMA
    both_shape, one_shape, sum_shape = ((ND * n, LANES) for n in (BOTH, ONE, SUMS))
    gates = [vm(A, H, LANES, dtype=BF16)] * 2

    send, normed = call(
        project_kernel,
        [mask, pair2, line(in_gain), line(in_bias), w_in],
        [(both_shape, BF16), ((CELLS, H), BF16)],
        [pltpu.SMEM((N,), jnp.int32), vm(CELLS, H, dtype=BF16), vm(1, H), vm(1, H),
         vm(H, 5 * H, dtype=BF16), vm(8, H, LANES), vm(*both_shape), dma((7,))],
        400_000_000, hbm_in=range(5),
    )
    recv = exchange(send, 9, 2)
    dproj, normal, scale, spread = call(
        gate_kernel,
        [normed, w_in, cot2, pair2, line(out_gain)],
        [((CELLS, H), BF16), ((CELLS, H), F32), ((CELLS, H), F32), ((H, LANES), F32)],
        [],
        100_000_000,
    )
    send, left, right = call(
        mix_kernel,
        [recv],
        [(one_shape, BF16), ((N, 512), BF16), ((512, 512), BF16)],
        [vm(N, 512, dtype=BF16), vm(512, 512, dtype=BF16), vm(*both_shape), vm(512, LANES),
         vm(4 * N, LANES), vm(*one_shape), dma((2,))],
        400_000_000, hbm_out=(1, 2),
    )
    mixed = exchange(send, 5, 2)
    (send,) = call(
        d_mixed_kernel,
        [mixed, dproj, w_out, spread],
        [(one_shape, BF16)],
        [vm(*one_shape)],
        50_000_000,
    )
    recv = exchange(send, 5, 2)
    update, d_og, grads, pg, pvg = call(
        update_kernel,
        [mask, mixed, w_out, line(out_gain), line(out_bias), dproj, cot2, normed, w_in],
        [((CELLS, H), BF16), ((CELLS, H), BF16), ((2, H, H), BF16),
         ((A, H, LANES), BF16), ((A, H, LANES), BF16)],
        [vm(*one_shape), *gates, dma((2,))],
        600_000_000, smem_in=(0,), hbm_out=(3, 4),
    )
    send, pg_near, pvg_near = call(
        back_kernel,
        [recv, left, right, pg, pvg],
        [(both_shape, BF16), ((A, H, LANES), BF16), ((A, H, LANES), BF16)],
        [vm(N, 512, dtype=BF16), vm(512, 512, dtype=BF16), vm(*one_shape), vm(4 * N, LANES),
         vm(N, 512), vm(4 * 512, LANES), vm(*both_shape), dma((4,))],
        800_000_000, hbm_in=(1, 2, 3, 4),
    )
    recv = exchange(send, 9, 2)
    (send,) = call(
        grad_kernel,
        [recv, pg_near, pvg_near, normed, grads],
        [(sum_shape, BF16)],
        [vm(*both_shape), vm(*sum_shape)],
        400_000_000,
    )
    parts = exchange(send, 3, 2)
    (pair_grad,) = call(
        pair_grad_kernel,
        [recv, pg, pvg, d_og, normal, scale, line(in_gain), w_in],
        [((CELLS, H), BF16)],
        [vm(*both_shape), *gates, dma((2,))],
        400_000_000, hbm_in=(1, 2),
    )
    (send,) = call(sum_kernel, [parts], [(sum_shape, BF16)], [], 1_000_000)
    sums = exchange(send, 3, 2)
    w_in_grad, w_out_grad = call(
        unpack_kernel,
        [sums],
        [((H, 5 * H), F32), ((H, H), F32)],
        [vm(*sum_shape)],
        1_000_000,
    )
    return (update.reshape(A, B, H), pair_grad.reshape(A, B, H), w_in_grad, w_out_grad)


def solution(mesh):
    placed = (P("row", "col", None), P(), P(), P(), P(), P(), P(), P(), P("row", "col", None))
    return jax.shard_map(
        on_device,
        mesh=mesh,
        in_specs=placed,
        out_specs=(P("row", "col", None), P("row", "col", None), P(), P()),
        check_vma=False,
    )
```

```python
import math

import jax
import jax.numpy as jnp
from jax import lax
from jax.experimental import pallas as pl
from jax.experimental.pallas import tpu as pltpu
from jax.sharding import PartitionSpec as P

F32 = jnp.float32
BF16 = jnp.bfloat16
EPS = 1e-05
AXES = ("row", "col")

A, B, HALF, LANES = 24, 48, 64, 128
NR, NC, ND = 16, 8, 128
CELLS = A * B
H = 128
N = NR * A
BOTH, ONE, SUMS = 18, 10, 6

NT = ((1,), (1,))
TN = ((0,), (0,))
NN = ((1,), (0,))
VMEM_SPEC = pl.BlockSpec(memory_space=pltpu.VMEM)
HBM_SPEC = pl.BlockSpec(memory_space=pltpu.HBM)


def dot(x, y, contract):
    return lax.dot_general(x, y, (contract, ((), ())), preferred_element_type=F32)


def roll(x, shift):
    return pltpu.roll(x, shift % LANES, x.ndim - 1)


def lane_of(shape):
    return lax.broadcasted_iota(jnp.int32, shape, len(shape) - 1)


def two_sided(x):
    none = jnp.zeros_like(x)
    rest = jnp.zeros((LANES - 2 * B, 2 * x.shape[1]), x.dtype)
    return jnp.concatenate(
        [jnp.concatenate([x, none], 1), jnp.concatenate([none, x], 1), rest], 0
    )


def pieces(q):
    if q == 8:
        return [((16 + n) * B + 32, 16 * n, 16) for n in range(8)]
    return [(q * B, 0, B), ((8 + q) * B, B, B), ((16 + q) * B, 2 * B, 32)]


def row_cells(ref, q):
    return jnp.concatenate([ref[at : at + size, :] for at, _, size in pieces(q)], 0)


def column(row):
    at = lax.broadcasted_iota(jnp.int32, (H, LANES), 0)
    return jnp.sum(jnp.where(at == lane_of((H, LANES)), row, 0.0), 1, keepdims=True)


def stacked_weights(w_ref):
    part = [w_ref[:, p * H : (p + 1) * H].astype(F32).T.astype(BF16) for p in range(4)]
    return jnp.concatenate(
        [jnp.concatenate([part[0], part[2]], 1), jnp.concatenate([part[1], part[3]], 1)], 0
    )


def column_mask(mask_s):
    start = lax.axis_index("col") * B
    lane = lane_of((8, LANES))
    place = jnp.where(lane < B, lane, lane - B)
    out = jnp.zeros((8, LANES), F32)
    for b in range(B):
        out = jnp.where(place == b, mask_s[start + b].astype(F32), out)
    return out[0:1, :]


def gate_parts(weights, normed, pair_at, col_mask, mask_s):
    cells = jnp.concatenate([two_sided(normed[:B]), two_sided(normed[B:])], 0)
    pre = dot(weights, cells, NT)
    start = lax.axis_index("row") * A
    for k in range(2):
        value = pre[:H, k * LANES : (k + 1) * LANES]
        gate = jax.nn.sigmoid(pre[H:, k * LANES : (k + 1) * LANES])
        seen = col_mask * mask_s[start + 2 * pair_at + k].astype(F32)
        yield value, gate, gate * seen


def pack_both(block, third, a):
    shift = LANES - 32 if a < 8 else HALF
    return jnp.where(lane_of(block.shape) < 2 * B, block, roll(third, shift))


def pack_tail(third, n):
    lane = lane_of((H, LANES))
    out = roll(third[4 * n], -HALF)
    for m in range(1, 4):
        out = jnp.where(lane >= 32 * m, roll(third[4 * n + m], 32 * m - HALF), out)
    return out


def unpack_third(block, s):
    first, second, last = block(s), block(8 + s), block(16 + s // 4)
    lane = lane_of(first.shape)
    return jnp.where(
        lane < 32, roll(first, 32),
        jnp.where(lane < HALF, roll(second, HALF), roll(last, HALF - 32 * (s % 4))),
    )


def norm_rows(x):
    center = x - jnp.mean(x, 1, keepdims=True)
    scale = lax.rsqrt(jnp.mean(center * center, 1, keepdims=True) + EPS)
    return center * scale, scale


def norm_cells(x):
    center = x - jnp.mean(x, 0, keepdims=True)
    scale = lax.rsqrt(jnp.mean(center * center, 0, keepdims=True) + EPS)
    return center * scale, scale


def project_kernel(mask_h, pair_h, gain_h, bias_h, w_h, cot_h, out_gain_h, w_out_h,
                   send_ref, normed_ref, dproj_ref, spread_ref, w_out_ref,
                   mask_s, pair_v, gain_v, bias_v, w_v, cot_v, out_gain_v, third, scratch, sems):
    copies = [
        pltpu.make_async_copy(src, dst, sems.at[n])
        for n, (src, dst) in enumerate([
            (w_h, w_v), (pair_h, pair_v), (mask_h, mask_s), (gain_h, gain_v), (bias_h, bias_v),
            (cot_h, cot_v), (out_gain_h, out_gain_v), (w_out_h, w_out_ref),
        ])
    ]
    for copy in copies:
        copy.start()
    copies[0].wait()
    weights = stacked_weights(w_v)
    w_og = w_v[:, 4 * H :]
    for copy in copies[1:]:
        copy.wait()
    spread_ref[...] = jnp.broadcast_to(column(out_gain_v[...]), (H, LANES))
    col_mask = column_mask(mask_s)
    gain, bias = gain_v[...], bias_v[...]
    for pair_at in (8, 9, 10, 11, 0, 1, 2, 3, 4, 5, 6, 7):
        rows = pl.ds(pair_at * 2 * B, 2 * B)
        normal, _ = norm_rows(pair_v[rows, :].astype(F32))
        normed = (normal * gain + bias).astype(BF16)
        normed_ref[rows, :] = normed
        sig = jax.nn.sigmoid(dot(normed, w_og, NN))
        dproj_ref[rows, :] = (cot_v[rows, :].astype(F32) * sig).astype(BF16)
        for k, (value, _, pg) in enumerate(gate_parts(weights, normed, pair_at, col_mask, mask_s)):
            a = pair_at * 2 + k
            if a >= 16:
                third[a - 16] = pg * value
            else:
                scratch[pl.ds(a, H, stride=BOTH), :] = pack_both(pg * value, third[a % 8], a)
        if pair_at == 11:
            for n in range(2):
                scratch[pl.ds(16 + n, H, stride=BOTH), :] = pack_tail(third, n)
    send_ref[...] = scratch[...].astype(BF16)


def pick(lane, *parts):
    out = parts[-1]
    for n in range(len(parts) - 3, -1, -2):
        out = jnp.where(lane < parts[n + 1], parts[n], out)
    return out


def mix_kernel(recv_ref, send_ref, left_h, right_h, left_ref, right_ref, scratch, third, mixed,
               out, sems):
    scratch[...] = recv_ref[...].astype(F32)
    lane, wide = lane_of((8, LANES)), lane_of((NR, LANES))
    for p in range(NC // 2):
        for n in range(8):
            x, y = (
                scratch[pl.ds(c * BOTH + 16 + n // 4, NR, stride=NC * BOTH), :]
                for c in (2 * p, 2 * p + 1)
            )
            shift = -32 * (n % 4)
            third[pl.ds(p * LANES + n, NR, stride=8), :] = jnp.where(
                wide < HALF, roll(x, shift + 16), roll(y, shift + 80)
            )
    for r2 in range(NR // 2):
        right_ref[r2 * HALF + B : (r2 + 1) * HALF, :] = jnp.zeros((HALF - B, 512), BF16)
        for p in range(NC // 2):
            lefts, rights = [], []
            for r in (2 * r2, 2 * r2 + 1):
                start = (r * NC + 2 * p) * BOTH
                x, y = scratch[pl.ds(start, 16), :], scratch[pl.ds(start + BOTH, 16), :]
                tail = third[p * LANES + r * 8 : p * LANES + r * 8 + 8, :]
                lefts += [
                    jnp.where(wide < HALF, x, roll(y, HALF)),
                    pick(lane, roll(x[:8], 32), 32, roll(x[8:], HALF), HALF, roll(y[:8], 96), 96, y[8:]),
                ]
                rights += [
                    pick(wide, roll(x, -B), B, 0.0, HALF, roll(y, HALF - B), HALF + B, 0.0),
                    pick(lane, roll(x[8:], 16), 16, tail, B, 0.0, HALF,
                         roll(y[8:], 80), 80, tail, HALF + B, 0.0),
                ]
            lanes = slice(p * LANES, (p + 1) * LANES)
            left_ref[r2 * B : (r2 + 1) * B, lanes] = jnp.concatenate(lefts, 0).astype(BF16)
            right_ref[r2 * HALF : r2 * HALF + B, lanes] = jnp.concatenate(rights, 0).astype(BF16)
    copies = [pltpu.make_async_copy(left_ref, left_h, sems.at[0]),
              pltpu.make_async_copy(right_ref, right_h, sems.at[1])]
    for copy in copies:
        copy.start()
    product = dot(left_ref[...], right_ref[...], NT)
    for p in range(NC // 2):
        mixed[p * N : (p + 1) * N, :] = product[:, p * LANES : (p + 1) * LANES]
    for r in range(NR):
        for p in range(NC // 2):
            t0, t1, t2 = (
                mixed[p * N + r * A + 8 * t : p * N + r * A + 8 * t + 8, :] for t in range(3)
            )
            start = (r * NC + 2 * p) * ONE
            out[pl.ds(start, 8), :] = pick(lane, t0, B, roll(t1, B), 2 * B, roll(t2, 96))
            out[pl.ds(start + ONE, 8), :] = pick(
                lane, roll(t0, HALF), B, roll(t1, -16), 2 * B, roll(t2, 32)
            )
    out[pl.ds(9, ND, stride=ONE), :] = jnp.zeros((ND, LANES), F32)
    group = wide >> 4
    for p in range(NC // 2):
        first = second = jnp.zeros((NR, LANES), F32)
        for n in range(8):
            t2 = mixed[pl.ds(p * N + 16 + n, NR, stride=A), :]
            first = jnp.where(group == n, roll(t2, 16 * n - 32), first)
            second = jnp.where(group == n, roll(t2, 16 * n - 96), second)
        out[pl.ds(2 * p * ONE + 8, NR, stride=NC * ONE), :] = first
        out[pl.ds((2 * p + 1) * ONE + 8, NR, stride=NC * ONE), :] = second
    send_ref[...] = out[...].astype(BF16)
    for copy in copies:
        copy.wait()


def d_mixed_kernel(recv_ref, dproj_ref, w_out_ref, spread_ref, send_ref, scratch):
    scratch[...] = recv_ref[...].astype(F32)
    gain = spread_ref[...]
    w_out = w_out_ref[...]
    for q in range(9):
        wt = dot(w_out, row_cells(dproj_ref, q), NT) * gain
        normal, scale = norm_cells(scratch[pl.ds(q, H, stride=ONE), :])
        scratch[pl.ds(q, H, stride=ONE), :] = scale * (
            wt - jnp.mean(wt, 0, keepdims=True) - normal * jnp.mean(wt * normal, 0, keepdims=True)
        )
    send_ref[...] = scratch[...].astype(BF16)


def update_kernel(mask_s, recv_ref, w_out_ref, gain_ref, bias_ref, dproj_ref, cot_ref,
                  normed_ref, w_ref, update_ref, d_og_ref, grads_ref, pg_h, pvg_h,
                  scratch, pg_v, pvg_v, sems):
    weights = stacked_weights(w_ref)
    col_mask = column_mask(mask_s)
    for pair_at in range(A // 2):
        normed = normed_ref[pl.ds(pair_at * 2 * B, 2 * B), :]
        for k, (value, gate, pg) in enumerate(gate_parts(weights, normed, pair_at, col_mask, mask_s)):
            pg_v[2 * pair_at + k] = pg.astype(BF16)
            pvg_v[2 * pair_at + k] = (pg * value * (1.0 - gate)).astype(BF16)
    copies = [pltpu.make_async_copy(pg_v, pg_h, sems.at[0]),
              pltpu.make_async_copy(pvg_v, pvg_h, sems.at[1])]
    for copy in copies:
        copy.start()
    scratch[...] = recv_ref[...].astype(F32)
    gain, bias = column(gain_ref[...]), column(bias_ref[...])
    w_out, w_og = w_out_ref[...], w_ref[:, 4 * H :]
    grad = jnp.zeros((H, H), F32)
    for q in range(9):
        normal, _ = norm_cells(scratch[pl.ds(q, H, stride=ONE), :])
        out_normed = (normal * gain + bias).astype(BF16)
        projected = dot(out_normed, w_out, TN)
        grad = grad + dot(out_normed, row_cells(dproj_ref, q), NN)
        gates = jax.nn.sigmoid(dot(row_cells(normed_ref, q), w_og, NN))
        for at, lane, size in pieces(q):
            rows = pl.ds(at, size)
            sig, proj = gates[lane : lane + size], projected[lane : lane + size]
            update_ref[rows, :] = (sig * proj).astype(BF16)
            d_og_ref[rows, :] = (
                cot_ref[rows, :].astype(F32) * proj * sig * (1.0 - sig)
            ).astype(BF16)
    grads_ref[0] = dot(d_og_ref[...], normed_ref[...], TN).astype(BF16)
    grads_ref[1] = grad.astype(BF16)
    for copy in copies:
        copy.wait()


def back_kernel(recv_ref, left_h, right_h, pg_h, pvg_h, send_ref, pg_ref, pvg_ref,
                left_ref, right_ref, scratch, d_tile, d_left, d_right, out, sems):
    copies = [
        pltpu.make_async_copy(src, dst, sems.at[n])
        for n, (src, dst) in enumerate(
            [(right_h, right_ref), (left_h, left_ref), (pg_h, pg_ref), (pvg_h, pvg_ref)]
        )
    ]
    for copy in copies:
        copy.start()
    scratch[...] = recv_ref[...].astype(F32)
    lane, wide = lane_of((8, LANES)), lane_of((NR, LANES))
    for p in range(NC // 2):
        x, y = (
            scratch[pl.ds(c * ONE + 8, NR, stride=NC * ONE), :] for c in (2 * p, 2 * p + 1)
        )
        for n in range(8):
            d_tile[pl.ds(p * N + 16 + n, NR, stride=A), :] = jnp.where(
                wide < HALF, roll(x, 32 - 16 * n), roll(y, 96 - 16 * n)
            )
    for r in range(NR):
        for p in range(NC // 2):
            start = (r * NC + 2 * p) * ONE
            x, y = scratch[pl.ds(start, 8), :], scratch[pl.ds(start + ONE, 8), :]
            at = p * N + r * A
            tail = d_tile[at + 16 : at + 24, :]
            d_tile[at : at + 8, :] = jnp.where(lane < HALF, x, roll(y, HALF))
            d_tile[at + 8 : at + 16, :] = jnp.where(lane < HALF, roll(x, -B), roll(y, 16))
            d_tile[at + 16 : at + 24, :] = pick(
                lane, roll(x, 32), 32, tail, HALF, roll(y, 96), 96, tail
            )
    d = jnp.concatenate([d_tile[p * N : (p + 1) * N, :].astype(BF16) for p in range(4)], 1)
    copies[0].wait()
    copies[1].wait()
    d_left[...] = dot(d, right_ref[...], NN)
    product = dot(d, left_ref[...], TN)
    for p in range(NC // 2):
        d_right[p * 512 : (p + 1) * 512, :] = product[:, p * LANES : (p + 1) * LANES]
    for r in range(NR):
        for p in range(NC // 2):
            lanes = slice(p * LANES, (p + 1) * LANES)
            at = p * 512 + (r // 2) * HALF + (r % 2) * A
            x0, x1, x2 = (d_left[r * A + 8 * t : r * A + 8 * t + 8, lanes] for t in range(3))
            y0, y1, y2 = (d_right[at + 8 * t : at + 8 * t + 8, :] for t in range(3))
            start = (r * NC + 2 * p) * BOTH
            out[pl.ds(start, 8), :] = pick(lane, x0, B, roll(y0, B), 2 * B, roll(x2, 96))
            out[pl.ds(start + 8, 8), :] = pick(
                lane, x1, B, roll(y1, B), 2 * B, roll(x2, HALF), 112, roll(y2, 112)
            )
            start = start + BOTH
            out[pl.ds(start, 8), :] = pick(lane, roll(x0, HALF), B, roll(y0, -16), 2 * B, roll(x2, 32))
            out[pl.ds(start + 8, 8), :] = pick(
                lane, roll(x1, HALF), B, roll(y1, -16), 2 * B, x2, 112, roll(y2, B)
            )
    group = lane >> 5
    for p in range(NC // 2):
        for odd in range(2):
            for half in range(2):
                first = second = jnp.zeros((8, LANES), F32)
                for m in range(4):
                    at = p * 512 + odd * A + 16 + 4 * half + m
                    y2 = d_right[pl.ds(at, 8, stride=HALF), :]
                    first = jnp.where(group == m, roll(y2, 32 * m - 16), first)
                    second = jnp.where(group == m, roll(y2, 32 * m - 80), second)
                start = (odd * NC + 2 * p) * BOTH + 16 + half
                out[pl.ds(start, 8, stride=2 * NC * BOTH), :] = first
                out[pl.ds(start + BOTH, 8, stride=2 * NC * BOTH), :] = second
    send_ref[...] = out[...].astype(BF16)
    copies[2].wait()
    copies[3].wait()


def gated(scratch, a, pg_v, pvg_v):
    block = lambda p: scratch[pl.ds(p, H, stride=BOTH), :]
    d = block(a) if a < 16 else unpack_third(block, a - 16)
    return jnp.concatenate([d * pg_v[a].astype(F32), d * pvg_v[a].astype(F32)], 0).astype(BF16)


def grad_kernel(recv_ref, pg_v, pvg_v, normed_ref, grads_ref, send_ref, scratch, packed):
    scratch[...] = recv_ref[...].astype(F32)
    for g in range(2):
        packed[pl.ds(4 + g, H, stride=SUMS), :] = grads_ref[g].astype(F32)
    total = jnp.zeros((2 * H, 2 * H), F32)
    for pair_at in range(A // 2):
        a = 2 * pair_at
        sides = [gated(scratch, a + k, pg_v, pvg_v) for k in range(2)]
        cells = [two_sided(normed_ref[(a + k) * B : (a + k + 1) * B, :]) for k in range(2)]
        total = total + dot(jnp.concatenate(sides, 1), jnp.concatenate(cells, 0), NN)
    for g, block in enumerate([total[:H, :H], total[H:, :H], total[:H, H:], total[H:, H:]]):
        packed[pl.ds(g, H, stride=SUMS), :] = block
    send_ref[...] = packed[...].astype(BF16)


def pair_grad_kernel(recv_ref, pg_h, pvg_h, d_og_ref, pair_ref, gain_ref, w_ref,
                     out_ref, scratch, pg_v, pvg_v, sems):
    copies = [pltpu.make_async_copy(pg_h, pg_v, sems.at[0]),
              pltpu.make_async_copy(pvg_h, pvg_v, sems.at[1])]
    for copy in copies:
        copy.start()
    scratch[...] = recv_ref[...].astype(F32)
    weights = stacked_weights(w_ref)
    w_og = w_ref[:, 4 * H :]
    gain = gain_ref[...]
    for copy in copies:
        copy.wait()
    for a in range(A):
        rows = pl.ds(a * B, B)
        both = dot(gated(scratch, a, pg_v, pvg_v), weights, TN)
        d = both[:B, :H] + both[B : 2 * B, H:] + dot(d_og_ref[rows, :], w_og, NT)
        normal, scale = norm_rows(pair_ref[rows, :].astype(F32))
        weighted = d * gain
        out_ref[rows, :] = (
            scale * (weighted - jnp.mean(weighted, 1, keepdims=True)
                     - normal * jnp.mean(weighted * normal, 1, keepdims=True))
        ).astype(BF16)


def sum_kernel(recv_ref, send_ref):
    parts = jnp.sum(recv_ref[...].astype(F32).reshape(16, 8 * SUMS, LANES), 0)
    total = parts[:SUMS]
    for k in range(1, 8):
        total = total + parts[k * SUMS : (k + 1) * SUMS]
    many = jnp.concatenate([total] * 8, 0).astype(BF16)
    for s in range(16):
        send_ref[s * 8 * SUMS : (s + 1) * 8 * SUMS, :] = many


def unpack_kernel(recv_ref, w_in_ref, w_out_ref, scratch):
    scratch[...] = recv_ref[...].astype(F32)
    for g in range(5):
        w_in_ref[:, g * H : (g + 1) * H] = scratch[pl.ds(g, H, stride=SUMS), :].T
    w_out_ref[...] = scratch[pl.ds(5, H, stride=SUMS), :]


def call(kernel, args, outs, scratch, flops, hbm_in=(), smem_in=(), hbm_out=()):
    shapes = [
        pltpu.HBM(s, d) if n in hbm_out else jax.ShapeDtypeStruct(s, d)
        for n, (s, d) in enumerate(outs)
    ]
    args = [
        pltpu.with_memory_space_constraint(v, pltpu.HBM) if n in hbm_in else v
        for n, v in enumerate(args)
    ]
    specs = [
        HBM_SPEC if n in hbm_in else pl.BlockSpec(memory_space=pltpu.SMEM) if n in smem_in else VMEM_SPEC
        for n in range(len(args))
    ]
    moved = 2 * (sum(v.size for v in args) + sum(math.prod(s) for s, _ in outs))
    return pl.pallas_call(
        kernel,
        out_shape=shapes,
        in_specs=specs,
        out_specs=[HBM_SPEC if n in hbm_out else VMEM_SPEC for n in range(len(shapes))],
        scratch_shapes=scratch,
        cost_estimate=pl.CostEstimate(flops=flops, bytes_accessed=moved, transcendentals=0),
        compiler_params=pltpu.CompilerParams(vmem_limit_bytes=40 * 2**20),
    )(*args)


def vm(*shape, dtype=F32):
    return pltpu.VMEM(shape, dtype)


def exchange(x, *tile):
    moved = lax.all_to_all(x.reshape(ND, *tile, LANES), AXES, 0, 0, tiled=True)
    return moved.reshape(x.shape)


def on_device(pair, mask, in_gain, in_bias, w_in, out_gain, out_bias, w_out, cotangent):
    pair2 = pair.reshape(CELLS, H)
    cot2 = cotangent.reshape(CELLS, H)
    line = lambda v: v.reshape(1, -1)
    dma = pltpu.SemaphoreType.DMA
    both_shape, one_shape, sum_shape = ((ND * n, LANES) for n in (BOTH, ONE, SUMS))
    gates = [vm(A, H, LANES, dtype=BF16)] * 2

    send, normed, dproj, spread, w_out_near = call(
        project_kernel,
        [mask, pair2, line(in_gain), line(in_bias), w_in, cot2, line(out_gain), w_out],
        [(both_shape, BF16), ((CELLS, H), BF16), ((CELLS, H), BF16), ((H, LANES), F32),
         ((H, H), BF16)],
        [pltpu.SMEM((N,), jnp.int32), vm(CELLS, H, dtype=BF16), vm(1, H), vm(1, H),
         vm(H, 5 * H, dtype=BF16), vm(CELLS, H, dtype=BF16), vm(1, H), vm(8, H, LANES),
         vm(*both_shape), dma((8,))],
        500_000_000, hbm_in=range(8),
    )
    recv = exchange(send, 9, 2)
    send, left, right = call(
        mix_kernel,
        [recv],
        [(one_shape, BF16), ((N, 512), BF16), ((512, 512), BF16)],
        [vm(N, 512, dtype=BF16), vm(512, 512, dtype=BF16), vm(*both_shape), vm(512, LANES),
         vm(4 * N, LANES), vm(*one_shape), dma((2,))],
        400_000_000, hbm_out=(1, 2),
    )
    mixed = exchange(send, 5, 2)
    (send,) = call(
        d_mixed_kernel,
        [mixed, dproj, w_out_near, spread],
        [(one_shape, BF16)],
        [vm(*one_shape)],
        50_000_000,
    )
    recv = exchange(send, 5, 2)
    update, d_og, grads, pg, pvg = call(
        update_kernel,
        [mask, mixed, w_out_near, line(out_gain), line(out_bias), dproj, cot2, normed, w_in],
        [((CELLS, H), BF16), ((CELLS, H), BF16), ((2, H, H), BF16),
         ((A, H, LANES), BF16), ((A, H, LANES), BF16)],
        [vm(*one_shape), *gates, dma((2,))],
        600_000_000, smem_in=(0,), hbm_out=(3, 4),
    )
    send, pg_near, pvg_near = call(
        back_kernel,
        [recv, left, right, pg, pvg],
        [(both_shape, BF16), ((A, H, LANES), BF16), ((A, H, LANES), BF16)],
        [vm(N, 512, dtype=BF16), vm(512, 512, dtype=BF16), vm(*one_shape), vm(4 * N, LANES),
         vm(N, 512), vm(4 * 512, LANES), vm(*both_shape), dma((4,))],
        800_000_000, hbm_in=(1, 2, 3, 4),
    )
    recv = exchange(send, 9, 2)
    (send,) = call(
        grad_kernel,
        [recv, pg_near, pvg_near, normed, grads],
        [(sum_shape, BF16)],
        [vm(*both_shape), vm(*sum_shape)],
        400_000_000,
    )
    parts = exchange(send, 3, 2)
    (pair_grad,) = call(
        pair_grad_kernel,
        [recv, pg, pvg, d_og, pair2, line(in_gain), w_in],
        [((CELLS, H), BF16)],
        [vm(*both_shape), *gates, dma((2,))],
        400_000_000, hbm_in=(1, 2),
    )
    (send,) = call(sum_kernel, [parts], [(sum_shape, BF16)], [], 1_000_000)
    sums = exchange(send, 3, 2)
    w_in_grad, w_out_grad = call(
        unpack_kernel,
        [sums],
        [((H, 5 * H), F32), ((H, H), F32)],
        [vm(*sum_shape)],
        1_000_000,
    )
    return (update.reshape(A, B, H), pair_grad.reshape(A, B, H), w_in_grad, w_out_grad)


def solution(mesh):
    placed = (P("row", "col", None), P(), P(), P(), P(), P(), P(), P(), P("row", "col", None))
    return jax.shard_map(
        on_device,
        mesh=mesh,
        in_specs=placed,
        out_specs=(P("row", "col", None), P("row", "col", None), P(), P()),
        check_vma=False,
    )
```

```python
import math

import jax
import jax.numpy as jnp
from jax import lax
from jax.experimental import pallas as pl
from jax.experimental.pallas import tpu as pltpu
from jax.sharding import PartitionSpec as P

F32 = jnp.float32
BF16 = jnp.bfloat16
EPS = 1e-05
AXES = ("row", "col")

A, B, HALF, LANES = 24, 48, 64, 128
NR, NC, ND = 16, 8, 128
CELLS = A * B
H = 128
N = NR * A
BOTH, ONE, SUMS = 18, 10, 6

NT = ((1,), (1,))
TN = ((0,), (0,))
NN = ((1,), (0,))
VMEM_SPEC = pl.BlockSpec(memory_space=pltpu.VMEM)
HBM_SPEC = pl.BlockSpec(memory_space=pltpu.HBM)


def dot(x, y, contract):
    return lax.dot_general(x, y, (contract, ((), ())), preferred_element_type=F32)


def roll(x, shift):
    return pltpu.roll(x, shift % LANES, x.ndim - 1)


def lane_of(shape):
    return lax.broadcasted_iota(jnp.int32, shape, len(shape) - 1)


def two_sided(x):
    none = jnp.zeros_like(x)
    rest = jnp.zeros((LANES - 2 * B, 2 * x.shape[1]), x.dtype)
    return jnp.concatenate(
        [jnp.concatenate([x, none], 1), jnp.concatenate([none, x], 1), rest], 0
    )


def pieces(q):
    if q == 8:
        return [((16 + n) * B + 32, 16 * n, 16) for n in range(8)]
    return [(q * B, 0, B), ((8 + q) * B, B, B), ((16 + q) * B, 2 * B, 32)]


def row_cells(ref, q):
    return jnp.concatenate([ref[at : at + size, :] for at, _, size in pieces(q)], 0)


def column(row):
    at = lax.broadcasted_iota(jnp.int32, (H, LANES), 0)
    return jnp.sum(jnp.where(at == lane_of((H, LANES)), row, 0.0), 1, keepdims=True)


def stacked_weights(w_ref):
    part = [w_ref[:, p * H : (p + 1) * H].astype(F32).T.astype(BF16) for p in range(4)]
    return jnp.concatenate(
        [jnp.concatenate([part[0], part[2]], 1), jnp.concatenate([part[1], part[3]], 1)], 0
    )


def column_mask(mask_s):
    start = lax.axis_index("col") * B
    lane = lane_of((8, LANES))
    place = jnp.where(lane < B, lane, lane - B)
    out = jnp.zeros((8, LANES), F32)
    for b in range(B):
        out = jnp.where(place == b, mask_s[start + b].astype(F32), out)
    return out[0:1, :]


def gate_parts(weights, normed, pair_at, col_mask, mask_s):
    cells = jnp.concatenate([two_sided(normed[:B]), two_sided(normed[B:])], 0)
    pre = dot(weights, cells, NT)
    start = lax.axis_index("row") * A
    for k in range(2):
        value = pre[:H, k * LANES : (k + 1) * LANES]
        gate = jax.nn.sigmoid(pre[H:, k * LANES : (k + 1) * LANES])
        seen = col_mask * mask_s[start + 2 * pair_at + k].astype(F32)
        yield value, gate, gate * seen


def pack_both(block, third, a):
    shift = LANES - 32 if a < 8 else HALF
    return jnp.where(lane_of(block.shape) < 2 * B, block, roll(third, shift))


def pack_tail(third, n):
    lane = lane_of((H, LANES))
    out = roll(third[4 * n], -HALF)
    for m in range(1, 4):
        out = jnp.where(lane >= 32 * m, roll(third[4 * n + m], 32 * m - HALF), out)
    return out


def unpack_third(block, s):
    first, second, last = block(s), block(8 + s), block(16 + s // 4)
    lane = lane_of(first.shape)
    return jnp.where(
        lane < 32, roll(first, 32),
        jnp.where(lane < HALF, roll(second, HALF), roll(last, HALF - 32 * (s % 4))),
    )


def norm_rows(x):
    center = x - jnp.mean(x, 1, keepdims=True)
    scale = lax.rsqrt(jnp.mean(center * center, 1, keepdims=True) + EPS)
    return center * scale, scale


def norm_cells(x):
    center = x - jnp.mean(x, 0, keepdims=True)
    scale = lax.rsqrt(jnp.mean(center * center, 0, keepdims=True) + EPS)
    return center * scale, scale


def project_kernel(mask_h, pair_h, gain_h, bias_h, w_h, cot_h, out_gain_h, w_out_h,
                   send_ref, normed_ref, dproj_ref, spread_ref, w_out_ref,
                   mask_s, pair_v, gain_v, bias_v, w_v, cot_v, out_gain_v, third, scratch, sems):
    copies = [
        pltpu.make_async_copy(src, dst, sems.at[n])
        for n, (src, dst) in enumerate([
            (w_h, w_v), (pair_h, pair_v), (mask_h, mask_s), (gain_h, gain_v), (bias_h, bias_v),
            (cot_h, cot_v), (out_gain_h, out_gain_v), (w_out_h, w_out_ref),
        ])
    ]
    for copy in copies:
        copy.start()
    copies[0].wait()
    weights = stacked_weights(w_v)
    w_og = w_v[:, 4 * H :]
    for copy in copies[1:]:
        copy.wait()
    spread_ref[...] = jnp.broadcast_to(column(out_gain_v[...]), (H, LANES))
    col_mask = column_mask(mask_s)
    gain, bias = gain_v[...], bias_v[...]
    for pair_at in (8, 9, 10, 11, 0, 1, 2, 3, 4, 5, 6, 7):
        rows = pl.ds(pair_at * 2 * B, 2 * B)
        normal, _ = norm_rows(pair_v[rows, :].astype(F32))
        normed = (normal * gain + bias).astype(BF16)
        normed_ref[rows, :] = normed
        sig = jax.nn.sigmoid(dot(normed, w_og, NN))
        dproj_ref[rows, :] = (cot_v[rows, :].astype(F32) * sig).astype(BF16)
        for k, (value, _, pg) in enumerate(gate_parts(weights, normed, pair_at, col_mask, mask_s)):
            a = pair_at * 2 + k
            if a >= 16:
                third[a - 16] = pg * value
            else:
                scratch[pl.ds(a, H, stride=BOTH), :] = pack_both(pg * value, third[a % 8], a)
        if pair_at == 11:
            for n in range(2):
                scratch[pl.ds(16 + n, H, stride=BOTH), :] = pack_tail(third, n)
    send_ref[...] = scratch[...].astype(BF16)


def pick(lane, *parts):
    out = parts[-1]
    for n in range(len(parts) - 3, -1, -2):
        out = jnp.where(lane < parts[n + 1], parts[n], out)
    return out


def mix_kernel(recv_ref, send_ref, left_ref, right_ref, scratch, third, mixed, out):
    scratch[...] = recv_ref[...].astype(F32)
    lane, wide = lane_of((8, LANES)), lane_of((NR, LANES))
    for p in range(NC // 2):
        for n in range(8):
            x, y = (
                scratch[pl.ds(c * BOTH + 16 + n // 4, NR, stride=NC * BOTH), :]
                for c in (2 * p, 2 * p + 1)
            )
            shift = -32 * (n % 4)
            third[pl.ds(p * LANES + n, NR, stride=8), :] = jnp.where(
                wide < HALF, roll(x, shift + 16), roll(y, shift + 80)
            )
    for r2 in range(NR // 2):
        right_ref[r2 * HALF + B : (r2 + 1) * HALF, :] = jnp.zeros((HALF - B, 512), BF16)
        for p in range(NC // 2):
            lefts, rights = [], []
            for r in (2 * r2, 2 * r2 + 1):
                start = (r * NC + 2 * p) * BOTH
                x, y = scratch[pl.ds(start, 16), :], scratch[pl.ds(start + BOTH, 16), :]
                tail = third[p * LANES + r * 8 : p * LANES + r * 8 + 8, :]
                lefts += [
                    jnp.where(wide < HALF, x, roll(y, HALF)),
                    pick(lane, roll(x[:8], 32), 32, roll(x[8:], HALF), HALF, roll(y[:8], 96), 96, y[8:]),
                ]
                rights += [
                    pick(wide, roll(x, -B), B, 0.0, HALF, roll(y, HALF - B), HALF + B, 0.0),
                    pick(lane, roll(x[8:], 16), 16, tail, B, 0.0, HALF,
                         roll(y[8:], 80), 80, tail, HALF + B, 0.0),
                ]
            lanes = slice(p * LANES, (p + 1) * LANES)
            left_ref[r2 * B : (r2 + 1) * B, lanes] = jnp.concatenate(lefts, 0).astype(BF16)
            right_ref[r2 * HALF : r2 * HALF + B, lanes] = jnp.concatenate(rights, 0).astype(BF16)
    product = dot(left_ref[...], right_ref[...], NT)
    for p in range(NC // 2):
        mixed[p * N : (p + 1) * N, :] = product[:, p * LANES : (p + 1) * LANES]
    for r in range(NR):
        for p in range(NC // 2):
            t0, t1, t2 = (
                mixed[p * N + r * A + 8 * t : p * N + r * A + 8 * t + 8, :] for t in range(3)
            )
            start = (r * NC + 2 * p) * ONE
            out[pl.ds(start, 8), :] = pick(lane, t0, B, roll(t1, B), 2 * B, roll(t2, 96))
            out[pl.ds(start + ONE, 8), :] = pick(
                lane, roll(t0, HALF), B, roll(t1, -16), 2 * B, roll(t2, 32)
            )
    out[pl.ds(9, ND, stride=ONE), :] = jnp.zeros((ND, LANES), F32)
    group = wide >> 4
    for p in range(NC // 2):
        first = second = jnp.zeros((NR, LANES), F32)
        for n in range(8):
            t2 = mixed[pl.ds(p * N + 16 + n, NR, stride=A), :]
            first = jnp.where(group == n, roll(t2, 16 * n - 32), first)
            second = jnp.where(group == n, roll(t2, 16 * n - 96), second)
        out[pl.ds(2 * p * ONE + 8, NR, stride=NC * ONE), :] = first
        out[pl.ds((2 * p + 1) * ONE + 8, NR, stride=NC * ONE), :] = second
    send_ref[...] = out[...].astype(BF16)


def d_mixed_kernel(recv_ref, dproj_ref, w_out_ref, spread_ref, send_ref, scratch):
    scratch[...] = recv_ref[...].astype(F32)
    gain = spread_ref[...]
    w_out = w_out_ref[...]
    for q in range(9):
        wt = dot(w_out, row_cells(dproj_ref, q), NT) * gain
        normal, scale = norm_cells(scratch[pl.ds(q, H, stride=ONE), :])
        scratch[pl.ds(q, H, stride=ONE), :] = scale * (
            wt - jnp.mean(wt, 0, keepdims=True) - normal * jnp.mean(wt * normal, 0, keepdims=True)
        )
    send_ref[...] = scratch[...].astype(BF16)


def update_kernel(mask_s, recv_ref, w_out_ref, gain_ref, bias_ref, dproj_ref, cot_ref,
                  normed_ref, w_ref, update_ref, d_og_ref, grads_ref, pg_h, pvg_h,
                  scratch, pg_v, pvg_v, sems):
    weights = stacked_weights(w_ref)
    col_mask = column_mask(mask_s)
    for pair_at in range(A // 2):
        normed = normed_ref[pl.ds(pair_at * 2 * B, 2 * B), :]
        for k, (value, gate, pg) in enumerate(gate_parts(weights, normed, pair_at, col_mask, mask_s)):
            pg_v[2 * pair_at + k] = pg.astype(BF16)
            pvg_v[2 * pair_at + k] = (pg * value * (1.0 - gate)).astype(BF16)
    copies = [pltpu.make_async_copy(pg_v, pg_h, sems.at[0]),
              pltpu.make_async_copy(pvg_v, pvg_h, sems.at[1])]
    for copy in copies:
        copy.start()
    scratch[...] = recv_ref[...].astype(F32)
    gain, bias = column(gain_ref[...]), column(bias_ref[...])
    w_out, w_og = w_out_ref[...], w_ref[:, 4 * H :]
    grad = jnp.zeros((H, H), F32)
    for q in range(9):
        normal, _ = norm_cells(scratch[pl.ds(q, H, stride=ONE), :])
        out_normed = (normal * gain + bias).astype(BF16)
        projected = dot(out_normed, w_out, TN)
        grad = grad + dot(out_normed, row_cells(dproj_ref, q), NN)
        gates = jax.nn.sigmoid(dot(row_cells(normed_ref, q), w_og, NN))
        for at, lane, size in pieces(q):
            rows = pl.ds(at, size)
            sig, proj = gates[lane : lane + size], projected[lane : lane + size]
            update_ref[rows, :] = (sig * proj).astype(BF16)
            d_og_ref[rows, :] = (
                cot_ref[rows, :].astype(F32) * proj * sig * (1.0 - sig)
            ).astype(BF16)
    grads_ref[0] = dot(d_og_ref[...], normed_ref[...], TN).astype(BF16)
    grads_ref[1] = grad.astype(BF16)
    for copy in copies:
        copy.wait()


def back_kernel(recv_ref, left_ref, right_ref, pg_h, pvg_h, send_ref, pg_ref, pvg_ref,
                scratch, d_tile, d_left, d_right, out, sems):
    copies = [
        pltpu.make_async_copy(src, dst, sems.at[n])
        for n, (src, dst) in enumerate(
            [(pg_h, pg_ref), (pvg_h, pvg_ref)]
        )
    ]
    for copy in copies:
        copy.start()
    scratch[...] = recv_ref[...].astype(F32)
    lane, wide = lane_of((8, LANES)), lane_of((NR, LANES))
    for p in range(NC // 2):
        x, y = (
            scratch[pl.ds(c * ONE + 8, NR, stride=NC * ONE), :] for c in (2 * p, 2 * p + 1)
        )
        for n in range(8):
            d_tile[pl.ds(p * N + 16 + n, NR, stride=A), :] = jnp.where(
                wide < HALF, roll(x, 32 - 16 * n), roll(y, 96 - 16 * n)
            )
    for r in range(NR):
        for p in range(NC // 2):
            start = (r * NC + 2 * p) * ONE
            x, y = scratch[pl.ds(start, 8), :], scratch[pl.ds(start + ONE, 8), :]
            at = p * N + r * A
            tail = d_tile[at + 16 : at + 24, :]
            d_tile[at : at + 8, :] = jnp.where(lane < HALF, x, roll(y, HALF))
            d_tile[at + 8 : at + 16, :] = jnp.where(lane < HALF, roll(x, -B), roll(y, 16))
            d_tile[at + 16 : at + 24, :] = pick(
                lane, roll(x, 32), 32, tail, HALF, roll(y, 96), 96, tail
            )
    d = jnp.concatenate([d_tile[p * N : (p + 1) * N, :].astype(BF16) for p in range(4)], 1)
    d_left[...] = dot(d, right_ref[...], NN)
    product = dot(d, left_ref[...], TN)
    for p in range(NC // 2):
        d_right[p * 512 : (p + 1) * 512, :] = product[:, p * LANES : (p + 1) * LANES]
    for r in range(NR):
        for p in range(NC // 2):
            lanes = slice(p * LANES, (p + 1) * LANES)
            at = p * 512 + (r // 2) * HALF + (r % 2) * A
            x0, x1, x2 = (d_left[r * A + 8 * t : r * A + 8 * t + 8, lanes] for t in range(3))
            y0, y1, y2 = (d_right[at + 8 * t : at + 8 * t + 8, :] for t in range(3))
            start = (r * NC + 2 * p) * BOTH
            out[pl.ds(start, 8), :] = pick(lane, x0, B, roll(y0, B), 2 * B, roll(x2, 96))
            out[pl.ds(start + 8, 8), :] = pick(
                lane, x1, B, roll(y1, B), 2 * B, roll(x2, HALF), 112, roll(y2, 112)
            )
            start = start + BOTH
            out[pl.ds(start, 8), :] = pick(lane, roll(x0, HALF), B, roll(y0, -16), 2 * B, roll(x2, 32))
            out[pl.ds(start + 8, 8), :] = pick(
                lane, roll(x1, HALF), B, roll(y1, -16), 2 * B, x2, 112, roll(y2, B)
            )
    group = lane >> 5
    for p in range(NC // 2):
        for odd in range(2):
            for half in range(2):
                first = second = jnp.zeros((8, LANES), F32)
                for m in range(4):
                    at = p * 512 + odd * A + 16 + 4 * half + m
                    y2 = d_right[pl.ds(at, 8, stride=HALF), :]
                    first = jnp.where(group == m, roll(y2, 32 * m - 16), first)
                    second = jnp.where(group == m, roll(y2, 32 * m - 80), second)
                start = (odd * NC + 2 * p) * BOTH + 16 + half
                out[pl.ds(start, 8, stride=2 * NC * BOTH), :] = first
                out[pl.ds(start + BOTH, 8, stride=2 * NC * BOTH), :] = second
    send_ref[...] = out[...].astype(BF16)
    for copy in copies:
        copy.wait()


def gated(scratch, a, pg_v, pvg_v):
    block = lambda p: scratch[pl.ds(p, H, stride=BOTH), :]
    d = block(a) if a < 16 else unpack_third(block, a - 16)
    return jnp.concatenate([d * pg_v[a].astype(F32), d * pvg_v[a].astype(F32)], 0).astype(BF16)


def grad_kernel(recv_ref, pg_v, pvg_v, normed_ref, grads_ref, send_ref, scratch, packed):
    scratch[...] = recv_ref[...].astype(F32)
    for g in range(2):
        packed[pl.ds(4 + g, H, stride=SUMS), :] = grads_ref[g].astype(F32)
    total = jnp.zeros((2 * H, 2 * H), F32)
    for pair_at in range(A // 2):
        a = 2 * pair_at
        sides = [gated(scratch, a + k, pg_v, pvg_v) for k in range(2)]
        cells = [two_sided(normed_ref[(a + k) * B : (a + k + 1) * B, :]) for k in range(2)]
        total = total + dot(jnp.concatenate(sides, 1), jnp.concatenate(cells, 0), NN)
    for g, block in enumerate([total[:H, :H], total[H:, :H], total[:H, H:], total[H:, H:]]):
        packed[pl.ds(g, H, stride=SUMS), :] = block
    send_ref[...] = packed[...].astype(BF16)


def pair_grad_kernel(recv_ref, pg_h, pvg_h, d_og_ref, pair_ref, gain_ref, w_ref,
                     out_ref, scratch, pg_v, pvg_v, sems):
    copies = [pltpu.make_async_copy(pg_h, pg_v, sems.at[0]),
              pltpu.make_async_copy(pvg_h, pvg_v, sems.at[1])]
    for copy in copies:
        copy.start()
    scratch[...] = recv_ref[...].astype(F32)
    weights = stacked_weights(w_ref)
    w_og = w_ref[:, 4 * H :]
    gain = gain_ref[...]
    for copy in copies:
        copy.wait()
    for a in range(A):
        rows = pl.ds(a * B, B)
        both = dot(gated(scratch, a, pg_v, pvg_v), weights, TN)
        d = both[:B, :H] + both[B : 2 * B, H:] + dot(d_og_ref[rows, :], w_og, NT)
        normal, scale = norm_rows(pair_ref[rows, :].astype(F32))
        weighted = d * gain
        out_ref[rows, :] = (
            scale * (weighted - jnp.mean(weighted, 1, keepdims=True)
                     - normal * jnp.mean(weighted * normal, 1, keepdims=True))
        ).astype(BF16)


def sum_kernel(recv_ref, send_ref):
    parts = jnp.sum(recv_ref[...].astype(F32).reshape(16, 8 * SUMS, LANES), 0)
    total = parts[:SUMS]
    for k in range(1, 8):
        total = total + parts[k * SUMS : (k + 1) * SUMS]
    many = jnp.concatenate([total] * 8, 0).astype(BF16)
    for s in range(16):
        send_ref[s * 8 * SUMS : (s + 1) * 8 * SUMS, :] = many


def unpack_kernel(recv_ref, w_in_ref, w_out_ref, scratch):
    scratch[...] = recv_ref[...].astype(F32)
    for g in range(5):
        w_in_ref[:, g * H : (g + 1) * H] = scratch[pl.ds(g, H, stride=SUMS), :].T
    w_out_ref[...] = scratch[pl.ds(5, H, stride=SUMS), :]


def call(kernel, args, outs, scratch, flops, hbm_in=(), smem_in=(), hbm_out=()):
    shapes = [
        pltpu.HBM(s, d) if n in hbm_out else jax.ShapeDtypeStruct(s, d)
        for n, (s, d) in enumerate(outs)
    ]
    args = [
        pltpu.with_memory_space_constraint(v, pltpu.HBM) if n in hbm_in else v
        for n, v in enumerate(args)
    ]
    specs = [
        HBM_SPEC if n in hbm_in else pl.BlockSpec(memory_space=pltpu.SMEM) if n in smem_in else VMEM_SPEC
        for n in range(len(args))
    ]
    moved = 2 * (sum(v.size for v in args) + sum(math.prod(s) for s, _ in outs))
    return pl.pallas_call(
        kernel,
        out_shape=shapes,
        in_specs=specs,
        out_specs=[HBM_SPEC if n in hbm_out else VMEM_SPEC for n in range(len(shapes))],
        scratch_shapes=scratch,
        cost_estimate=pl.CostEstimate(flops=flops, bytes_accessed=moved, transcendentals=0),
        compiler_params=pltpu.CompilerParams(vmem_limit_bytes=40 * 2**20),
    )(*args)


def vm(*shape, dtype=F32):
    return pltpu.VMEM(shape, dtype)


def exchange(x, *tile):
    moved = lax.all_to_all(x.reshape(ND, *tile, LANES), AXES, 0, 0, tiled=True)
    return moved.reshape(x.shape)


def on_device(pair, mask, in_gain, in_bias, w_in, out_gain, out_bias, w_out, cotangent):
    pair2 = pair.reshape(CELLS, H)
    cot2 = cotangent.reshape(CELLS, H)
    line = lambda v: v.reshape(1, -1)
    dma = pltpu.SemaphoreType.DMA
    both_shape, one_shape, sum_shape = ((ND * n, LANES) for n in (BOTH, ONE, SUMS))
    gates = [vm(A, H, LANES, dtype=BF16)] * 2

    send, normed, dproj, spread, w_out_near = call(
        project_kernel,
        [mask, pair2, line(in_gain), line(in_bias), w_in, cot2, line(out_gain), w_out],
        [(both_shape, BF16), ((CELLS, H), BF16), ((CELLS, H), BF16), ((H, LANES), F32),
         ((H, H), BF16)],
        [pltpu.SMEM((N,), jnp.int32), vm(CELLS, H, dtype=BF16), vm(1, H), vm(1, H),
         vm(H, 5 * H, dtype=BF16), vm(CELLS, H, dtype=BF16), vm(1, H), vm(8, H, LANES),
         vm(*both_shape), dma((8,))],
        500_000_000, hbm_in=range(8),
    )
    recv = exchange(send, 9, 2)
    send, left, right = call(
        mix_kernel,
        [recv],
        [(one_shape, BF16), ((N, 512), BF16), ((512, 512), BF16)],
        [vm(*both_shape), vm(512, LANES), vm(4 * N, LANES), vm(*one_shape)],
        400_000_000,
    )
    mixed = exchange(send, 5, 2)
    (send,) = call(
        d_mixed_kernel,
        [mixed, dproj, w_out_near, spread],
        [(one_shape, BF16)],
        [vm(*one_shape)],
        50_000_000,
    )
    recv = exchange(send, 5, 2)
    update, d_og, grads, pg, pvg = call(
        update_kernel,
        [mask, mixed, w_out_near, line(out_gain), line(out_bias), dproj, cot2, normed, w_in],
        [((CELLS, H), BF16), ((CELLS, H), BF16), ((2, H, H), BF16),
         ((A, H, LANES), BF16), ((A, H, LANES), BF16)],
        [vm(*one_shape), *gates, dma((2,))],
        600_000_000, smem_in=(0,), hbm_out=(3, 4),
    )
    send, pg_near, pvg_near = call(
        back_kernel,
        [recv, left, right, pg, pvg],
        [(both_shape, BF16), ((A, H, LANES), BF16), ((A, H, LANES), BF16)],
        [vm(*one_shape), vm(4 * N, LANES), vm(N, 512), vm(4 * 512, LANES), vm(*both_shape),
         dma((2,))],
        800_000_000, hbm_in=(3, 4),
    )
    recv = exchange(send, 9, 2)
    (send,) = call(
        grad_kernel,
        [recv, pg_near, pvg_near, normed, grads],
        [(sum_shape, BF16)],
        [vm(*both_shape), vm(*sum_shape)],
        400_000_000,
    )
    parts = exchange(send, 3, 2)
    (pair_grad,) = call(
        pair_grad_kernel,
        [recv, pg, pvg, d_og, pair2, line(in_gain), w_in],
        [((CELLS, H), BF16)],
        [vm(*both_shape), *gates, dma((2,))],
        400_000_000, hbm_in=(1, 2),
    )
    (send,) = call(sum_kernel, [parts], [(sum_shape, BF16)], [], 1_000_000)
    sums = exchange(send, 3, 2)
    w_in_grad, w_out_grad = call(
        unpack_kernel,
        [sums],
        [((H, 5 * H), F32), ((H, H), F32)],
        [vm(*sum_shape)],
        1_000_000,
    )
    return (update.reshape(A, B, H), pair_grad.reshape(A, B, H), w_in_grad, w_out_grad)


def solution(mesh):
    placed = (P("row", "col", None), P(), P(), P(), P(), P(), P(), P(), P("row", "col", None))
    return jax.shard_map(
        on_device,
        mesh=mesh,
        in_specs=placed,
        out_specs=(P("row", "col", None), P("row", "col", None), P(), P()),
        check_vma=False,
    )
```

```python
import math

import jax
import jax.numpy as jnp
from jax import lax
from jax.experimental import pallas as pl
from jax.experimental.pallas import tpu as pltpu
from jax.sharding import PartitionSpec as P

F32 = jnp.float32
BF16 = jnp.bfloat16
EPS = 1e-05
AXES = ("row", "col")

A, B, HALF, LANES = 24, 48, 64, 128
NR, NC, ND = 16, 8, 128
CELLS = A * B
H = 128
N = NR * A
BOTH, ONE, SUMS = 18, 10, 6

NT = ((1,), (1,))
TN = ((0,), (0,))
NN = ((1,), (0,))
VMEM_SPEC = pl.BlockSpec(memory_space=pltpu.VMEM)
HBM_SPEC = pl.BlockSpec(memory_space=pltpu.HBM)


def dot(x, y, contract):
    return lax.dot_general(x, y, (contract, ((), ())), preferred_element_type=F32)


def roll(x, shift):
    return pltpu.roll(x, shift % LANES, x.ndim - 1)


def lane_of(shape):
    return lax.broadcasted_iota(jnp.int32, shape, len(shape) - 1)


def two_sided(x):
    none = jnp.zeros_like(x)
    rest = jnp.zeros((LANES - 2 * B, 2 * x.shape[1]), x.dtype)
    return jnp.concatenate(
        [jnp.concatenate([x, none], 1), jnp.concatenate([none, x], 1), rest], 0
    )


def pieces(q):
    if q == 8:
        return [((16 + n) * B + 32, 16 * n, 16) for n in range(8)]
    return [(q * B, 0, B), ((8 + q) * B, B, B), ((16 + q) * B, 2 * B, 32)]


def row_cells(ref, q):
    return jnp.concatenate([ref[at : at + size, :] for at, _, size in pieces(q)], 0)


def column(row):
    at = lax.broadcasted_iota(jnp.int32, (H, LANES), 0)
    return jnp.sum(jnp.where(at == lane_of((H, LANES)), row, 0.0), 1, keepdims=True)


def stacked_weights(w_ref):
    part = [w_ref[:, p * H : (p + 1) * H].astype(F32).T.astype(BF16) for p in range(4)]
    return jnp.concatenate(
        [jnp.concatenate([part[0], part[2]], 1), jnp.concatenate([part[1], part[3]], 1)], 0
    )


def column_mask(mask_s):
    start = lax.axis_index("col") * B
    lane = lane_of((8, LANES))
    place = jnp.where(lane < B, lane, lane - B)
    out = jnp.zeros((8, LANES), F32)
    for b in range(B):
        out = jnp.where(place == b, mask_s[start + b].astype(F32), out)
    return out[0:1, :]


def gate_parts(weights, normed, pair_at, col_mask, mask_s):
    cells = jnp.concatenate([two_sided(normed[:B]), two_sided(normed[B:])], 0)
    pre = dot(weights, cells, NT)
    start = lax.axis_index("row") * A
    for k in range(2):
        value = pre[:H, k * LANES : (k + 1) * LANES]
        gate = jax.nn.sigmoid(pre[H:, k * LANES : (k + 1) * LANES])
        seen = col_mask * mask_s[start + 2 * pair_at + k].astype(F32)
        yield value, gate, gate * seen


def pack_both(block, third, a):
    shift = LANES - 32 if a < 8 else HALF
    return jnp.where(lane_of(block.shape) < 2 * B, block, roll(third, shift))


def pack_tail(third, n):
    lane = lane_of((H, LANES))
    out = roll(third[4 * n], -HALF)
    for m in range(1, 4):
        out = jnp.where(lane >= 32 * m, roll(third[4 * n + m], 32 * m - HALF), out)
    return out


def unpack_third(block, s):
    first, second, last = block(s), block(8 + s), block(16 + s // 4)
    lane = lane_of(first.shape)
    return jnp.where(
        lane < 32, roll(first, 32),
        jnp.where(lane < HALF, roll(second, HALF), roll(last, HALF - 32 * (s % 4))),
    )


def norm_rows(x):
    center = x - jnp.mean(x, 1, keepdims=True)
    scale = lax.rsqrt(jnp.mean(center * center, 1, keepdims=True) + EPS)
    return center * scale, scale


def norm_cells(x):
    center = x - jnp.mean(x, 0, keepdims=True)
    scale = lax.rsqrt(jnp.mean(center * center, 0, keepdims=True) + EPS)
    return center * scale, scale


def project_kernel(mask_h, pair_h, gain_h, bias_h, w_h, cot_h, out_gain_h, w_out_h,
                   send_ref, normed_ref, dproj_ref, spread_ref, w_out_ref,
                   mask_s, pair_v, gain_v, bias_v, w_v, cot_v, out_gain_v, third, scratch, sems):
    copies = [
        pltpu.make_async_copy(src, dst, sems.at[n])
        for n, (src, dst) in enumerate([
            (w_h, w_v), (pair_h, pair_v), (mask_h, mask_s), (gain_h, gain_v), (bias_h, bias_v),
            (cot_h, cot_v), (out_gain_h, out_gain_v), (w_out_h, w_out_ref),
        ])
    ]
    for copy in copies:
        copy.start()
    copies[0].wait()
    weights = stacked_weights(w_v)
    w_og = w_v[:, 4 * H :]
    for copy in copies[1:5]:
        copy.wait()
    col_mask = column_mask(mask_s)
    gain, bias = gain_v[...], bias_v[...]
    for pair_at in (8, 9, 10, 11, 0, 1, 2, 3, 4, 5, 6, 7):
        rows = pl.ds(pair_at * 2 * B, 2 * B)
        normal, _ = norm_rows(pair_v[rows, :].astype(F32))
        normed = (normal * gain + bias).astype(BF16)
        normed_ref[rows, :] = normed
        for k, (value, _, pg) in enumerate(gate_parts(weights, normed, pair_at, col_mask, mask_s)):
            a = pair_at * 2 + k
            if a >= 16:
                third[a - 16] = pg * value
            else:
                scratch[pl.ds(a, H, stride=BOTH), :] = pack_both(pg * value, third[a % 8], a)
        if pair_at == 11:
            for n in range(2):
                scratch[pl.ds(16 + n, H, stride=BOTH), :] = pack_tail(third, n)
    send_ref[...] = scratch[...].astype(BF16)
    for copy in copies[5:]:
        copy.wait()
    spread_ref[...] = jnp.broadcast_to(column(out_gain_v[...]), (H, LANES))
    for n in range(6):
        rows = pl.ds(n * CELLS // 6, CELLS // 6)
        sig = jax.nn.sigmoid(dot(normed_ref[rows, :], w_og, NN))
        dproj_ref[rows, :] = (cot_v[rows, :].astype(F32) * sig).astype(BF16)


def pick(lane, *parts):
    out = parts[-1]
    for n in range(len(parts) - 3, -1, -2):
        out = jnp.where(lane < parts[n + 1], parts[n], out)
    return out


def mix_kernel(recv_ref, send_ref, left_ref, right_ref, scratch, third, mixed, out):
    scratch[...] = recv_ref[...].astype(F32)
    lane, wide = lane_of((8, LANES)), lane_of((NR, LANES))
    for p in range(NC // 2):
        for n in range(8):
            x, y = (
                scratch[pl.ds(c * BOTH + 16 + n // 4, NR, stride=NC * BOTH), :]
                for c in (2 * p, 2 * p + 1)
            )
            shift = -32 * (n % 4)
            third[pl.ds(p * LANES + n, NR, stride=8), :] = jnp.where(
                wide < HALF, roll(x, shift + 16), roll(y, shift + 80)
            )
    for r2 in range(NR // 2):
        right_ref[r2 * HALF + B : (r2 + 1) * HALF, :] = jnp.zeros((HALF - B, 512), BF16)
        for p in range(NC // 2):
            lefts, rights = [], []
            for r in (2 * r2, 2 * r2 + 1):
                start = (r * NC + 2 * p) * BOTH
                x, y = scratch[pl.ds(start, 16), :], scratch[pl.ds(start + BOTH, 16), :]
                tail = third[p * LANES + r * 8 : p * LANES + r * 8 + 8, :]
                lefts += [
                    jnp.where(wide < HALF, x, roll(y, HALF)),
                    pick(lane, roll(x[:8], 32), 32, roll(x[8:], HALF), HALF, roll(y[:8], 96), 96, y[8:]),
                ]
                rights += [
                    pick(wide, roll(x, -B), B, 0.0, HALF, roll(y, HALF - B), HALF + B, 0.0),
                    pick(lane, roll(x[8:], 16), 16, tail, B, 0.0, HALF,
                         roll(y[8:], 80), 80, tail, HALF + B, 0.0),
                ]
            lanes = slice(p * LANES, (p + 1) * LANES)
            left_ref[r2 * B : (r2 + 1) * B, lanes] = jnp.concatenate(lefts, 0).astype(BF16)
            right_ref[r2 * HALF : r2 * HALF + B, lanes] = jnp.concatenate(rights, 0).astype(BF16)
    product = dot(left_ref[...], right_ref[...], NT)
    for p in range(NC // 2):
        mixed[p * N : (p + 1) * N, :] = product[:, p * LANES : (p + 1) * LANES]
    for r in range(NR):
        for p in range(NC // 2):
            t0, t1, t2 = (
                mixed[p * N + r * A + 8 * t : p * N + r * A + 8 * t + 8, :] for t in range(3)
            )
            start = (r * NC + 2 * p) * ONE
            out[pl.ds(start, 8), :] = pick(lane, t0, B, roll(t1, B), 2 * B, roll(t2, 96))
            out[pl.ds(start + ONE, 8), :] = pick(
                lane, roll(t0, HALF), B, roll(t1, -16), 2 * B, roll(t2, 32)
            )
    out[pl.ds(9, ND, stride=ONE), :] = jnp.zeros((ND, LANES), F32)
    group = wide >> 4
    for p in range(NC // 2):
        first = second = jnp.zeros((NR, LANES), F32)
        for n in range(8):
            t2 = mixed[pl.ds(p * N + 16 + n, NR, stride=A), :]
            first = jnp.where(group == n, roll(t2, 16 * n - 32), first)
            second = jnp.where(group == n, roll(t2, 16 * n - 96), second)
        out[pl.ds(2 * p * ONE + 8, NR, stride=NC * ONE), :] = first
        out[pl.ds((2 * p + 1) * ONE + 8, NR, stride=NC * ONE), :] = second
    send_ref[...] = out[...].astype(BF16)


def d_mixed_kernel(recv_ref, dproj_ref, w_out_ref, spread_ref, send_ref, scratch):
    scratch[...] = recv_ref[...].astype(F32)
    gain = spread_ref[...]
    w_out = w_out_ref[...]
    for q in range(9):
        wt = dot(w_out, row_cells(dproj_ref, q), NT) * gain
        normal, scale = norm_cells(scratch[pl.ds(q, H, stride=ONE), :])
        scratch[pl.ds(q, H, stride=ONE), :] = scale * (
            wt - jnp.mean(wt, 0, keepdims=True) - normal * jnp.mean(wt * normal, 0, keepdims=True)
        )
    send_ref[...] = scratch[...].astype(BF16)


def update_kernel(mask_s, recv_ref, w_out_ref, gain_ref, bias_ref, dproj_ref, cot_ref,
                  normed_ref, w_ref, update_ref, grads_ref, pg_v, pvg_v, d_og_h, pg_h, pvg_h,
                  scratch, d_og_ref, sems):
    weights = stacked_weights(w_ref)
    col_mask = column_mask(mask_s)
    for pair_at in range(A // 2):
        normed = normed_ref[pl.ds(pair_at * 2 * B, 2 * B), :]
        for k, (value, gate, pg) in enumerate(gate_parts(weights, normed, pair_at, col_mask, mask_s)):
            pg_v[2 * pair_at + k] = pg.astype(BF16)
            pvg_v[2 * pair_at + k] = (pg * value * (1.0 - gate)).astype(BF16)
    copies = [pltpu.make_async_copy(pg_v, pg_h, sems.at[0]),
              pltpu.make_async_copy(pvg_v, pvg_h, sems.at[1])]
    for copy in copies:
        copy.start()
    scratch[...] = recv_ref[...].astype(F32)
    gain, bias = column(gain_ref[...]), column(bias_ref[...])
    w_out, w_og = w_out_ref[...], w_ref[:, 4 * H :]
    grad = jnp.zeros((H, H), F32)
    for q in range(9):
        normal, _ = norm_cells(scratch[pl.ds(q, H, stride=ONE), :])
        out_normed = (normal * gain + bias).astype(BF16)
        projected = dot(out_normed, w_out, TN)
        grad = grad + dot(out_normed, row_cells(dproj_ref, q), NN)
        gates = jax.nn.sigmoid(dot(row_cells(normed_ref, q), w_og, NN))
        for at, lane, size in pieces(q):
            rows = pl.ds(at, size)
            sig, proj = gates[lane : lane + size], projected[lane : lane + size]
            update_ref[rows, :] = (sig * proj).astype(BF16)
            d_og_ref[rows, :] = (
                cot_ref[rows, :].astype(F32) * proj * sig * (1.0 - sig)
            ).astype(BF16)
    copies.append(pltpu.make_async_copy(d_og_ref, d_og_h, sems.at[2]))
    copies[2].start()
    grads_ref[0] = dot(d_og_ref[...], normed_ref[...], TN).astype(BF16)
    grads_ref[1] = grad.astype(BF16)
    for copy in copies:
        copy.wait()


def back_kernel(recv_ref, left_ref, right_ref, send_ref, scratch, d_tile, d_left, d_right, out):
    scratch[...] = recv_ref[...].astype(F32)
    lane, wide = lane_of((8, LANES)), lane_of((NR, LANES))
    for p in range(NC // 2):
        x, y = (
            scratch[pl.ds(c * ONE + 8, NR, stride=NC * ONE), :] for c in (2 * p, 2 * p + 1)
        )
        for n in range(8):
            d_tile[pl.ds(p * N + 16 + n, NR, stride=A), :] = jnp.where(
                wide < HALF, roll(x, 32 - 16 * n), roll(y, 96 - 16 * n)
            )
    for r in range(NR):
        for p in range(NC // 2):
            start = (r * NC + 2 * p) * ONE
            x, y = scratch[pl.ds(start, 8), :], scratch[pl.ds(start + ONE, 8), :]
            at = p * N + r * A
            tail = d_tile[at + 16 : at + 24, :]
            d_tile[at : at + 8, :] = jnp.where(lane < HALF, x, roll(y, HALF))
            d_tile[at + 8 : at + 16, :] = jnp.where(lane < HALF, roll(x, -B), roll(y, 16))
            d_tile[at + 16 : at + 24, :] = pick(
                lane, roll(x, 32), 32, tail, HALF, roll(y, 96), 96, tail
            )
    d = jnp.concatenate([d_tile[p * N : (p + 1) * N, :].astype(BF16) for p in range(4)], 1)
    d_left[...] = dot(d, right_ref[...], NN)
    product = dot(d, left_ref[...], TN)
    for p in range(NC // 2):
        d_right[p * 512 : (p + 1) * 512, :] = product[:, p * LANES : (p + 1) * LANES]
    for r in range(NR):
        for p in range(NC // 2):
            lanes = slice(p * LANES, (p + 1) * LANES)
            at = p * 512 + (r // 2) * HALF + (r % 2) * A
            x0, x1, x2 = (d_left[r * A + 8 * t : r * A + 8 * t + 8, lanes] for t in range(3))
            y0, y1, y2 = (d_right[at + 8 * t : at + 8 * t + 8, :] for t in range(3))
            start = (r * NC + 2 * p) * BOTH
            out[pl.ds(start, 8), :] = pick(lane, x0, B, roll(y0, B), 2 * B, roll(x2, 96))
            out[pl.ds(start + 8, 8), :] = pick(
                lane, x1, B, roll(y1, B), 2 * B, roll(x2, HALF), 112, roll(y2, 112)
            )
            start = start + BOTH
            out[pl.ds(start, 8), :] = pick(lane, roll(x0, HALF), B, roll(y0, -16), 2 * B, roll(x2, 32))
            out[pl.ds(start + 8, 8), :] = pick(
                lane, roll(x1, HALF), B, roll(y1, -16), 2 * B, x2, 112, roll(y2, B)
            )
    group = lane >> 5
    for p in range(NC // 2):
        for odd in range(2):
            for half in range(2):
                first = second = jnp.zeros((8, LANES), F32)
                for m in range(4):
                    at = p * 512 + odd * A + 16 + 4 * half + m
                    y2 = d_right[pl.ds(at, 8, stride=HALF), :]
                    first = jnp.where(group == m, roll(y2, 32 * m - 16), first)
                    second = jnp.where(group == m, roll(y2, 32 * m - 80), second)
                start = (odd * NC + 2 * p) * BOTH + 16 + half
                out[pl.ds(start, 8, stride=2 * NC * BOTH), :] = first
                out[pl.ds(start + BOTH, 8, stride=2 * NC * BOTH), :] = second
    send_ref[...] = out[...].astype(BF16)


def gated(scratch, a, pg_v, pvg_v):
    block = lambda p: scratch[pl.ds(p, H, stride=BOTH), :]
    d = block(a) if a < 16 else unpack_third(block, a - 16)
    return jnp.concatenate([d * pg_v[a].astype(F32), d * pvg_v[a].astype(F32)], 0).astype(BF16)


def grad_kernel(recv_ref, pg_v, pvg_v, normed_ref, grads_ref, send_ref, scratch, packed):
    scratch[...] = recv_ref[...].astype(F32)
    for g in range(2):
        packed[pl.ds(4 + g, H, stride=SUMS), :] = grads_ref[g].astype(F32)
    total = jnp.zeros((2 * H, 2 * H), F32)
    for pair_at in range(A // 2):
        a = 2 * pair_at
        sides = [gated(scratch, a + k, pg_v, pvg_v) for k in range(2)]
        cells = [two_sided(normed_ref[(a + k) * B : (a + k + 1) * B, :]) for k in range(2)]
        total = total + dot(jnp.concatenate(sides, 1), jnp.concatenate(cells, 0), NN)
    for g, block in enumerate([total[:H, :H], total[H:, :H], total[:H, H:], total[H:, H:]]):
        packed[pl.ds(g, H, stride=SUMS), :] = block
    send_ref[...] = packed[...].astype(BF16)


def pair_grad_kernel(recv_ref, pg_h, pvg_h, d_og_h, pair_ref, gain_ref, w_ref,
                     out_ref, scratch, pg_v, pvg_v, d_og_ref, sems):
    copies = [
        pltpu.make_async_copy(src, dst, sems.at[n])
        for n, (src, dst) in enumerate([(pg_h, pg_v), (pvg_h, pvg_v), (d_og_h, d_og_ref)])
    ]
    for copy in copies:
        copy.start()
    scratch[...] = recv_ref[...].astype(F32)
    weights = stacked_weights(w_ref)
    w_og = w_ref[:, 4 * H :]
    gain = gain_ref[...]
    for copy in copies:
        copy.wait()
    for a in range(A):
        rows = pl.ds(a * B, B)
        both = dot(gated(scratch, a, pg_v, pvg_v), weights, TN)
        d = both[:B, :H] + both[B : 2 * B, H:] + dot(d_og_ref[rows, :], w_og, NT)
        normal, scale = norm_rows(pair_ref[rows, :].astype(F32))
        weighted = d * gain
        out_ref[rows, :] = (
            scale * (weighted - jnp.mean(weighted, 1, keepdims=True)
                     - normal * jnp.mean(weighted * normal, 1, keepdims=True))
        ).astype(BF16)


def sum_kernel(recv_ref, send_ref):
    parts = jnp.sum(recv_ref[...].astype(F32).reshape(16, 8 * SUMS, LANES), 0)
    total = parts[:SUMS]
    for k in range(1, 8):
        total = total + parts[k * SUMS : (k + 1) * SUMS]
    many = jnp.concatenate([total] * 8, 0).astype(BF16)
    for s in range(16):
        send_ref[s * 8 * SUMS : (s + 1) * 8 * SUMS, :] = many


def unpack_kernel(recv_ref, w_in_ref, w_out_ref, scratch):
    scratch[...] = recv_ref[...].astype(F32)
    for g in range(5):
        w_in_ref[:, g * H : (g + 1) * H] = scratch[pl.ds(g, H, stride=SUMS), :].T
    w_out_ref[...] = scratch[pl.ds(5, H, stride=SUMS), :]


def call(kernel, args, outs, scratch, flops, hbm_in=(), smem_in=(), hbm_out=()):
    shapes = [
        pltpu.HBM(s, d) if n in hbm_out else jax.ShapeDtypeStruct(s, d)
        for n, (s, d) in enumerate(outs)
    ]
    args = [
        pltpu.with_memory_space_constraint(v, pltpu.HBM) if n in hbm_in else v
        for n, v in enumerate(args)
    ]
    specs = [
        HBM_SPEC if n in hbm_in else pl.BlockSpec(memory_space=pltpu.SMEM) if n in smem_in else VMEM_SPEC
        for n in range(len(args))
    ]
    moved = 2 * (sum(v.size for v in args) + sum(math.prod(s) for s, _ in outs))
    return pl.pallas_call(
        kernel,
        out_shape=shapes,
        in_specs=specs,
        out_specs=[HBM_SPEC if n in hbm_out else VMEM_SPEC for n in range(len(shapes))],
        scratch_shapes=scratch,
        cost_estimate=pl.CostEstimate(flops=flops, bytes_accessed=moved, transcendentals=0),
        compiler_params=pltpu.CompilerParams(vmem_limit_bytes=40 * 2**20),
    )(*args)


def vm(*shape, dtype=F32):
    return pltpu.VMEM(shape, dtype)


def exchange(x, *tile):
    moved = lax.all_to_all(x.reshape(ND, *tile, LANES), AXES, 0, 0, tiled=True)
    return moved.reshape(x.shape)


def on_device(pair, mask, in_gain, in_bias, w_in, out_gain, out_bias, w_out, cotangent):
    pair2 = pair.reshape(CELLS, H)
    cot2 = cotangent.reshape(CELLS, H)
    line = lambda v: v.reshape(1, -1)
    dma = pltpu.SemaphoreType.DMA
    both_shape, one_shape, sum_shape = ((ND * n, LANES) for n in (BOTH, ONE, SUMS))
    gates = [vm(A, H, LANES, dtype=BF16)] * 2

    send, normed, dproj, spread, w_out_near = call(
        project_kernel,
        [mask, pair2, line(in_gain), line(in_bias), w_in, cot2, line(out_gain), w_out],
        [(both_shape, BF16), ((CELLS, H), BF16), ((CELLS, H), BF16), ((H, LANES), F32),
         ((H, H), BF16)],
        [pltpu.SMEM((N,), jnp.int32), vm(CELLS, H, dtype=BF16), vm(1, H), vm(1, H),
         vm(H, 5 * H, dtype=BF16), vm(CELLS, H, dtype=BF16), vm(1, H), vm(8, H, LANES),
         vm(*both_shape), dma((8,))],
        500_000_000, hbm_in=range(8),
    )
    recv = exchange(send, 9, 2)
    send, left, right = call(
        mix_kernel,
        [recv],
        [(one_shape, BF16), ((N, 512), BF16), ((512, 512), BF16)],
        [vm(*both_shape), vm(512, LANES), vm(4 * N, LANES), vm(*one_shape)],
        400_000_000,
    )
    mixed = exchange(send, 5, 2)
    (send,) = call(
        d_mixed_kernel,
        [mixed, dproj, w_out_near, spread],
        [(one_shape, BF16)],
        [vm(*one_shape)],
        50_000_000,
    )
    recv = exchange(send, 5, 2)
    update, grads, pg_near, pvg_near, d_og, pg, pvg = call(
        update_kernel,
        [mask, mixed, w_out_near, line(out_gain), line(out_bias), dproj, cot2, normed, w_in],
        [((CELLS, H), BF16), ((2, H, H), BF16), ((A, H, LANES), BF16), ((A, H, LANES), BF16),
         ((CELLS, H), BF16), ((A, H, LANES), BF16), ((A, H, LANES), BF16)],
        [vm(*one_shape), vm(CELLS, H, dtype=BF16), dma((3,))],
        600_000_000, smem_in=(0,), hbm_out=(4, 5, 6),
    )
    (send,) = call(
        back_kernel,
        [recv, left, right],
        [(both_shape, BF16)],
        [vm(*one_shape), vm(4 * N, LANES), vm(N, 512), vm(4 * 512, LANES), vm(*both_shape)],
        800_000_000,
    )
    recv = exchange(send, 9, 2)
    (send,) = call(
        grad_kernel,
        [recv, pg_near, pvg_near, normed, grads],
        [(sum_shape, BF16)],
        [vm(*both_shape), vm(*sum_shape)],
        400_000_000,
    )
    parts = exchange(send, 3, 2)
    (pair_grad,) = call(
        pair_grad_kernel,
        [recv, pg, pvg, d_og, pair2, line(in_gain), w_in],
        [((CELLS, H), BF16)],
        [vm(*both_shape), *gates, vm(CELLS, H, dtype=BF16), dma((3,))],
        400_000_000, hbm_in=(1, 2, 3),
    )
    (send,) = call(sum_kernel, [parts], [(sum_shape, BF16)], [], 1_000_000)
    sums = exchange(send, 3, 2)
    w_in_grad, w_out_grad = call(
        unpack_kernel,
        [sums],
        [((H, 5 * H), F32), ((H, H), F32)],
        [vm(*sum_shape)],
        1_000_000,
    )
    return (update.reshape(A, B, H), pair_grad.reshape(A, B, H), w_in_grad, w_out_grad)


def solution(mesh):
    placed = (P("row", "col", None), P(), P(), P(), P(), P(), P(), P(), P("row", "col", None))
    return jax.shard_map(
        on_device,
        mesh=mesh,
        in_specs=placed,
        out_specs=(P("row", "col", None), P("row", "col", None), P(), P()),
        check_vma=False,
    )
```

```python
import math

import jax
import jax.numpy as jnp
from jax import lax
from jax.experimental import pallas as pl
from jax.experimental.pallas import tpu as pltpu
from jax.sharding import PartitionSpec as P

F32 = jnp.float32
BF16 = jnp.bfloat16
EPS = 1e-05
AXES = ("row", "col")

A, B, HALF, LANES = 24, 48, 64, 128
NR, NC, ND = 16, 8, 128
CELLS = A * B
H = 128
N = NR * A
BOTH, ONE, SUMS = 18, 10, 6

NT = ((1,), (1,))
TN = ((0,), (0,))
NN = ((1,), (0,))
VMEM_SPEC = pl.BlockSpec(memory_space=pltpu.VMEM)
HBM_SPEC = pl.BlockSpec(memory_space=pltpu.HBM)


def dot(x, y, contract):
    return lax.dot_general(x, y, (contract, ((), ())), preferred_element_type=F32)


def roll(x, shift):
    return pltpu.roll(x, shift % LANES, x.ndim - 1)


def lane_of(shape):
    return lax.broadcasted_iota(jnp.int32, shape, len(shape) - 1)


def two_sided(x):
    none = jnp.zeros_like(x)
    rest = jnp.zeros((LANES - 2 * B, 2 * x.shape[1]), x.dtype)
    return jnp.concatenate(
        [jnp.concatenate([x, none], 1), jnp.concatenate([none, x], 1), rest], 0
    )


def pieces(q):
    if q == 8:
        return [((16 + n) * B + 32, 16 * n, 16) for n in range(8)]
    return [(q * B, 0, B), ((8 + q) * B, B, B), ((16 + q) * B, 2 * B, 32)]


def row_cells(ref, q):
    return jnp.concatenate([ref[at : at + size, :] for at, _, size in pieces(q)], 0)


def column(row):
    at = lax.broadcasted_iota(jnp.int32, (H, LANES), 0)
    return jnp.sum(jnp.where(at == lane_of((H, LANES)), row, 0.0), 1, keepdims=True)


def stacked_weights(w_ref):
    part = [w_ref[:, p * H : (p + 1) * H].astype(F32).T.astype(BF16) for p in range(4)]
    return jnp.concatenate(
        [jnp.concatenate([part[0], part[2]], 1), jnp.concatenate([part[1], part[3]], 1)], 0
    )


def column_mask(mask_s):
    start = lax.axis_index("col") * B
    lane = lane_of((8, LANES))
    place = jnp.where(lane < B, lane, lane - B)
    out = jnp.zeros((8, LANES), F32)
    for b in range(B):
        out = jnp.where(place == b, mask_s[start + b].astype(F32), out)
    return out[0:1, :]


def gate_parts(weights, normed, pair_at, col_mask, mask_s):
    cells = jnp.concatenate([two_sided(normed[:B]), two_sided(normed[B:])], 0)
    pre = dot(weights, cells, NT)
    start = lax.axis_index("row") * A
    for k in range(2):
        value = pre[:H, k * LANES : (k + 1) * LANES]
        gate = jax.nn.sigmoid(pre[H:, k * LANES : (k + 1) * LANES])
        seen = col_mask * mask_s[start + 2 * pair_at + k].astype(F32)
        yield value, gate, gate * seen


def pack_both(block, third, a):
    shift = LANES - 32 if a < 8 else HALF
    return jnp.where(lane_of(block.shape) < 2 * B, block, roll(third, shift))


def pack_tail(third, n):
    lane = lane_of((H, LANES))
    out = roll(third[4 * n], -HALF)
    for m in range(1, 4):
        out = jnp.where(lane >= 32 * m, roll(third[4 * n + m], 32 * m - HALF), out)
    return out


def unpack_third(block, s):
    first, second, last = block(s), block(8 + s), block(16 + s // 4)
    lane = lane_of(first.shape)
    return jnp.where(
        lane < 32, roll(first, 32),
        jnp.where(lane < HALF, roll(second, HALF), roll(last, HALF - 32 * (s % 4))),
    )


def norm_rows(x):
    center = x - jnp.mean(x, 1, keepdims=True)
    scale = lax.rsqrt(jnp.mean(center * center, 1, keepdims=True) + EPS)
    return center * scale, scale


def norm_cells(x):
    center = x - jnp.mean(x, 0, keepdims=True)
    scale = lax.rsqrt(jnp.mean(center * center, 0, keepdims=True) + EPS)
    return center * scale, scale


def project_kernel(mask_h, pair_h, gain_h, bias_h, w_h, cot_h, out_gain_h, w_out_h,
                   send_ref, normed_ref, dproj_ref, spread_ref, w_out_ref,
                   mask_s, pair_v, gain_v, bias_v, w_v, cot_v, out_gain_v, third, scratch, sems):
    copies = [
        pltpu.make_async_copy(src, dst, sems.at[n])
        for n, (src, dst) in enumerate([
            (w_h, w_v), (pair_h, pair_v), (mask_h, mask_s), (gain_h, gain_v), (bias_h, bias_v),
            (cot_h, cot_v), (out_gain_h, out_gain_v), (w_out_h, w_out_ref),
        ])
    ]
    for copy in copies:
        copy.start()
    copies[0].wait()
    weights = stacked_weights(w_v)
    w_og = w_v[:, 4 * H :]
    for copy in copies[1:5]:
        copy.wait()
    col_mask = column_mask(mask_s)
    gain, bias = gain_v[...], bias_v[...]
    for pair_at in (8, 9, 10, 11, 0, 1, 2, 3, 4, 5, 6, 7):
        rows = pl.ds(pair_at * 2 * B, 2 * B)
        normal, _ = norm_rows(pair_v[rows, :].astype(F32))
        normed = (normal * gain + bias).astype(BF16)
        normed_ref[rows, :] = normed
        for k, (value, _, pg) in enumerate(gate_parts(weights, normed, pair_at, col_mask, mask_s)):
            a = pair_at * 2 + k
            if a >= 16:
                third[a - 16] = pg * value
            else:
                scratch[pl.ds(a, H, stride=BOTH), :] = pack_both(pg * value, third[a % 8], a)
        if pair_at == 11:
            for n in range(2):
                scratch[pl.ds(16 + n, H, stride=BOTH), :] = pack_tail(third, n)
    send_ref[...] = scratch[...].astype(BF16)
    for copy in copies[5:]:
        copy.wait()
    spread_ref[...] = jnp.broadcast_to(column(out_gain_v[...]), (H, LANES))
    for n in range(6):
        rows = pl.ds(n * CELLS // 6, CELLS // 6)
        sig = jax.nn.sigmoid(dot(normed_ref[rows, :], w_og, NN))
        dproj_ref[rows, :] = (cot_v[rows, :].astype(F32) * sig).astype(BF16)


def pick(lane, *parts):
    out = parts[-1]
    for n in range(len(parts) - 3, -1, -2):
        out = jnp.where(lane < parts[n + 1], parts[n], out)
    return out


def mix_kernel(recv_ref, send_ref, left_ref, right_ref, scratch, third, mixed, out):
    scratch[...] = recv_ref[...].astype(F32)
    lane, wide = lane_of((8, LANES)), lane_of((NR, LANES))
    for p in range(NC // 2):
        for n in range(8):
            x, y = (
                scratch[pl.ds(c * BOTH + 16 + n // 4, NR, stride=NC * BOTH), :]
                for c in (2 * p, 2 * p + 1)
            )
            shift = -32 * (n % 4)
            third[pl.ds(p * LANES + n, NR, stride=8), :] = jnp.where(
                wide < HALF, roll(x, shift + 16), roll(y, shift + 80)
            )
    for r2 in range(NR // 2):
        right_ref[r2 * HALF + B : (r2 + 1) * HALF, :] = jnp.zeros((HALF - B, 512), BF16)
        for p in range(NC // 2):
            lefts, rights = [], []
            for r in (2 * r2, 2 * r2 + 1):
                start = (r * NC + 2 * p) * BOTH
                x, y = scratch[pl.ds(start, 16), :], scratch[pl.ds(start + BOTH, 16), :]
                tail = third[p * LANES + r * 8 : p * LANES + r * 8 + 8, :]
                lefts += [
                    jnp.where(wide < HALF, x, roll(y, HALF)),
                    pick(lane, roll(x[:8], 32), 32, roll(x[8:], HALF), HALF, roll(y[:8], 96), 96, y[8:]),
                ]
                rights += [
                    pick(wide, roll(x, -B), B, 0.0, HALF, roll(y, HALF - B), HALF + B, 0.0),
                    pick(lane, roll(x[8:], 16), 16, tail, B, 0.0, HALF,
                         roll(y[8:], 80), 80, tail, HALF + B, 0.0),
                ]
            lanes = slice(p * LANES, (p + 1) * LANES)
            left_ref[r2 * B : (r2 + 1) * B, lanes] = jnp.concatenate(lefts, 0).astype(BF16)
            right_ref[r2 * HALF : r2 * HALF + B, lanes] = jnp.concatenate(rights, 0).astype(BF16)
    product = dot(left_ref[...], right_ref[...], NT)
    for p in range(NC // 2):
        mixed[p * N : (p + 1) * N, :] = product[:, p * LANES : (p + 1) * LANES]
    for r in range(NR):
        for p in range(NC // 2):
            t0, t1, t2 = (
                mixed[p * N + r * A + 8 * t : p * N + r * A + 8 * t + 8, :] for t in range(3)
            )
            start = (r * NC + 2 * p) * ONE
            out[pl.ds(start, 8), :] = pick(lane, t0, B, roll(t1, B), 2 * B, roll(t2, 96))
            out[pl.ds(start + ONE, 8), :] = pick(
                lane, roll(t0, HALF), B, roll(t1, -16), 2 * B, roll(t2, 32)
            )
    out[pl.ds(9, ND, stride=ONE), :] = jnp.zeros((ND, LANES), F32)
    group = wide >> 4
    for p in range(NC // 2):
        first = second = jnp.zeros((NR, LANES), F32)
        for n in range(8):
            t2 = mixed[pl.ds(p * N + 16 + n, NR, stride=A), :]
            first = jnp.where(group == n, roll(t2, 16 * n - 32), first)
            second = jnp.where(group == n, roll(t2, 16 * n - 96), second)
        out[pl.ds(2 * p * ONE + 8, NR, stride=NC * ONE), :] = first
        out[pl.ds((2 * p + 1) * ONE + 8, NR, stride=NC * ONE), :] = second
    send_ref[...] = out[...].astype(BF16)


def d_mixed_kernel(recv_ref, dproj_ref, w_out_ref, spread_ref, send_ref, scratch):
    scratch[...] = recv_ref[...].astype(F32)
    gain = spread_ref[...]
    w_out = w_out_ref[...]
    for q in range(9):
        wt = dot(w_out, row_cells(dproj_ref, q), NT) * gain
        normal, scale = norm_cells(scratch[pl.ds(q, H, stride=ONE), :])
        scratch[pl.ds(q, H, stride=ONE), :] = scale * (
            wt - jnp.mean(wt, 0, keepdims=True) - normal * jnp.mean(wt * normal, 0, keepdims=True)
        )
    send_ref[...] = scratch[...].astype(BF16)


def update_kernel(mask_s, recv_ref, w_out_ref, gain_ref, bias_ref, dproj_ref, cot_ref,
                  normed_ref, w_ref, update_ref, d_og_ref, grads_ref, pg_h, pvg_h,
                  scratch, pg_v, pvg_v, sems):
    weights = stacked_weights(w_ref)
    col_mask = column_mask(mask_s)
    for pair_at in range(A // 2):
        normed = normed_ref[pl.ds(pair_at * 2 * B, 2 * B), :]
        for k, (value, gate, pg) in enumerate(gate_parts(weights, normed, pair_at, col_mask, mask_s)):
            pg_v[2 * pair_at + k] = pg.astype(BF16)
            pvg_v[2 * pair_at + k] = (pg * value * (1.0 - gate)).astype(BF16)
    copies = [pltpu.make_async_copy(pg_v, pg_h, sems.at[0]),
              pltpu.make_async_copy(pvg_v, pvg_h, sems.at[1])]
    for copy in copies:
        copy.start()
    scratch[...] = recv_ref[...].astype(F32)
    gain, bias = column(gain_ref[...]), column(bias_ref[...])
    w_out, w_og = w_out_ref[...], w_ref[:, 4 * H :]
    grad = jnp.zeros((H, H), F32)
    for q in range(9):
        normal, _ = norm_cells(scratch[pl.ds(q, H, stride=ONE), :])
        out_normed = (normal * gain + bias).astype(BF16)
        projected = dot(out_normed, w_out, TN)
        grad = grad + dot(out_normed, row_cells(dproj_ref, q), NN)
        gates = jax.nn.sigmoid(dot(row_cells(normed_ref, q), w_og, NN))
        for at, lane, size in pieces(q):
            rows = pl.ds(at, size)
            sig, proj = gates[lane : lane + size], projected[lane : lane + size]
            update_ref[rows, :] = (sig * proj).astype(BF16)
            d_og_ref[rows, :] = (
                cot_ref[rows, :].astype(F32) * proj * sig * (1.0 - sig)
            ).astype(BF16)
    grads_ref[0] = dot(d_og_ref[...], normed_ref[...], TN).astype(BF16)
    grads_ref[1] = grad.astype(BF16)
    for copy in copies:
        copy.wait()


def back_kernel(recv_ref, left_ref, right_ref, pg_h, pvg_h, send_ref, pg_ref, pvg_ref,
                scratch, d_tile, d_left, d_right, out, sems):
    copies = [
        pltpu.make_async_copy(src, dst, sems.at[n])
        for n, (src, dst) in enumerate(
            [(pg_h, pg_ref), (pvg_h, pvg_ref)]
        )
    ]
    for copy in copies:
        copy.start()
    scratch[...] = recv_ref[...].astype(F32)
    lane, wide = lane_of((8, LANES)), lane_of((NR, LANES))
    for p in range(NC // 2):
        x, y = (
            scratch[pl.ds(c * ONE + 8, NR, stride=NC * ONE), :] for c in (2 * p, 2 * p + 1)
        )
        for n in range(8):
            d_tile[pl.ds(p * N + 16 + n, NR, stride=A), :] = jnp.where(
                wide < HALF, roll(x, 32 - 16 * n), roll(y, 96 - 16 * n)
            )
    for r in range(NR):
        for p in range(NC // 2):
            start = (r * NC + 2 * p) * ONE
            x, y = scratch[pl.ds(start, 8), :], scratch[pl.ds(start + ONE, 8), :]
            at = p * N + r * A
            tail = d_tile[at + 16 : at + 24, :]
            d_tile[at : at + 8, :] = jnp.where(lane < HALF, x, roll(y, HALF))
            d_tile[at + 8 : at + 16, :] = jnp.where(lane < HALF, roll(x, -B), roll(y, 16))
            d_tile[at + 16 : at + 24, :] = pick(
                lane, roll(x, 32), 32, tail, HALF, roll(y, 96), 96, tail
            )
    d = jnp.concatenate([d_tile[p * N : (p + 1) * N, :].astype(BF16) for p in range(4)], 1)
    d_left[...] = dot(d, right_ref[...], NN)
    product = dot(d, left_ref[...], TN)
    for p in range(NC // 2):
        d_right[p * 512 : (p + 1) * 512, :] = product[:, p * LANES : (p + 1) * LANES]
    for r in range(NR):
        for p in range(NC // 2):
            lanes = slice(p * LANES, (p + 1) * LANES)
            at = p * 512 + (r // 2) * HALF + (r % 2) * A
            x0, x1, x2 = (d_left[r * A + 8 * t : r * A + 8 * t + 8, lanes] for t in range(3))
            y0, y1, y2 = (d_right[at + 8 * t : at + 8 * t + 8, :] for t in range(3))
            start = (r * NC + 2 * p) * BOTH
            out[pl.ds(start, 8), :] = pick(lane, x0, B, roll(y0, B), 2 * B, roll(x2, 96))
            out[pl.ds(start + 8, 8), :] = pick(
                lane, x1, B, roll(y1, B), 2 * B, roll(x2, HALF), 112, roll(y2, 112)
            )
            start = start + BOTH
            out[pl.ds(start, 8), :] = pick(lane, roll(x0, HALF), B, roll(y0, -16), 2 * B, roll(x2, 32))
            out[pl.ds(start + 8, 8), :] = pick(
                lane, roll(x1, HALF), B, roll(y1, -16), 2 * B, x2, 112, roll(y2, B)
            )
    group = lane >> 5
    for p in range(NC // 2):
        for odd in range(2):
            for half in range(2):
                first = second = jnp.zeros((8, LANES), F32)
                for m in range(4):
                    at = p * 512 + odd * A + 16 + 4 * half + m
                    y2 = d_right[pl.ds(at, 8, stride=HALF), :]
                    first = jnp.where(group == m, roll(y2, 32 * m - 16), first)
                    second = jnp.where(group == m, roll(y2, 32 * m - 80), second)
                start = (odd * NC + 2 * p) * BOTH + 16 + half
                out[pl.ds(start, 8, stride=2 * NC * BOTH), :] = first
                out[pl.ds(start + BOTH, 8, stride=2 * NC * BOTH), :] = second
    send_ref[...] = out[...].astype(BF16)
    for copy in copies:
        copy.wait()


def gated(scratch, a, pg_v, pvg_v):
    block = lambda p: scratch[pl.ds(p, H, stride=BOTH), :]
    d = block(a) if a < 16 else unpack_third(block, a - 16)
    return jnp.concatenate([d * pg_v[a].astype(F32), d * pvg_v[a].astype(F32)], 0).astype(BF16)


def grad_kernel(recv_ref, pg_v, pvg_v, normed_ref, grads_ref, send_ref, scratch, packed):
    scratch[...] = recv_ref[...].astype(F32)
    for g in range(2):
        packed[pl.ds(4 + g, H, stride=SUMS), :] = grads_ref[g].astype(F32)
    total = jnp.zeros((2 * H, 2 * H), F32)
    for pair_at in range(A // 2):
        a = 2 * pair_at
        sides = [gated(scratch, a + k, pg_v, pvg_v) for k in range(2)]
        cells = [two_sided(normed_ref[(a + k) * B : (a + k + 1) * B, :]) for k in range(2)]
        total = total + dot(jnp.concatenate(sides, 1), jnp.concatenate(cells, 0), NN)
    for g, block in enumerate([total[:H, :H], total[H:, :H], total[:H, H:], total[H:, H:]]):
        packed[pl.ds(g, H, stride=SUMS), :] = block
    send_ref[...] = packed[...].astype(BF16)


def pair_grad_kernel(recv_ref, pg_h, pvg_h, d_og_ref, pair_ref, gain_ref, w_ref,
                     out_ref, scratch, pg_v, pvg_v, sems):
    copies = [pltpu.make_async_copy(pg_h, pg_v, sems.at[0]),
              pltpu.make_async_copy(pvg_h, pvg_v, sems.at[1])]
    for copy in copies:
        copy.start()
    scratch[...] = recv_ref[...].astype(F32)
    weights = stacked_weights(w_ref)
    w_og = w_ref[:, 4 * H :]
    gain = gain_ref[...]
    for copy in copies:
        copy.wait()
    for a in range(A):
        rows = pl.ds(a * B, B)
        both = dot(gated(scratch, a, pg_v, pvg_v), weights, TN)
        d = both[:B, :H] + both[B : 2 * B, H:] + dot(d_og_ref[rows, :], w_og, NT)
        normal, scale = norm_rows(pair_ref[rows, :].astype(F32))
        weighted = d * gain
        out_ref[rows, :] = (
            scale * (weighted - jnp.mean(weighted, 1, keepdims=True)
                     - normal * jnp.mean(weighted * normal, 1, keepdims=True))
        ).astype(BF16)


def sum_kernel(recv_ref, send_ref):
    parts = jnp.sum(recv_ref[...].astype(F32).reshape(16, 8 * SUMS, LANES), 0)
    total = parts[:SUMS]
    for k in range(1, 8):
        total = total + parts[k * SUMS : (k + 1) * SUMS]
    many = jnp.concatenate([total] * 8, 0).astype(BF16)
    for s in range(16):
        send_ref[s * 8 * SUMS : (s + 1) * 8 * SUMS, :] = many


def unpack_kernel(recv_ref, w_in_ref, w_out_ref, scratch):
    scratch[...] = recv_ref[...].astype(F32)
    for g in range(5):
        w_in_ref[:, g * H : (g + 1) * H] = scratch[pl.ds(g, H, stride=SUMS), :].T
    w_out_ref[...] = scratch[pl.ds(5, H, stride=SUMS), :]


def call(kernel, args, outs, scratch, flops, hbm_in=(), smem_in=(), hbm_out=(),
         flags=None):
    shapes = [
        pltpu.HBM(s, d) if n in hbm_out else jax.ShapeDtypeStruct(s, d)
        for n, (s, d) in enumerate(outs)
    ]
    args = [
        pltpu.with_memory_space_constraint(v, pltpu.HBM) if n in hbm_in else v
        for n, v in enumerate(args)
    ]
    specs = [
        HBM_SPEC if n in hbm_in else pl.BlockSpec(memory_space=pltpu.SMEM) if n in smem_in else VMEM_SPEC
        for n in range(len(args))
    ]
    moved = 2 * (sum(v.size for v in args) + sum(math.prod(s) for s, _ in outs))
    return pl.pallas_call(
        kernel,
        out_shape=shapes,
        in_specs=specs,
        out_specs=[HBM_SPEC if n in hbm_out else VMEM_SPEC for n in range(len(shapes))],
        scratch_shapes=scratch,
        cost_estimate=pl.CostEstimate(flops=flops, bytes_accessed=moved, transcendentals=0),
        compiler_params=pltpu.CompilerParams(vmem_limit_bytes=40 * 2**20, flags=flags),
    )(*args)


def vm(*shape, dtype=F32):
    return pltpu.VMEM(shape, dtype)


def exchange(x, *tile):
    moved = lax.all_to_all(x.reshape(ND, *tile, LANES), AXES, 0, 0, tiled=True)
    return moved.reshape(x.shape)


def on_device(pair, mask, in_gain, in_bias, w_in, out_gain, out_bias, w_out, cotangent):
    pair2 = pair.reshape(CELLS, H)
    cot2 = cotangent.reshape(CELLS, H)
    line = lambda v: v.reshape(1, -1)
    dma = pltpu.SemaphoreType.DMA
    both_shape, one_shape, sum_shape = ((ND * n, LANES) for n in (BOTH, ONE, SUMS))
    gates = [vm(A, H, LANES, dtype=BF16)] * 2

    send, normed, dproj, spread, w_out_near = call(
        project_kernel,
        [mask, pair2, line(in_gain), line(in_bias), w_in, cot2, line(out_gain), w_out],
        [(both_shape, BF16), ((CELLS, H), BF16), ((CELLS, H), BF16), ((H, LANES), F32),
         ((H, H), BF16)],
        [pltpu.SMEM((N,), jnp.int32), vm(CELLS, H, dtype=BF16), vm(1, H), vm(1, H),
         vm(H, 5 * H, dtype=BF16), vm(CELLS, H, dtype=BF16), vm(1, H), vm(8, H, LANES),
         vm(*both_shape), dma((8,))],
        500_000_000, hbm_in=range(8),
    )
    recv = exchange(send, 9, 2)
    send, left, right = call(
        mix_kernel,
        [recv],
        [(one_shape, BF16), ((N, 512), BF16), ((512, 512), BF16)],
        [vm(*both_shape), vm(512, LANES), vm(4 * N, LANES), vm(*one_shape)],
        400_000_000,
    )
    mixed = exchange(send, 5, 2)
    (send,) = call(
        d_mixed_kernel,
        [mixed, dproj, w_out_near, spread],
        [(one_shape, BF16)],
        [vm(*one_shape)],
        50_000_000,
    )
    recv = exchange(send, 5, 2)
    update, d_og, grads, pg, pvg = call(
        update_kernel,
        [mask, mixed, w_out_near, line(out_gain), line(out_bias), dproj, cot2, normed, w_in],
        [((CELLS, H), BF16), ((CELLS, H), BF16), ((2, H, H), BF16),
         ((A, H, LANES), BF16), ((A, H, LANES), BF16)],
        [vm(*one_shape), *gates, dma((2,))],
        600_000_000, smem_in=(0,), hbm_out=(3, 4),
    )
    send, pg_near, pvg_near = call(
        back_kernel,
        [recv, left, right, pg, pvg],
        [(both_shape, BF16), ((A, H, LANES), BF16), ((A, H, LANES), BF16)],
        [vm(*one_shape), vm(4 * N, LANES), vm(N, 512), vm(4 * 512, LANES), vm(*both_shape),
         dma((2,))],
        800_000_000, hbm_in=(3, 4),
    )
    recv = exchange(send, 9, 2)
    (send,) = call(
        grad_kernel,
        [recv, pg_near, pvg_near, normed, grads],
        [(sum_shape, BF16)],
        [vm(*both_shape), vm(*sum_shape)],
        400_000_000,
    )
    parts = exchange(send, 3, 2)
    (pair_grad,) = call(
        pair_grad_kernel,
        [recv, pg, pvg, d_og, pair2, line(in_gain), w_in],
        [((CELLS, H), BF16)],
        [vm(*both_shape), *gates, dma((2,))],
        400_000_000, hbm_in=(1, 2),
    )
    (send,) = call(sum_kernel, [parts], [(sum_shape, BF16)], [], 1_000_000)
    sums = exchange(send, 3, 2)
    w_in_grad, w_out_grad = call(
        unpack_kernel,
        [sums],
        [((H, 5 * H), F32), ((H, H), F32)],
        [vm(*sum_shape)],
        1_000_000,
    )
    return (update.reshape(A, B, H), pair_grad.reshape(A, B, H), w_in_grad, w_out_grad)


def solution(mesh):
    placed = (P("row", "col", None), P(), P(), P(), P(), P(), P(), P(), P("row", "col", None))
    return jax.shard_map(
        on_device,
        mesh=mesh,
        in_specs=placed,
        out_specs=(P("row", "col", None), P("row", "col", None), P(), P()),
        check_vma=False,
    )
```

```python
import math

import jax
import jax.numpy as jnp
from jax import lax
from jax.experimental import pallas as pl
from jax.experimental.pallas import tpu as pltpu
from jax.sharding import PartitionSpec as P

F32 = jnp.float32
BF16 = jnp.bfloat16
EPS = 1e-05
AXES = ("row", "col")

A, B, HALF, LANES = 24, 48, 64, 128
NR, NC, ND = 16, 8, 128
CELLS = A * B
H = 128
N = NR * A
BOTH, ONE, SUMS = 18, 10, 6

NT = ((1,), (1,))
TN = ((0,), (0,))
NN = ((1,), (0,))
VMEM_SPEC = pl.BlockSpec(memory_space=pltpu.VMEM)
HBM_SPEC = pl.BlockSpec(memory_space=pltpu.HBM)


def dot(x, y, contract):
    return lax.dot_general(x, y, (contract, ((), ())), preferred_element_type=F32)


def roll(x, shift):
    return pltpu.roll(x, shift % LANES, x.ndim - 1)


def lane_of(shape):
    return lax.broadcasted_iota(jnp.int32, shape, len(shape) - 1)


def two_sided(x):
    none = jnp.zeros_like(x)
    rest = jnp.zeros((LANES - 2 * B, 2 * x.shape[1]), x.dtype)
    return jnp.concatenate(
        [jnp.concatenate([x, none], 1), jnp.concatenate([none, x], 1), rest], 0
    )


def pieces(q):
    if q == 8:
        return [((16 + n) * B + 32, 16 * n, 16) for n in range(8)]
    return [(q * B, 0, B), ((8 + q) * B, B, B), ((16 + q) * B, 2 * B, 32)]


def row_cells(ref, q):
    return jnp.concatenate([ref[at : at + size, :] for at, _, size in pieces(q)], 0)


def column(row):
    at = lax.broadcasted_iota(jnp.int32, (H, LANES), 0)
    return jnp.sum(jnp.where(at == lane_of((H, LANES)), row, 0.0), 1, keepdims=True)


def stacked_weights(w_ref):
    part = [w_ref[:, p * H : (p + 1) * H].astype(F32).T.astype(BF16) for p in range(4)]
    return jnp.concatenate(
        [jnp.concatenate([part[0], part[2]], 1), jnp.concatenate([part[1], part[3]], 1)], 0
    )


def column_mask(mask_s):
    start = lax.axis_index("col") * B
    lane = lane_of((8, LANES))
    place = jnp.where(lane < B, lane, lane - B)
    out = jnp.zeros((8, LANES), F32)
    for b in range(B):
        out = jnp.where(place == b, mask_s[start + b].astype(F32), out)
    return out[0:1, :]


def gate_parts(weights, normed, pair_at, col_mask, mask_s):
    cells = jnp.concatenate([two_sided(normed[:B]), two_sided(normed[B:])], 0)
    pre = dot(weights, cells, NT)
    start = lax.axis_index("row") * A
    for k in range(2):
        value = pre[:H, k * LANES : (k + 1) * LANES]
        gate = jax.nn.sigmoid(pre[H:, k * LANES : (k + 1) * LANES])
        seen = col_mask * mask_s[start + 2 * pair_at + k].astype(F32)
        yield value, gate, gate * seen


def pack_both(block, third, a):
    shift = LANES - 32 if a < 8 else HALF
    return jnp.where(lane_of(block.shape) < 2 * B, block, roll(third, shift))


def pack_tail(third, n):
    lane = lane_of((H, LANES))
    out = roll(third[4 * n], -HALF)
    for m in range(1, 4):
        out = jnp.where(lane >= 32 * m, roll(third[4 * n + m], 32 * m - HALF), out)
    return out


def unpack_third(block, s):
    first, second, last = block(s), block(8 + s), block(16 + s // 4)
    lane = lane_of(first.shape)
    return jnp.where(
        lane < 32, roll(first, 32),
        jnp.where(lane < HALF, roll(second, HALF), roll(last, HALF - 32 * (s % 4))),
    )


def norm_rows(x):
    center = x - jnp.mean(x, 1, keepdims=True)
    scale = lax.rsqrt(jnp.mean(center * center, 1, keepdims=True) + EPS)
    return center * scale, scale


def norm_cells(x):
    center = x - jnp.mean(x, 0, keepdims=True)
    scale = lax.rsqrt(jnp.mean(center * center, 0, keepdims=True) + EPS)
    return center * scale, scale


def project_kernel(mask_h, pair_h, gain_h, bias_h, w_h, cot_h, out_gain_h, w_out_h,
                   send_ref, normed_ref, dproj_ref, spread_ref, w_out_ref,
                   mask_s, pair_v, gain_v, bias_v, w_v, cot_v, out_gain_v, third, scratch, sems):
    copies = [
        pltpu.make_async_copy(src, dst, sems.at[n])
        for n, (src, dst) in enumerate([
            (w_h, w_v), (pair_h, pair_v), (mask_h, mask_s), (gain_h, gain_v), (bias_h, bias_v),
            (cot_h, cot_v), (out_gain_h, out_gain_v), (w_out_h, w_out_ref),
        ])
    ]
    for copy in [copies[1], copies[0]] + copies[2:]:
        copy.start()
    copies[0].wait()
    weights = stacked_weights(w_v)
    w_og = w_v[:, 4 * H :]
    for copy in copies[1:5]:
        copy.wait()
    col_mask = column_mask(mask_s)
    gain, bias = gain_v[...], bias_v[...]
    for pair_at in (8, 9, 10, 11, 0, 1, 2, 3, 4, 5, 6, 7):
        rows = pl.ds(pair_at * 2 * B, 2 * B)
        normal, _ = norm_rows(pair_v[rows, :].astype(F32))
        normed = (normal * gain + bias).astype(BF16)
        normed_ref[rows, :] = normed
        for k, (value, _, pg) in enumerate(gate_parts(weights, normed, pair_at, col_mask, mask_s)):
            a = pair_at * 2 + k
            if a >= 16:
                third[a - 16] = pg * value
            else:
                scratch[pl.ds(a, H, stride=BOTH), :] = pack_both(pg * value, third[a % 8], a)
        if pair_at == 11:
            for n in range(2):
                scratch[pl.ds(16 + n, H, stride=BOTH), :] = pack_tail(third, n)
    send_ref[...] = scratch[...].astype(BF16)
    for copy in copies[5:]:
        copy.wait()
    spread_ref[...] = jnp.broadcast_to(column(out_gain_v[...]), (H, LANES))
    for n in range(6):
        rows = pl.ds(n * CELLS // 6, CELLS // 6)
        sig = jax.nn.sigmoid(dot(normed_ref[rows, :], w_og, NN))
        dproj_ref[rows, :] = (cot_v[rows, :].astype(F32) * sig).astype(BF16)


def pick(lane, *parts):
    out = parts[-1]
    for n in range(len(parts) - 3, -1, -2):
        out = jnp.where(lane < parts[n + 1], parts[n], out)
    return out


def mix_kernel(recv_ref, send_ref, left_ref, right_ref, scratch, third, mixed, out):
    scratch[...] = recv_ref[...].astype(F32)
    lane, wide = lane_of((8, LANES)), lane_of((NR, LANES))
    for p in range(NC // 2):
        for n in range(8):
            x, y = (
                scratch[pl.ds(c * BOTH + 16 + n // 4, NR, stride=NC * BOTH), :]
                for c in (2 * p, 2 * p + 1)
            )
            shift = -32 * (n % 4)
            third[pl.ds(p * LANES + n, NR, stride=8), :] = jnp.where(
                wide < HALF, roll(x, shift + 16), roll(y, shift + 80)
            )
    for r2 in range(NR // 2):
        right_ref[r2 * HALF + B : (r2 + 1) * HALF, :] = jnp.zeros((HALF - B, 512), BF16)
        for p in range(NC // 2):
            lefts, rights = [], []
            for r in (2 * r2, 2 * r2 + 1):
                start = (r * NC + 2 * p) * BOTH
                x, y = scratch[pl.ds(start, 16), :], scratch[pl.ds(start + BOTH, 16), :]
                tail = third[p * LANES + r * 8 : p * LANES + r * 8 + 8, :]
                lefts += [
                    jnp.where(wide < HALF, x, roll(y, HALF)),
                    pick(lane, roll(x[:8], 32), 32, roll(x[8:], HALF), HALF, roll(y[:8], 96), 96, y[8:]),
                ]
                rights += [
                    pick(wide, roll(x, -B), B, 0.0, HALF, roll(y, HALF - B), HALF + B, 0.0),
                    pick(lane, roll(x[8:], 16), 16, tail, B, 0.0, HALF,
                         roll(y[8:], 80), 80, tail, HALF + B, 0.0),
                ]
            lanes = slice(p * LANES, (p + 1) * LANES)
            left_ref[r2 * B : (r2 + 1) * B, lanes] = jnp.concatenate(lefts, 0).astype(BF16)
            right_ref[r2 * HALF : r2 * HALF + B, lanes] = jnp.concatenate(rights, 0).astype(BF16)
    product = dot(left_ref[...], right_ref[...], NT)
    for p in range(NC // 2):
        mixed[p * N : (p + 1) * N, :] = product[:, p * LANES : (p + 1) * LANES]
    for r in range(NR):
        for p in range(NC // 2):
            t0, t1, t2 = (
                mixed[p * N + r * A + 8 * t : p * N + r * A + 8 * t + 8, :] for t in range(3)
            )
            start = (r * NC + 2 * p) * ONE
            out[pl.ds(start, 8), :] = pick(lane, t0, B, roll(t1, B), 2 * B, roll(t2, 96))
            out[pl.ds(start + ONE, 8), :] = pick(
                lane, roll(t0, HALF), B, roll(t1, -16), 2 * B, roll(t2, 32)
            )
    out[pl.ds(9, ND, stride=ONE), :] = jnp.zeros((ND, LANES), F32)
    group = wide >> 4
    for p in range(NC // 2):
        first = second = jnp.zeros((NR, LANES), F32)
        for n in range(8):
            t2 = mixed[pl.ds(p * N + 16 + n, NR, stride=A), :]
            first = jnp.where(group == n, roll(t2, 16 * n - 32), first)
            second = jnp.where(group == n, roll(t2, 16 * n - 96), second)
        out[pl.ds(2 * p * ONE + 8, NR, stride=NC * ONE), :] = first
        out[pl.ds((2 * p + 1) * ONE + 8, NR, stride=NC * ONE), :] = second
    send_ref[...] = out[...].astype(BF16)


def d_mixed_kernel(recv_ref, dproj_ref, w_out_ref, spread_ref, send_ref, scratch):
    scratch[...] = recv_ref[...].astype(F32)
    gain = spread_ref[...]
    w_out = w_out_ref[...]
    for q in range(9):
        wt = dot(w_out, row_cells(dproj_ref, q), NT) * gain
        normal, scale = norm_cells(scratch[pl.ds(q, H, stride=ONE), :])
        scratch[pl.ds(q, H, stride=ONE), :] = scale * (
            wt - jnp.mean(wt, 0, keepdims=True) - normal * jnp.mean(wt * normal, 0, keepdims=True)
        )
    send_ref[...] = scratch[...].astype(BF16)


def update_kernel(mask_s, recv_ref, w_out_ref, gain_ref, bias_ref, dproj_ref, cot_ref,
                  normed_ref, w_ref, update_ref, d_og_ref, grads_ref, pg_h, pvg_h,
                  scratch, pg_v, pvg_v, sems):
    weights = stacked_weights(w_ref)
    col_mask = column_mask(mask_s)
    for pair_at in range(A // 2):
        normed = normed_ref[pl.ds(pair_at * 2 * B, 2 * B), :]
        for k, (value, gate, pg) in enumerate(gate_parts(weights, normed, pair_at, col_mask, mask_s)):
            pg_v[2 * pair_at + k] = pg.astype(BF16)
            pvg_v[2 * pair_at + k] = (pg * value * (1.0 - gate)).astype(BF16)
    copies = [pltpu.make_async_copy(pg_v, pg_h, sems.at[0]),
              pltpu.make_async_copy(pvg_v, pvg_h, sems.at[1])]
    for copy in copies:
        copy.start()
    scratch[...] = recv_ref[...].astype(F32)
    gain, bias = column(gain_ref[...]), column(bias_ref[...])
    w_out, w_og = w_out_ref[...], w_ref[:, 4 * H :]
    grad = jnp.zeros((H, H), F32)
    for q in range(9):
        normal, _ = norm_cells(scratch[pl.ds(q, H, stride=ONE), :])
        out_normed = (normal * gain + bias).astype(BF16)
        projected = dot(out_normed, w_out, TN)
        grad = grad + dot(out_normed, row_cells(dproj_ref, q), NN)
        gates = jax.nn.sigmoid(dot(row_cells(normed_ref, q), w_og, NN))
        for at, lane, size in pieces(q):
            rows = pl.ds(at, size)
            sig, proj = gates[lane : lane + size], projected[lane : lane + size]
            update_ref[rows, :] = (sig * proj).astype(BF16)
            d_og_ref[rows, :] = (
                cot_ref[rows, :].astype(F32) * proj * sig * (1.0 - sig)
            ).astype(BF16)
    grads_ref[0] = dot(d_og_ref[...], normed_ref[...], TN).astype(BF16)
    grads_ref[1] = grad.astype(BF16)
    for copy in copies:
        copy.wait()


def back_kernel(recv_ref, left_ref, right_ref, pg_h, pvg_h, send_ref, pg_ref, pvg_ref,
                scratch, d_tile, d_left, d_right, out, sems):
    copies = [
        pltpu.make_async_copy(src, dst, sems.at[n])
        for n, (src, dst) in enumerate(
            [(pg_h, pg_ref), (pvg_h, pvg_ref)]
        )
    ]
    for copy in copies:
        copy.start()
    scratch[...] = recv_ref[...].astype(F32)
    lane, wide = lane_of((8, LANES)), lane_of((NR, LANES))
    for p in range(NC // 2):
        x, y = (
            scratch[pl.ds(c * ONE + 8, NR, stride=NC * ONE), :] for c in (2 * p, 2 * p + 1)
        )
        for n in range(8):
            d_tile[pl.ds(p * N + 16 + n, NR, stride=A), :] = jnp.where(
                wide < HALF, roll(x, 32 - 16 * n), roll(y, 96 - 16 * n)
            )
    for r in range(NR):
        for p in range(NC // 2):
            start = (r * NC + 2 * p) * ONE
            x, y = scratch[pl.ds(start, 8), :], scratch[pl.ds(start + ONE, 8), :]
            at = p * N + r * A
            tail = d_tile[at + 16 : at + 24, :]
            d_tile[at : at + 8, :] = jnp.where(lane < HALF, x, roll(y, HALF))
            d_tile[at + 8 : at + 16, :] = jnp.where(lane < HALF, roll(x, -B), roll(y, 16))
            d_tile[at + 16 : at + 24, :] = pick(
                lane, roll(x, 32), 32, tail, HALF, roll(y, 96), 96, tail
            )
    d = jnp.concatenate([d_tile[p * N : (p + 1) * N, :].astype(BF16) for p in range(4)], 1)
    d_left[...] = dot(d, right_ref[...], NN)
    product = dot(d, left_ref[...], TN)
    for p in range(NC // 2):
        d_right[p * 512 : (p + 1) * 512, :] = product[:, p * LANES : (p + 1) * LANES]
    for r in range(NR):
        for p in range(NC // 2):
            lanes = slice(p * LANES, (p + 1) * LANES)
            at = p * 512 + (r // 2) * HALF + (r % 2) * A
            x0, x1, x2 = (d_left[r * A + 8 * t : r * A + 8 * t + 8, lanes] for t in range(3))
            y0, y1, y2 = (d_right[at + 8 * t : at + 8 * t + 8, :] for t in range(3))
            start = (r * NC + 2 * p) * BOTH
            out[pl.ds(start, 8), :] = pick(lane, x0, B, roll(y0, B), 2 * B, roll(x2, 96))
            out[pl.ds(start + 8, 8), :] = pick(
                lane, x1, B, roll(y1, B), 2 * B, roll(x2, HALF), 112, roll(y2, 112)
            )
            start = start + BOTH
            out[pl.ds(start, 8), :] = pick(lane, roll(x0, HALF), B, roll(y0, -16), 2 * B, roll(x2, 32))
            out[pl.ds(start + 8, 8), :] = pick(
                lane, roll(x1, HALF), B, roll(y1, -16), 2 * B, x2, 112, roll(y2, B)
            )
    group = lane >> 5
    for p in range(NC // 2):
        for odd in range(2):
            for half in range(2):
                first = second = jnp.zeros((8, LANES), F32)
                for m in range(4):
                    at = p * 512 + odd * A + 16 + 4 * half + m
                    y2 = d_right[pl.ds(at, 8, stride=HALF), :]
                    first = jnp.where(group == m, roll(y2, 32 * m - 16), first)
                    second = jnp.where(group == m, roll(y2, 32 * m - 80), second)
                start = (odd * NC + 2 * p) * BOTH + 16 + half
                out[pl.ds(start, 8, stride=2 * NC * BOTH), :] = first
                out[pl.ds(start + BOTH, 8, stride=2 * NC * BOTH), :] = second
    send_ref[...] = out[...].astype(BF16)
    for copy in copies:
        copy.wait()


def gated(scratch, a, pg_v, pvg_v):
    block = lambda p: scratch[pl.ds(p, H, stride=BOTH), :]
    d = block(a) if a < 16 else unpack_third(block, a - 16)
    return jnp.concatenate([d * pg_v[a].astype(F32), d * pvg_v[a].astype(F32)], 0).astype(BF16)


def grad_kernel(recv_ref, pg_v, pvg_v, normed_ref, grads_ref, send_ref, scratch, packed):
    scratch[...] = recv_ref[...].astype(F32)
    for g in range(2):
        packed[pl.ds(4 + g, H, stride=SUMS), :] = grads_ref[g].astype(F32)
    total = jnp.zeros((2 * H, 2 * H), F32)
    for pair_at in range(A // 2):
        a = 2 * pair_at
        sides = [gated(scratch, a + k, pg_v, pvg_v) for k in range(2)]
        cells = [two_sided(normed_ref[(a + k) * B : (a + k + 1) * B, :]) for k in range(2)]
        total = total + dot(jnp.concatenate(sides, 1), jnp.concatenate(cells, 0), NN)
    for g, block in enumerate([total[:H, :H], total[H:, :H], total[:H, H:], total[H:, H:]]):
        packed[pl.ds(g, H, stride=SUMS), :] = block
    send_ref[...] = packed[...].astype(BF16)


def pair_grad_kernel(recv_ref, pg_h, pvg_h, d_og_ref, pair_ref, gain_ref, w_ref,
                     out_ref, scratch, pg_v, pvg_v, sems):
    copies = [pltpu.make_async_copy(pg_h, pg_v, sems.at[0]),
              pltpu.make_async_copy(pvg_h, pvg_v, sems.at[1])]
    for copy in copies:
        copy.start()
    scratch[...] = recv_ref[...].astype(F32)
    weights = stacked_weights(w_ref)
    w_og = w_ref[:, 4 * H :]
    gain = gain_ref[...]
    for copy in copies:
        copy.wait()
    for a in range(A):
        rows = pl.ds(a * B, B)
        both = dot(gated(scratch, a, pg_v, pvg_v), weights, TN)
        d = both[:B, :H] + both[B : 2 * B, H:] + dot(d_og_ref[rows, :], w_og, NT)
        normal, scale = norm_rows(pair_ref[rows, :].astype(F32))
        weighted = d * gain
        out_ref[rows, :] = (
            scale * (weighted - jnp.mean(weighted, 1, keepdims=True)
                     - normal * jnp.mean(weighted * normal, 1, keepdims=True))
        ).astype(BF16)


def sum_kernel(recv_ref, send_ref):
    parts = jnp.sum(recv_ref[...].astype(F32).reshape(16, 8 * SUMS, LANES), 0)
    total = parts[:SUMS]
    for k in range(1, 8):
        total = total + parts[k * SUMS : (k + 1) * SUMS]
    many = jnp.concatenate([total] * 8, 0).astype(BF16)
    for s in range(16):
        send_ref[s * 8 * SUMS : (s + 1) * 8 * SUMS, :] = many


def unpack_kernel(recv_ref, w_in_ref, w_out_ref, scratch):
    scratch[...] = recv_ref[...].astype(F32)
    for g in range(5):
        w_in_ref[:, g * H : (g + 1) * H] = scratch[pl.ds(g, H, stride=SUMS), :].T
    w_out_ref[...] = scratch[pl.ds(5, H, stride=SUMS), :]


def call(kernel, args, outs, scratch, flops, hbm_in=(), smem_in=(), hbm_out=()):
    shapes = [
        pltpu.HBM(s, d) if n in hbm_out else jax.ShapeDtypeStruct(s, d)
        for n, (s, d) in enumerate(outs)
    ]
    args = [
        pltpu.with_memory_space_constraint(v, pltpu.HBM) if n in hbm_in else v
        for n, v in enumerate(args)
    ]
    specs = [
        HBM_SPEC if n in hbm_in else pl.BlockSpec(memory_space=pltpu.SMEM) if n in smem_in else VMEM_SPEC
        for n in range(len(args))
    ]
    moved = 2 * (sum(v.size for v in args) + sum(math.prod(s) for s, _ in outs))
    return pl.pallas_call(
        kernel,
        out_shape=shapes,
        in_specs=specs,
        out_specs=[HBM_SPEC if n in hbm_out else VMEM_SPEC for n in range(len(shapes))],
        scratch_shapes=scratch,
        cost_estimate=pl.CostEstimate(flops=flops, bytes_accessed=moved, transcendentals=0),
        compiler_params=pltpu.CompilerParams(vmem_limit_bytes=40 * 2**20),
    )(*args)


def vm(*shape, dtype=F32):
    return pltpu.VMEM(shape, dtype)


def exchange(x, *tile):
    moved = lax.all_to_all(x.reshape(ND, *tile, LANES), AXES, 0, 0, tiled=True)
    return moved.reshape(x.shape)


def on_device(pair, mask, in_gain, in_bias, w_in, out_gain, out_bias, w_out, cotangent):
    pair2 = pair.reshape(CELLS, H)
    cot2 = cotangent.reshape(CELLS, H)
    line = lambda v: v.reshape(1, -1)
    dma = pltpu.SemaphoreType.DMA
    both_shape, one_shape, sum_shape = ((ND * n, LANES) for n in (BOTH, ONE, SUMS))
    gates = [vm(A, H, LANES, dtype=BF16)] * 2

    send, normed, dproj, spread, w_out_near = call(
        project_kernel,
        [mask, pair2, line(in_gain), line(in_bias), w_in, cot2, line(out_gain), w_out],
        [(both_shape, BF16), ((CELLS, H), BF16), ((CELLS, H), BF16), ((H, LANES), F32),
         ((H, H), BF16)],
        [pltpu.SMEM((N,), jnp.int32), vm(CELLS, H, dtype=BF16), vm(1, H), vm(1, H),
         vm(H, 5 * H, dtype=BF16), vm(CELLS, H, dtype=BF16), vm(1, H), vm(8, H, LANES),
         vm(*both_shape), dma((8,))],
        500_000_000, hbm_in=range(8),
    )
    recv = exchange(send, 9, 2)
    send, left, right = call(
        mix_kernel,
        [recv],
        [(one_shape, BF16), ((N, 512), BF16), ((512, 512), BF16)],
        [vm(*both_shape), vm(512, LANES), vm(4 * N, LANES), vm(*one_shape)],
        400_000_000,
    )
    mixed = exchange(send, 5, 2)
    (send,) = call(
        d_mixed_kernel,
        [mixed, dproj, w_out_near, spread],
        [(one_shape, BF16)],
        [vm(*one_shape)],
        50_000_000,
    )
    recv = exchange(send, 5, 2)
    update, d_og, grads, pg, pvg = call(
        update_kernel,
        [mask, mixed, w_out_near, line(out_gain), line(out_bias), dproj, cot2, normed, w_in],
        [((CELLS, H), BF16), ((CELLS, H), BF16), ((2, H, H), BF16),
         ((A, H, LANES), BF16), ((A, H, LANES), BF16)],
        [vm(*one_shape), *gates, dma((2,))],
        600_000_000, smem_in=(0,), hbm_out=(3, 4),
    )
    send, pg_near, pvg_near = call(
        back_kernel,
        [recv, left, right, pg, pvg],
        [(both_shape, BF16), ((A, H, LANES), BF16), ((A, H, LANES), BF16)],
        [vm(*one_shape), vm(4 * N, LANES), vm(N, 512), vm(4 * 512, LANES), vm(*both_shape),
         dma((2,))],
        800_000_000, hbm_in=(3, 4),
    )
    recv = exchange(send, 9, 2)
    (send,) = call(
        grad_kernel,
        [recv, pg_near, pvg_near, normed, grads],
        [(sum_shape, BF16)],
        [vm(*both_shape), vm(*sum_shape)],
        400_000_000,
    )
    parts = exchange(send, 3, 2)
    (pair_grad,) = call(
        pair_grad_kernel,
        [recv, pg, pvg, d_og, pair2, line(in_gain), w_in],
        [((CELLS, H), BF16)],
        [vm(*both_shape), *gates, dma((2,))],
        400_000_000, hbm_in=(1, 2),
    )
    (send,) = call(sum_kernel, [parts], [(sum_shape, BF16)], [], 1_000_000)
    sums = exchange(send, 3, 2)
    w_in_grad, w_out_grad = call(
        unpack_kernel,
        [sums],
        [((H, 5 * H), F32), ((H, H), F32)],
        [vm(*sum_shape)],
        1_000_000,
    )
    return (update.reshape(A, B, H), pair_grad.reshape(A, B, H), w_in_grad, w_out_grad)


def solution(mesh):
    placed = (P("row", "col", None), P(), P(), P(), P(), P(), P(), P(), P("row", "col", None))
    return jax.shard_map(
        on_device,
        mesh=mesh,
        in_specs=placed,
        out_specs=(P("row", "col", None), P("row", "col", None), P(), P()),
        check_vma=False,
    )
```
